32 devices in a mesh: wide: 16 (over z, x, core), narrow: 2 (over y).
Axes of the slice: x: 2, y: 2, z: 4, core: 2. Of those that a mesh axis runs over, the one named last changes fastest.
Arguments:
- tokens: bfloat16 [2, 32, 320, 1024], P(None, ('wide', 'narrow')), may hold values from -6 to 6
- cotangent: bfloat16 [2, 32, 320, 1024], P(None, ('wide', 'narrow')), may hold values from -6 to 6
- cond: bfloat16 [8, 1024], replicated, may hold values from -6 to 6
- clip_frames: int32 [8], replicated, may hold values from 2 to 9, as said below
- window_clip: int32 [2, 32], P(None, ('wide', 'narrow')), may hold values from 0 to 7
- window_half: int32 [2, 32], P(None, ('wide', 'narrow')), may hold values from 0 to 1
- ada_weight: bfloat16 [1024, 6144], P('narrow', 'wide'), may hold values from -0.1875 to 0.1875
- qkv_weight: bfloat16 [1024, 3072], P('narrow', 'wide'), may hold values from -0.1875 to 0.1875
- out_weight: bfloat16 [1024, 1024], P('narrow', 'wide'), may hold values from -1 to 1
- up_weight: bfloat16 [1024, 4096], P('narrow', 'wide'), may hold values from -0.1875 to 0.1875
- down_weight: bfloat16 [4096, 1024], P('narrow', 'wide'), may hold values from -0.09375 to 0.09375
- offset_table: bfloat16 [16, 39], replicated, may hold values from -3 to 3
Outputs:
- mixed: bfloat16 [2, 32, 320, 1024], P(None, ('wide', 'narrow'))
- grad_tokens: float32 [2, 32, 320, 1024], P(None, ('wide', 'narrow'))
- grad_ada: float32 [1024, 6144], P('narrow', 'wide')
- grad_qkv: float32 [1024, 3072], P('narrow', 'wide')
- grad_out: float32 [1024, 1024], P('narrow', 'wide')
- grad_up: float32 [1024, 4096], P('narrow', 'wide')
- grad_down: float32 [4096, 1024], P('narrow', 'wide')
- grad_table: float32 [16, 39], replicated
The draws below stay inside these ranges and needn't reach their ends.
Inputs may be any that keep to these rules, and one draw needn't show every extreme that they name: `clip_frames`: latent frames of each clip; short clips are the most common, each longer count about half as frequent as the one below it, and some clip has the most. `window_clip`: a clip number.
All inputs are finite; a program needn't handle non-finite values.
Results may differ from the reference program's by a relative error of at most 0.017.
Values may be sent and summed in bfloat16 or wider, within the bound.
A program may use at most 256 MiB of HBM per device.

```python
import jax
import jax.numpy as jnp
from jax import lax

D = 1024
HEADS = 16
FF = 4096
WIN_FRAMES = 5
WIN_SIDE = 8
MICRO = 2
WIN_TOK = 320
NREL = 39
WINDOWS = 32
CLIPS = 8


def draw_clip_frames(key, part):
    levels = jax.random.randint(jax.random.fold_in(key, 17), (CLIPS,), 0, 1024)
    frames = jnp.full((CLIPS,), 2, jnp.int32)
    for step_idx in range(1, 2 * WIN_FRAMES - 2):
        frames = frames + (levels >= 1024 - (1024 >> step_idx)).astype(jnp.int32)
    frames = frames.at[0].set(2 * WIN_FRAMES - 1)
    frames = frames.at[1].set(2)
    return frames.astype(jnp.int32)


def with_ends(entries, rng, least, top_value):
    longest = entries.shape.index(max(entries.shape))
    spots = []
    for shift in (0, 1):
        where = [jax.random.randint(jax.random.fold_in(rng, axis), (), 0, length) for axis, length in enumerate(entries.shape)]
        where[longest] = (where[longest] + shift) % entries.shape[longest]
        spots.append(tuple(where))
    return entries.at[spots[0]].set(least).at[spots[1]].set(top_value)


def steps_of(key, shape, cuts, low, largest):
    factor_of, own = 1.0, jax.random.fold_in(key, 6)
    for dim, shards_of in cuts:
        heights = jnp.exp(jax.random.uniform(jax.random.fold_in(own, dim), (shards_of,), jnp.float32, low / len(cuts), largest / len(cuts)))
        factor_of = factor_of * jnp.repeat(heights, shape[dim] // shards_of).reshape([-1 if axis == dim else 1 for axis in range(len(shape))])
    return factor_of


def centred(rng, dims, spread, most, cuts=(), kind=jnp.bfloat16):
    values = spread * jax.random.normal(rng, dims, jnp.float32)
    if cuts:
        values = values * steps_of(rng, dims, cuts, -0.22, 0.18)
    return jnp.clip(values, -most, most).astype(kind)


def setup_inputs(seed: int = 0) -> dict:
    arg_keys = jax.random.split(jax.random.key(seed), 13)
    return {
        "tokens": centred(arg_keys[0], (MICRO, WINDOWS, WIN_TOK, D), 1.0, 6.0, ((1, 32),)),
        "cotangent": centred(arg_keys[1], (MICRO, WINDOWS, WIN_TOK, D), 1.0, 6.0, ((1, 32),)),
        "cond": centred(arg_keys[2], (CLIPS, D), 1.0, 6.0),
        "clip_frames": draw_clip_frames(jax.random.fold_in(arg_keys[12], 71), 0),
        "window_clip": with_ends(jax.random.randint(arg_keys[4], (MICRO, WINDOWS), 0, CLIPS), jax.random.fold_in(arg_keys[4], 1), 0, CLIPS - 1).astype(jnp.int32),
        "window_half": with_ends(jax.random.randint(arg_keys[5], (MICRO, WINDOWS), 0, 2), jax.random.fold_in(arg_keys[5], 1), 0, 1).astype(jnp.int32),
        "ada_weight": centred(arg_keys[6], (D, 6 * D), D ** -0.5, 0.1875, ((0, 2), (1, 16))),
        "qkv_weight": centred(arg_keys[7], (D, 3 * D), D ** -0.5, 0.1875, ((0, 2), (1, 16))),
        "out_weight": centred(arg_keys[8], (D, D), (D // 32) ** -0.5, 1.0, ((0, 2), (1, 16))),
        "up_weight": centred(arg_keys[9], (D, FF), D ** -0.5, 0.1875, ((0, 2), (1, 16))),
        "down_weight": centred(arg_keys[10], (FF, D), FF ** -0.5, 0.09375, ((0, 2), (1, 16))),
        "offset_table": centred(arg_keys[11], (HEADS, NREL), 0.5, 3.0),
    }


@jax.custom_vjp
def low(v):
    return lax.optimization_barrier(v.astype(jnp.bfloat16)).astype(jnp.float32)

@jax.custom_vjp
def low_back(v):
    return v

def low_keep(v):
    return (low(v), None)

def low_pass(kept, grad):
    return (grad,)

def back_keep(v):
    return (v, None)

def back_low(kept, grad):
    return (low(grad),)
low.defvjp(low_keep, low_pass)
low_back.defvjp(back_keep, back_low)
epsilon = 1e-06
masked_score = -1e+30
highest = lax.Precision.HIGHEST

def normalize(values):
    centre = lax.optimization_barrier(jnp.mean(values, -1, keepdims=True))
    shifted = values - centre
    return shifted * lax.rsqrt(lax.optimization_barrier(jnp.mean(shifted * shifted, -1, keepdims=True)) + epsilon)

def offset_maps():
    frame_pos = jnp.arange(WIN_FRAMES)
    side_pos = jnp.arange(WIN_SIDE)
    frame_off = frame_pos[:, None] - frame_pos[None, :] + WIN_FRAMES - 1
    side_off = side_pos[:, None] - side_pos[None, :] + WIN_SIDE - 1
    frame_map = (frame_off[:, :, None] == jnp.arange(2 * WIN_FRAMES - 1)[None, None, :]).astype(jnp.float32)
    side_map = (side_off[:, :, None] == jnp.arange(2 * WIN_SIDE - 1)[None, None, :]).astype(jnp.float32)
    return (frame_map, side_map)

def build_bias(table):
    frame_map, side_map = offset_maps()
    frame_span = 2 * WIN_FRAMES - 1
    side_span = 2 * WIN_SIDE - 1
    along_frame = jnp.einsum('hk,ijk->hij', table[:, :frame_span], frame_map, precision=highest)
    along_row = jnp.einsum('hk,ijk->hij', table[:, frame_span:frame_span + side_span], side_map, precision=highest)
    along_col = jnp.einsum('hk,ijk->hij', table[:, frame_span + side_span:], side_map, precision=highest)
    full_grid = along_frame[:, :, None, None, :, None, None] + along_row[:, None, :, None, None, :, None] + along_col[:, None, None, :, None, None, :]
    win_tokens = WIN_FRAMES * WIN_SIDE * WIN_SIDE
    return full_grid.reshape(table.shape[0], win_tokens, win_tokens)

def forward(inputs, cond_rows, valid, ada_mat, qkv_mat, out_mat, up_mat, down_mat, table_val):
    win_count, win_tokens, width = inputs.shape
    head_count = table_val.shape[0]
    head_dim = width // head_count
    scale_factor = head_dim ** (-0.5)
    cond_act = low(jax.nn.silu(cond_rows))
    modulation = low_back(jnp.dot(cond_act, ada_mat, precision=highest)).reshape(win_count, 6, 1, width)
    hidden_one = low(normalize(inputs) * (1.0 + modulation[:, 1]) + modulation[:, 0])
    qkv_vals = low(low_back(jnp.einsum('wtd,de->wte', hidden_one, qkv_mat, precision=highest)))
    bias = build_bias(table_val)

    def attend(win_pair):
        win_block, live_row = win_pair
        split_block = win_block.reshape(win_tokens, 3, head_count, head_dim)
        queries = split_block[:, 0]
        keys_in = split_block[:, 1]
        values_in = split_block[:, 2]
        raw_scores = low_back(jnp.einsum('ihe,jhe->hij', queries, keys_in, precision=highest) * scale_factor)
        scores = jnp.where(live_row[None, None, :], raw_scores + bias, masked_score)
        probs = low(jax.nn.softmax(scores, axis=-1))
        return jnp.einsum('hij,jhe->ihe', probs, values_in, precision=highest).reshape(win_tokens, width)
    heads_out = low(low_back(lax.map(jax.checkpoint(attend), (qkv_vals, valid))))
    attended = low_back(jnp.einsum('wtd,de->wte', heads_out, out_mat, precision=highest))
    resid_mid = inputs + modulation[:, 2] * attended
    hidden_two = low(normalize(resid_mid) * (1.0 + modulation[:, 4]) + modulation[:, 3])
    up_proj = low_back(jnp.einsum('wtd,df->wtf', hidden_two, up_mat, precision=highest))
    gelu_vals = low(jax.nn.gelu(up_proj, approximate=False))
    ffn_out = low_back(jnp.einsum('wtf,fd->wtd', gelu_vals, down_mat, precision=highest))
    return resid_mid + modulation[:, 5] * ffn_out

def reference(tokens, cotangent, cond, clip_frames, window_clip, window_half, ada_weight, qkv_weight, out_weight, up_weight, down_weight, offset_table):
    win_tokens = WIN_FRAMES * WIN_SIDE * WIN_SIDE
    all_windows = MICRO * WINDOWS
    group_len = 8
    group_count = all_windows // group_len
    window_ids = window_clip.reshape(all_windows).astype(jnp.int32)
    frames_of = clip_frames[window_ids]
    live = jnp.clip(frames_of - WIN_FRAMES * window_half.reshape(all_windows), 1, WIN_FRAMES)
    frame_of_pos = jnp.arange(win_tokens) // (WIN_SIDE * WIN_SIDE)
    valid = (frame_of_pos[None, :] < live[:, None]).reshape(group_count, group_len, win_tokens)
    cond_rows = cond.astype(jnp.float32)[window_ids].reshape(group_count, group_len, D)
    inputs = tokens.astype(jnp.float32).reshape(group_count, group_len, win_tokens, D)
    grads_in = cotangent.astype(jnp.float32).reshape(group_count, group_len, win_tokens, D)
    weights = (ada_weight.astype(jnp.float32), qkv_weight.astype(jnp.float32), out_weight.astype(jnp.float32), up_weight.astype(jnp.float32), down_weight.astype(jnp.float32), offset_table.astype(jnp.float32))

    def group_step(totals, group_data):
        group_in, group_grad, group_cond, group_valid = group_data

        def run(x_val, ada_mat, qkv_mat, out_mat, up_mat, down_mat, table_val):
            return forward(x_val, group_cond, group_valid, ada_mat, qkv_mat, out_mat, up_mat, down_mat, table_val)
        result, pullback = jax.vjp(run, group_in, *weights)
        grads = pullback(group_grad)
        new_totals = tuple((prior_val + new_val for prior_val, new_val in zip(totals, grads[1:])))
        return (new_totals, (result.astype(jnp.bfloat16), grads[0]))
    zero_totals = tuple((jnp.zeros(weight_val.shape, jnp.float32) for weight_val in weights))
    totals, outs_pair = lax.scan(group_step, zero_totals, (inputs, grads_in, cond_rows, valid))
    mixed = outs_pair[0].reshape(tokens.shape)
    grad_tokens = outs_pair[1].reshape(tokens.shape)
    return (mixed, grad_tokens, totals[0], totals[1], totals[2], totals[3], totals[4], totals[5])
```

```python
import functools
import math

import jax
import jax.numpy as jnp
import numpy as np
from jax import lax
from jax.experimental import pallas as pl
from jax.experimental.pallas import tpu as pltpu
from jax.sharding import PartitionSpec as P

HEADS = 16
WIN_FRAMES = 5
WIN_SIDE = 8
TOK = WIN_FRAMES * WIN_SIDE * WIN_SIDE
F_SPAN = 2 * WIN_FRAMES - 1
S_SPAN = 2 * WIN_SIDE - 1
epsilon = 1e-06
inv_root_two = 0.7071067811865476
inv_root_tau = 0.3989422804014327
highest = lax.Precision.HIGHEST
MESH = pl.DeviceIdType.MESH
bf16 = jnp.bfloat16
f32 = jnp.float32


def position_features():
    p = np.arange(TOK)
    feats = np.zeros((TOK, WIN_FRAMES + 2 * WIN_SIDE), np.float32)
    feats[p, p // 64] = 1
    feats[p, WIN_FRAMES + (p // 8) % 8] = 1
    feats[p, WIN_FRAMES + WIN_SIDE + p % 8] = 1
    return feats


def offset_selector():
    sel = np.zeros((21, 21, F_SPAN + 2 * S_SPAN), np.float32)
    for i in range(WIN_FRAMES):
        for j in range(WIN_FRAMES):
            sel[i, j, i - j + WIN_FRAMES - 1] = 1
    for i in range(WIN_SIDE):
        for j in range(WIN_SIDE):
            sel[5 + i, 5 + j, F_SPAN + i - j + WIN_SIDE - 1] = 1
            sel[13 + i, 13 + j, F_SPAN + S_SPAN + i - j + WIN_SIDE - 1] = 1
    return sel


def both_halves(features):
    pad = [(0, 0)] * (features.ndim - 1) + [(0, 64 - features.shape[-1])]
    half = jnp.pad(features, pad)
    return jnp.concatenate([half, half], -1)


class Place:
    def __init__(self, dims):
        self.A, self.B, self.C = dims
        w = lax.axis_index("wide")
        self.c = lax.axis_index("narrow")
        self.k = lax.rem(w, 2)
        self.b = lax.rem(w // 2, self.B)
        self.a = w // (2 * self.B)

    def dev(self, a=None, b=None, k=None, c=None):
        a = self.a if a is None else a
        b = self.b if b is None else b
        k = self.k if k is None else k
        c = self.c if c is None else c
        return ((a * self.B + b) * 2 + k, c)

    def a_peer(self, d):
        return lax.rem(self.a + d, self.A)

    def b_peer(self, d):
        return lax.rem(self.b + d, self.B)

    def c_peer(self, d):
        return lax.rem(self.c + d, self.C)

    def barrier(self):
        peers = [self.dev(a=self.a_peer(d)) for d in range(1, self.A)]
        peers += [self.dev(b=self.b_peer(d)) for d in range(1, self.B)]
        peers += [self.dev(c=self.c_peer(d)) for d in range(1, self.C)]
        peers += [self.dev(k=1 - self.k)]
        sem = pltpu.get_barrier_semaphore()
        for peer in peers:
            pl.semaphore_signal(sem, inc=1, device_id=peer, device_id_type=MESH)
        pl.semaphore_wait(sem, len(peers))


def send(src, dst, ssem, rsem, dev):
    copy = pltpu.make_async_remote_copy(
        src_ref=src, dst_ref=dst, send_sem=ssem, recv_sem=rsem, device_id=dev, device_id_type=MESH
    )
    copy.start()
    return copy


def cols(c, K):
    return pl.ds(pl.multiple_of(c * K, K), K)


def n_sems(dims):
    A, B, C = dims
    return (A - 1) + (B - 1) + (C - 1) + 1


class Gather:
    def __init__(self, place, block, own, part_a, part_b, part_c, order, ssem, rsem):
        self.p = place
        self.block, self.own = block, own
        self.part_a, self.part_b, self.part_c = part_a, part_b, part_c
        self.order = order
        self.ssem, self.rsem = ssem, rsem
        self.sent = []
        self.phases = []

    def start(self, phase):
        p = self.p
        out = []
        if phase == 0:
            for d in range(1, p.A):
                out.append(send(self.block, self.own, self.ssem.at[d - 1], self.rsem.at[d - 1], p.dev(a=p.a_peer(d))))
        elif phase < 3:
            first = phase == 1
            if self.order[phase - 1] == "b":
                ref = self.part_a if first else self.part_b
                base = p.A - 1
                for d in range(1, p.B):
                    s = base + d - 1
                    out.append(send(ref, ref, self.ssem.at[s], self.rsem.at[s], p.dev(b=p.b_peer(d))))
            else:
                ref = self.part_a if first else self.part_b
                base = p.A - 1 + p.B - 1
                for d in range(1, p.C):
                    s = base + d - 1
                    out.append(send(ref, ref, self.ssem.at[s], self.rsem.at[s], p.dev(c=p.c_peer(d))))
        else:
            s = p.A - 1 + p.B - 1 + p.C - 1
            out.append(send(self.part_c, self.part_c, self.ssem.at[s], self.rsem.at[s], p.dev(k=1 - p.k)))
        self.phases.append(out)

    def landed(self, phase):
        for copy in self.phases[phase]:
            copy.wait_recv()

    def drain(self):
        for out in self.phases:
            for copy in out:
                copy.wait_send()


def pieces_of_weight(place, block, full, K, rows_list, ssem, rsem, base):
    p = place
    mine = cols(p.c, K)
    made = []
    for i, (rows, order) in enumerate(rows_list):
        part_a = full.at[:, p.b, p.k, rows, mine]
        if order == "bc":
            part_b = full.at[:, :, p.k, rows, mine]
        else:
            part_b = full.at[:, p.b, p.k, rows, :]
        made.append(
            Gather(
                p,
                block.at[rows, :],
                full.at[p.a, p.b, p.k, rows, mine],
                part_a,
                part_b,
                full.at[:, :, p.k, rows, :],
                order,
                ssem.at[base + i],
                rsem.at[base + i],
            )
        )
    return made


def piece_of_small(place, block, full, ssem, rsem, base):
    p = place
    return Gather(
        p,
        block,
        full.at[p.a, p.b, p.k, p.c],
        full.at[:, p.b, p.k, p.c],
        full.at[:, :, p.k, p.c],
        full.at[:, :, p.k],
        "bc",
        ssem.at[base],
        rsem.at[base],
    )


def run_gathers(groups, owned):
    for copy in owned:
        copy.start()
    count = len(groups)
    for t in range(count + 4):
        if t < count:
            for g in groups[t]:
                g.start(0)
        if t == 0:
            for copy in owned:
                copy.wait()
        for phase in (1, 2, 3, 4):
            i = t - phase
            if 0 <= i < count:
                for g in groups[i]:
                    g.landed(phase - 1)
                    if phase < 4:
                        g.start(phase)
    for group in groups:
        for g in group:
            g.drain()


def gather_kernel(dims, widths, halves, mod_blk, qkv_b, out_b, up_b, down_b, mod_f, qkv_f, out_f, up_f, down_f, ssem, rsem, lsem):
    p = Place(dims)
    p.barrier()
    blocks = [qkv_b, out_b, up_b, down_b]
    fulls = [qkv_f, out_f, up_f, down_f]
    owned = [pltpu.make_async_copy(mod_blk, mod_f.at[p.a, p.b, p.k, p.c], lsem.at[4])]
    groups = [[piece_of_small(p, mod_blk, mod_f, ssem, rsem, 0)]]
    base = 1
    for i, (block, full) in enumerate(zip(blocks, fulls)):
        K = widths[i]
        owned.append(pltpu.make_async_copy(block, full.at[p.a, p.b, p.k, :, cols(p.c, K)], lsem.at[i]))
        groups.append(pieces_of_weight(p, block, full, K, halves[i], ssem, rsem, base))
        base += len(halves[i])
    run_gathers(groups, owned)


def gather_all(dims, mod_blk, blocks):
    A, B, C = dims
    widths = [blk.shape[1] for blk in blocks]
    halves = []
    for blk in blocks:
        R = blk.shape[0]
        halves.append([(pl.ds(0, R // 2), "bc"), (pl.ds(R // 2, R // 2), "cb")])
    out_shape = [jax.ShapeDtypeStruct((A, B, 2, C) + mod_blk.shape, mod_blk.dtype)]
    out_shape += [jax.ShapeDtypeStruct((A, B, 2, blk.shape[0], C * blk.shape[1]), blk.dtype) for blk in blocks]
    count = 1 + sum(len(h) for h in halves)
    hbm = pl.BlockSpec(memory_space=pltpu.HBM)
    return pl.pallas_call(
        functools.partial(gather_kernel, dims, widths, halves),
        out_shape=out_shape,
        in_specs=[hbm] * 5,
        out_specs=[hbm] * 5,
        scratch_shapes=[
            pltpu.SemaphoreType.DMA((count, n_sems(dims))),
            pltpu.SemaphoreType.DMA((count, n_sems(dims))),
            pltpu.SemaphoreType.DMA((5,)),
        ],
        compiler_params=pltpu.CompilerParams(collective_id=0, has_side_effects=True),
        name="gather_weights",
    )(mod_blk, *blocks)


class Scatter:
    def __init__(self, place, grad, held, sib, rx, rl, out, K, ssem, rsem, lsem):
        self.p, self.grad, self.held, self.sib, self.rx, self.rl = place, grad, held, sib, rx, rl
        self.out, self.K = out, K
        self.ssem, self.rsem, self.lsem = ssem, rsem, lsem
        self.R = grad.shape[3]
        self.sent = []

    def _send(self, src, dst, s, dev):
        copy = send(src, dst, self.ssem.at[s], self.rsem.at[s], dev)
        self.sent.append(copy)
        return copy

    def start_sibling(self):
        p = self.p
        self.local = pltpu.make_async_copy(self.grad.at[:, :, p.k], self.held, self.lsem)
        self.local.start()
        self.first = self._send(self.grad.at[:, :, 1 - p.k], self.sib, 0, p.dev(k=1 - p.k))

    def add_sibling(self):
        self.local.wait()
        self.first.wait_recv()
        p = self.p

        def step(i, _):
            a, b = i // p.B, lax.rem(i, p.B)
            self.held[a, b] = self.held[a, b] + self.sib[a, b]
            return 0

        lax.fori_loop(0, p.A * p.B, step, 0)

    def halves(self):
        h = self.R // 2
        return pl.ds(0, h), pl.ds(h, h)

    def start_two(self):
        p, K = self.p, self.K
        r0, r1 = self.halves()
        self.second = []
        for d in range(1, p.C):
            self.second.append(
                self._send(self.held.at[:, :, r0, cols(p.c_peer(d), K)], self.rx["c0"].at[d - 1], d, p.dev(c=p.c_peer(d)))
            )
        for d in range(1, p.B):
            self.second.append(
                self._send(self.held.at[:, p.b_peer(d), r1, :], self.rx["b1"].at[d - 1], p.C - 1 + d, p.dev(b=p.b_peer(d)))
            )

    def add_two(self):
        p, K = self.p, self.K
        r0, r1 = self.halves()
        for copy in self.second:
            copy.wait_recv()
        mine = cols(p.c, K)

        def step(i, _):
            a, b = i // p.B, lax.rem(i, p.B)
            total = self.held[a, b, r0, mine]
            for d in range(1, p.C):
                total = total + self.rx["c0"][d - 1, a, b]
            self.held[a, b, r0, mine] = total
            return 0

        lax.fori_loop(0, p.A * p.B, step, 0)

        def step1(a, _):
            total = self.held[a, p.b, r1, :]
            for d in range(1, p.B):
                total = total + self.rx["b1"][d - 1, a]
            self.held[a, p.b, r1, :] = total
            return 0

        lax.fori_loop(0, p.A, step1, 0)

    def start_three(self):
        p, K = self.p, self.K
        r0, r1 = self.halves()
        mine = cols(p.c, K)
        base = p.C - 1 + p.B - 1
        self.third = []
        for d in range(1, p.B):
            self.third.append(
                self._send(self.held.at[:, p.b_peer(d), r0, mine], self.rx["b0"].at[d - 1], base + d, p.dev(b=p.b_peer(d)))
            )
        base += p.B - 1
        for d in range(1, p.C):
            self.third.append(
                self._send(self.held.at[:, p.b, r1, cols(p.c_peer(d), K)], self.rx["c1"].at[d - 1], base + d, p.dev(c=p.c_peer(d)))
            )

    def add_three(self):
        p, K = self.p, self.K
        r0, r1 = self.halves()
        for copy in self.third:
            copy.wait_recv()
        mine = cols(p.c, K)

        def step(a, _):
            total = self.held[a, p.b, r0, mine]
            for d in range(1, p.B):
                total = total + self.rx["b0"][d - 1, a]
            self.held[a, p.b, r0, mine] = total
            other = self.held[a, p.b, r1, mine]
            for d in range(1, p.C):
                other = other + self.rx["c1"][d - 1, a]
            self.held[a, p.b, r1, mine] = other
            return 0

        lax.fori_loop(0, p.A, step, 0)

    def start_four(self):
        p, K = self.p, self.K
        mine = cols(p.c, K)
        base = 2 * (p.C - 1 + p.B - 1)
        self.fourth = []
        for d in range(1, p.A):
            self.fourth.append(
                self._send(self.held.at[p.a_peer(d), p.b, :, mine], self.rl.at[d - 1], base + d, p.dev(a=p.a_peer(d)))
            )

    def finish(self):
        p, K = self.p, self.K
        for copy in self.fourth:
            copy.wait_recv()
        total = self.held[p.a, p.b, :, cols(p.c, K)].astype(f32)
        for d in range(1, p.A):
            total = total + self.rl[d - 1].astype(f32)
        self.out[...] = total

    def drain(self):
        for copy in self.sent:
            copy.wait_send()


def scatter_kernel(dims, widths, n_grads, *refs):
    A, B, C = dims
    grads = refs[:n_grads]
    smalls = refs[n_grads : n_grads + 2]
    outs = refs[n_grads + 2 : 2 * n_grads + 2]
    small_fulls = refs[2 * n_grads + 2 : 2 * n_grads + 4]
    scratch = refs[2 * n_grads + 4 :]
    per = 7
    ssem, rsem, lsem, gssem, grsem, glsem = scratch[per * n_grads :]
    p = Place(dims)
    p.barrier()
    items = []
    for i in range(n_grads):
        held, sib, c0, b1, b0, c1, rl = scratch[per * i : per * (i + 1)]
        rx = {"c0": c0, "b1": b1, "b0": b0, "c1": c1}
        items.append(
            Scatter(p, grads[i], held, sib, rx, rl, outs[i], widths[i], ssem.at[i], rsem.at[i], lsem.at[i])
        )
    owned = [
        pltpu.make_async_copy(smalls[i], small_fulls[i].at[p.a, p.b, p.k, p.c], glsem.at[i]) for i in range(2)
    ]
    small = [piece_of_small(p, smalls[i], small_fulls[i], gssem, grsem, i) for i in range(2)]
    for copy in owned:
        copy.start()
    for g in small:
        g.start(0)
    for copy in owned:
        copy.wait()
    stages = [
        (None, "start_sibling"),
        ("add_sibling", "start_two"),
        ("add_two", "start_three"),
        ("add_three", "start_four"),
        ("finish", None),
    ]
    for t in range(n_grads + 4):
        for phase in range(5):
            i = t - phase
            if 0 <= i < n_grads:
                before, after = stages[phase]
                if before:
                    getattr(items[i], before)()
                if after:
                    getattr(items[i], after)()
        if 1 <= t <= 4:
            for g in small:
                g.landed(t - 1)
                if t < 4:
                    g.start(t)
    for item in items:
        item.drain()
    for g in small:
        g.drain()


def scatter_all(dims, grads, smalls):
    A, B, C = dims
    widths = [g.shape[4] // C for g in grads]
    scratch = []
    for g in grads:
        R, full = g.shape[3], g.shape[4]
        K, h = full // C, g.shape[3] // 2
        scratch += [
            pltpu.VMEM((A, B, R, full), bf16),
            pltpu.VMEM((A, B, R, full), bf16),
            pltpu.VMEM((C - 1, A, B, h, K), bf16),
            pltpu.VMEM((B - 1, A, h, full), bf16),
            pltpu.VMEM((B - 1, A, h, K), bf16),
            pltpu.VMEM((C - 1, A, h, K), bf16),
            pltpu.VMEM((A - 1, R, K), bf16),
        ]
    n = len(grads)
    count = 1 + 2 * (C - 1 + B - 1) + (A - 1)
    scratch += [
        pltpu.SemaphoreType.DMA((n, count)),
        pltpu.SemaphoreType.DMA((n, count)),
        pltpu.SemaphoreType.DMA((n,)),
        pltpu.SemaphoreType.DMA((2, n_sems(dims))),
        pltpu.SemaphoreType.DMA((2, n_sems(dims))),
        pltpu.SemaphoreType.DMA((2,)),
    ]
    hbm = pl.BlockSpec(memory_space=pltpu.HBM)
    vmem = pl.BlockSpec(memory_space=pltpu.VMEM)
    out_shape = [jax.ShapeDtypeStruct((g.shape[3], g.shape[4] // C), f32) for g in grads]
    out_shape += [jax.ShapeDtypeStruct((A, B, 2, C) + s.shape, s.dtype) for s in smalls]
    return pl.pallas_call(
        functools.partial(scatter_kernel, dims, widths, n),
        out_shape=out_shape,
        in_specs=[hbm] * (n + 2),
        out_specs=[vmem] * n + [hbm] * 2,
        scratch_shapes=scratch,
        compiler_params=pltpu.CompilerParams(
            collective_id=1, has_side_effects=True, vmem_limit_bytes=62 * 2**20
        ),
        name="scatter_grads",
    )(*grads, *smalls)


def nt(lhs, rhs):
    return lax.dot_general(lhs, rhs, (((1,), (1,)), ((), ())), preferred_element_type=f32)


def nn(lhs, rhs):
    return lax.dot_general(lhs, rhs, (((1,), (0,)), ((), ())), preferred_element_type=f32)


def tn(lhs, rhs):
    return lax.dot_general(lhs, rhs, (((0,), (0,)), ((), ())), preferred_element_type=f32)


def attend_fwd_kernel(q_ref, k_ref, v_ref, u_ref, g_ref, m_ref, o_ref, lse_ref):
    low_half = lax.broadcasted_iota(jnp.int32, (TOK, 128), 1) < 64
    q = q_ref[...] * jnp.asarray(0.125, bf16)
    k, v, u = k_ref[...], v_ref[...], u_ref[...]
    mask = m_ref[0]
    results = []
    for h in range(2):
        own = low_half if h == 0 else jnp.logical_not(low_half)
        q_ext = jnp.where(own, q, u)
        k_ext = jnp.where(own, k, g_ref[h] + mask)
        s = nt(q_ext, k_ext)
        peak = jnp.max(s, -1, keepdims=True)
        e = jnp.exp(s - peak)
        total = jnp.sum(e, -1, keepdims=True)
        probs = (e / total).astype(bf16)
        lse_ref[0, h] = peak + jnp.log(total)
        results.append(nn(probs, v))
    o_ref[...] = jnp.where(low_half, results[0], results[1]).astype(bf16)


def attend_fwd(qkv, u, g, mask):
    wins = mask.shape[0]
    width = qkv.shape[1] // 3
    pairs = width // 128
    return pl.pallas_call(
        attend_fwd_kernel,
        grid=(wins, pairs),
        in_specs=[
            pl.BlockSpec((TOK, 128), lambda w, h: (w, h)),
            pl.BlockSpec((TOK, 128), lambda w, h: (w, pairs + h)),
            pl.BlockSpec((TOK, 128), lambda w, h: (w, 2 * pairs + h)),
            pl.BlockSpec((TOK, 128), lambda w, h: (0, 0)),
            pl.BlockSpec((2, TOK, 128), lambda w, h: (h, 0, 0)),
            pl.BlockSpec((1, TOK, 128), lambda w, h: (w, 0, 0)),
        ],
        out_specs=[
            pl.BlockSpec((TOK, 128), lambda w, h: (w, h)),
            pl.BlockSpec((1, 2, TOK, 1), lambda w, h: (w, h, 0, 0)),
        ],
        out_shape=[
            jax.ShapeDtypeStruct((wins * TOK, width), bf16),
            jax.ShapeDtypeStruct((wins, 2 * pairs, TOK, 1), f32),
        ],
        name="attend_fwd",
    )(qkv, qkv, qkv, u, g, mask)


def attend_bwd_kernel(q_ref, k_ref, v_ref, do_ref, lse_ref, u_ref, g_ref, m_ref, dq_ref, dk_ref, dv_ref, z_ref):
    low_half = lax.broadcasted_iota(jnp.int32, (TOK, 128), 1) < 64
    zero = jnp.zeros((TOK, 128), bf16)
    q = q_ref[...] * jnp.asarray(0.125, bf16)
    k, v, u, do = k_ref[...], v_ref[...], u_ref[...], do_ref[...]
    mask = m_ref[0]
    dqs, dks, dvs = [], [], []
    for h in range(2):
        own = low_half if h == 0 else jnp.logical_not(low_half)
        q_ext = jnp.where(own, q, u)
        k_ext = jnp.where(own, k, g_ref[h] + mask)
        s = nt(q_ext, k_ext)
        probs = jnp.exp(s - lse_ref[0, h])
        do_h = jnp.where(own, do, zero)
        dvs.append(tn(probs.astype(bf16), do))
        dp = nt(do_h, v)
        ds = probs * (dp - jnp.sum(probs * dp, -1, keepdims=True))
        ds_low = ds.astype(bf16)
        dqs.append(nn(ds_low, k))
        dk_ext = tn(ds_low, q_ext)
        dks.append(dk_ext)
        z_ref[0, h] = lax.dot_general(
            dk_ext, u.astype(f32), (((0,), (0,)), ((), ())), precision=highest, preferred_element_type=f32
        )
    dq_ref[...] = (jnp.where(low_half, dqs[0], dqs[1]) * 0.125).astype(bf16)
    dk_ref[...] = jnp.where(low_half, dks[0], dks[1]).astype(bf16)
    dv_ref[...] = jnp.where(low_half, dvs[0], dvs[1]).astype(bf16)


def attend_bwd(qkv, do, lse, u, g, mask):
    wins = mask.shape[0]
    width = qkv.shape[1] // 3
    pairs = width // 128
    tile = jax.ShapeDtypeStruct((wins * TOK, width), bf16)
    spec = pl.BlockSpec((TOK, 128), lambda w, h: (w, h))
    return pl.pallas_call(
        attend_bwd_kernel,
        grid=(wins, pairs),
        in_specs=[
            pl.BlockSpec((TOK, 128), lambda w, h: (w, h)),
            pl.BlockSpec((TOK, 128), lambda w, h: (w, pairs + h)),
            pl.BlockSpec((TOK, 128), lambda w, h: (w, 2 * pairs + h)),
            spec,
            pl.BlockSpec((1, 2, TOK, 1), lambda w, h: (w, h, 0, 0)),
            pl.BlockSpec((TOK, 128), lambda w, h: (0, 0)),
            pl.BlockSpec((2, TOK, 128), lambda w, h: (h, 0, 0)),
            pl.BlockSpec((1, TOK, 128), lambda w, h: (w, 0, 0)),
        ],
        out_specs=[spec, spec, spec, pl.BlockSpec((1, 2, 128, 128), lambda w, h: (w, h, 0, 0))],
        out_shape=[tile, tile, tile, jax.ShapeDtypeStruct((wins, 2 * pairs, 128, 128), f32)],
        name="attend_bwd",
    )(qkv, qkv, qkv, do, lse, u, g, mask)


def normalize(values):
    centre = jnp.mean(values, -1, keepdims=True)
    shifted = values - centre
    inv_std = lax.rsqrt(jnp.mean(shifted * shifted, -1, keepdims=True) + epsilon)
    return shifted * inv_std, inv_std


def normalize_back(grad_norm, normed, inv_std):
    return inv_std * (
        grad_norm
        - jnp.mean(grad_norm, -1, keepdims=True)
        - normed * jnp.mean(grad_norm * normed, -1, keepdims=True)
    )


def gelu_parts(pre):
    gate = 0.5 * (1.0 + lax.erf(pre * inv_root_two))
    return pre * gate, gate + pre * inv_root_tau * jnp.exp(-0.5 * pre * pre)


def body(dims, tokens, cotangent, cond, clip_frames, window_clip, window_half, ada, qkv_w, out_w, up_w, down_w, table):
    A, B, C = dims
    devices = A * B * 2 * C
    micro, wl, toks, width = tokens.shape
    wins = micro * wl
    clips = cond.shape[0]
    n = lax.axis_index("narrow")
    x = tokens.reshape(wins, toks, width).astype(f32)
    dy = cotangent.reshape(wins, toks, width).astype(f32)
    ids = window_clip.reshape(wins)
    half = window_half.reshape(wins)

    cond_act = jax.nn.silu(cond.astype(f32)).astype(bf16)
    act_rows = lax.dynamic_slice_in_dim(cond_act, n * ada.shape[0], ada.shape[0], 1)
    mod_part = jnp.dot(act_rows, ada, preferred_element_type=f32)
    mod_blk = mod_part.reshape(-1, 128)
    blocks = [m.T for m in (qkv_w, out_w, up_w, down_w)]
    mod_full, *fulls = gather_all(dims, mod_blk, blocks)
    qkv_t, out_t, up_t, down_t = [f.reshape(-1, f.shape[-1]) for f in fulls]

    mod_all = mod_full.reshape(A * B * 2, C, clips, ada.shape[1]).sum(1)
    mod_all = mod_all.transpose(1, 0, 2).reshape(clips, -1)
    pick = (ids[:, None] == jnp.arange(clips)[None, :]).astype(f32)
    modulation = jnp.einsum("wc,ce->we", pick, mod_all, precision=highest).reshape(wins, 6, 1, width)

    live = jnp.clip(jnp.sum(pick.astype(jnp.int32) * clip_frames[None, :], 1) - WIN_FRAMES * half, 1, WIN_FRAMES)
    feats = jnp.asarray(position_features())
    sel = jnp.asarray(offset_selector())
    u = jnp.pad(feats, ((0, 0), (0, 11)))
    u = both_halves(u.at[:, 21].set(1.0)).astype(bf16)
    key_bias = jnp.einsum("iq,hqj->hji", jnp.eye(21, dtype=f32), jnp.einsum("qke,he,jk->hqj", sel, table.astype(f32), feats, precision=highest), precision=highest)
    g = both_halves(key_bias).astype(bf16)
    invalid = (jnp.arange(toks)[None, :] // (WIN_SIDE * WIN_SIDE)) >= live[:, None]
    lane = jnp.arange(128)
    mask = jnp.where(invalid[:, :, None] & (lane % 64 == 21)[None, None, :], -1e30, 0.0).astype(bf16)

    def flat(v):
        return v.reshape(wins * toks, v.shape[-1])

    def windows(v):
        return v.reshape(wins, toks, v.shape[-1])

    norm1, inv1 = normalize(x)
    hidden1 = flat((norm1 * (1.0 + modulation[:, 1]) + modulation[:, 0]).astype(bf16))
    qkv = nt(hidden1, qkv_t).astype(bf16)
    heads, lse = attend_fwd(qkv, u, g, mask)
    attended = windows(nt(heads, out_t))
    mid = x + modulation[:, 2] * attended
    norm2, inv2 = normalize(mid)
    hidden2 = flat((norm2 * (1.0 + modulation[:, 4]) + modulation[:, 3]).astype(bf16))
    pre = nt(hidden2, up_t)
    act, slope = gelu_parts(pre)
    act = act.astype(bf16)
    ffn = windows(nt(act, down_t))
    mixed = (mid + modulation[:, 5] * ffn).astype(bf16)

    d_gate2 = jnp.sum(dy * ffn, 1)
    d_ffn = flat((modulation[:, 5] * dy).astype(bf16))
    g_down = tn(d_ffn, act).astype(bf16)
    d_pre = (nn(d_ffn, down_t) * slope).astype(bf16)
    g_up = tn(d_pre, hidden2).astype(bf16)
    d_hidden2 = windows(nn(d_pre, up_t))
    d_shift2 = jnp.sum(d_hidden2, 1)
    d_scale2 = jnp.sum(d_hidden2 * norm2, 1)
    d_mid = dy + normalize_back(d_hidden2 * (1.0 + modulation[:, 4]), norm2, inv2)
    d_gate1 = jnp.sum(d_mid * attended, 1)
    d_att = flat((modulation[:, 2] * d_mid).astype(bf16))
    g_out = tn(d_att, heads).astype(bf16)
    d_heads = nn(d_att, out_t).astype(bf16)
    dq, dk, dv, z = attend_bwd(qkv, d_heads, lse, u, g, mask)
    d_qkv = jnp.concatenate([dq, dk, dv], 1)
    g_qkv = tn(d_qkv, hidden1).astype(bf16)
    d_hidden1 = windows(nn(d_qkv, qkv_t))
    d_shift1 = jnp.sum(d_hidden1, 1)
    d_scale1 = jnp.sum(d_hidden1 * norm1, 1)
    grad_x = d_mid + normalize_back(d_hidden1 * (1.0 + modulation[:, 1]), norm1, inv1)

    d_mod = jnp.concatenate([d_shift1, d_scale1, d_gate1, d_shift2, d_scale2, d_gate2], 1).astype(bf16)
    zsum = jnp.sum(z, 0)
    pairs_z = jnp.stack([zsum[0::2, 64:85, :21], zsum[1::2, 0:21, :21]], 1).reshape(HEADS, 21, 21)
    table_part = jnp.einsum("hqk,qke->he", pairs_z, sel, precision=highest)
    table_blk = jnp.pad(table_part, ((0, 0), (0, 128 - table_part.shape[1])))
    table_blk = table_blk.at[0, 128 - wins :].set(ids.astype(f32))

    shaped = [
        full.reshape(f.shape) for full, f in zip((g_down, g_up, g_out, g_qkv), (fulls[3], fulls[2], fulls[1], fulls[0]))
    ]
    r_down, r_up, r_out, r_qkv, mod_grads, table_parts = scatter_all(
        dims, shaped, [d_mod.reshape(-1, 128), table_blk]
    )
    table_parts = table_parts.reshape(devices, HEADS, 128)
    grad_table = table_parts.sum(0)[:, : table.shape[1]]
    all_ids = table_parts[:, 0, 128 - wins :].reshape(devices, micro, wl).transpose(1, 0, 2).reshape(-1)

    w = lax.axis_index("wide")
    ncol = ada.shape[1]
    dm = mod_grads.reshape(devices, micro, wl, 6 * width)
    dm = lax.dynamic_slice_in_dim(dm, w * ncol, ncol, 3)
    dm = dm.transpose(1, 0, 2, 3).reshape(-1, ncol)
    picked = (all_ids[:, None] == jnp.arange(clips, dtype=f32)[None, :]).astype(f32)
    by_clip = jnp.einsum("wc,we->ce", picked, dm.astype(f32), precision=highest)
    grad_ada = jnp.einsum("cr,ce->re", act_rows.astype(f32), by_clip, precision=highest)
    return (
        mixed.reshape(tokens.shape),
        grad_x.reshape(tokens.shape),
        grad_ada,
        r_qkv.T,
        r_out.T,
        r_up.T,
        r_down.T,
        grad_table,
    )


def solution(mesh):
    W, C = mesh.shape["wide"], mesh.shape["narrow"]
    A = min(4, W // 2)
    dims = (A, W // 2 // A, C)
    sh = ("wide", "narrow")
    weight = P("narrow", "wide")
    return jax.shard_map(
        functools.partial(body, dims),
        mesh=mesh,
        in_specs=(P(None, sh), P(None, sh), P(), P(), P(None, sh), P(None, sh)) + (weight,) * 5 + (P(),),
        out_specs=(P(None, sh), P(None, sh)) + (weight,) * 5 + (P(),),
        check_vma=False,
    )
```

```python
import functools
import math

import jax
import jax.numpy as jnp
import numpy as np
from jax import lax
from jax.experimental import pallas as pl
from jax.experimental.pallas import tpu as pltpu
from jax.sharding import PartitionSpec as P

HEADS = 16
WIN_FRAMES = 5
WIN_SIDE = 8
TOK = WIN_FRAMES * WIN_SIDE * WIN_SIDE
F_SPAN = 2 * WIN_FRAMES - 1
S_SPAN = 2 * WIN_SIDE - 1
epsilon = 1e-06
inv_root_two = 0.7071067811865476
inv_root_tau = 0.3989422804014327
highest = lax.Precision.HIGHEST
MESH = pl.DeviceIdType.MESH
bf16 = jnp.bfloat16
f32 = jnp.float32


def position_features():
    p = np.arange(TOK)
    feats = np.zeros((TOK, WIN_FRAMES + 2 * WIN_SIDE), np.float32)
    feats[p, p // 64] = 1
    feats[p, WIN_FRAMES + (p // 8) % 8] = 1
    feats[p, WIN_FRAMES + WIN_SIDE + p % 8] = 1
    return feats


def offset_selector():
    sel = np.zeros((21, 21, F_SPAN + 2 * S_SPAN), np.float32)
    for i in range(WIN_FRAMES):
        for j in range(WIN_FRAMES):
            sel[i, j, i - j + WIN_FRAMES - 1] = 1
    for i in range(WIN_SIDE):
        for j in range(WIN_SIDE):
            sel[5 + i, 5 + j, F_SPAN + i - j + WIN_SIDE - 1] = 1
            sel[13 + i, 13 + j, F_SPAN + S_SPAN + i - j + WIN_SIDE - 1] = 1
    return sel


def nt(lhs, rhs):
    return lax.dot_general(lhs, rhs, (((1,), (1,)), ((), ())), preferred_element_type=f32)


def nn(lhs, rhs):
    return lax.dot_general(lhs, rhs, (((1,), (0,)), ((), ())), preferred_element_type=f32)


def tn(lhs, rhs):
    return lax.dot_general(lhs, rhs, (((0,), (0,)), ((), ())), preferred_element_type=f32)


def normalize(values):
    centre = jnp.mean(values, -1, keepdims=True)
    shifted = values - centre
    inv_std = lax.rsqrt(jnp.mean(shifted * shifted, -1, keepdims=True) + epsilon)
    return shifted * inv_std, inv_std


def normalize_back(grad_norm, normed, inv_std):
    return inv_std * (
        grad_norm
        - jnp.mean(grad_norm, -1, keepdims=True)
        - normed * jnp.mean(grad_norm * normed, -1, keepdims=True)
    )


def gelu_parts(pre):
    gate = 0.5 * (1.0 + lax.erf(pre * inv_root_two))
    return pre * gate, gate + pre * inv_root_tau * jnp.exp(-0.5 * pre * pre)


def guard(cond, fn):
    if isinstance(cond, bool):
        if cond:
            fn()
    else:
        pl.when(cond)(fn)


def both(*conds):
    total = True
    for cond in conds:
        if isinstance(cond, bool):
            if not cond:
                return False
        elif total is True:
            total = cond
        else:
            total = jnp.logical_and(total, cond)
    return total


def loop(count, fn):
    def step(i, carry):
        fn(i)
        return carry

    lax.fori_loop(0, count, step, 0)


def cols(c, K):
    return pl.ds(pl.multiple_of(c * K, K), K)


class Place:
    def __init__(self, dims):
        self.A, self.B, self.C = dims
        w = lax.axis_index("wide")
        self.c = lax.axis_index("narrow")
        self.k = lax.rem(w, 2)
        self.b = lax.rem(w // 2, self.B)
        self.a = w // (2 * self.B)

    def dev(self, a=None, b=None, k=None, c=None):
        a = self.a if a is None else a
        b = self.b if b is None else b
        k = self.k if k is None else k
        c = self.c if c is None else c
        return ((a * self.B + b) * 2 + k, c)

    def a_peer(self, d):
        return lax.rem(self.a + d, self.A)

    def b_peer(self, d):
        return lax.rem(self.b + d, self.B)

    def c_peer(self, d):
        return lax.rem(self.c + d, self.C)

    def barrier(self):
        peers = [self.dev(a=self.a_peer(d)) for d in range(1, self.A)]
        peers += [self.dev(b=self.b_peer(d)) for d in range(1, self.B)]
        peers += [self.dev(c=self.c_peer(d)) for d in range(1, self.C)]
        peers += [self.dev(k=1 - self.k)]
        sem = pltpu.get_barrier_semaphore()
        for peer in peers:
            pl.semaphore_signal(sem, inc=1, device_id=peer, device_id_type=MESH)
        pl.semaphore_wait(sem, len(peers))


def remote(src, dst, ssem, rsem, dev):
    return pltpu.make_async_remote_copy(
        src_ref=src, dst_ref=dst, send_sem=ssem, recv_sem=rsem, device_id=dev, device_id_type=MESH
    )


class Gather:
    def __init__(self, place, blocks, full, ssem, rsem):
        self.p, self.blocks, self.full, self.ssem, self.rsem = place, blocks, full, ssem, rsem
        self.Rp, self.K = blocks.shape[1], blocks.shape[2]
        self.count = blocks.shape[0]

    @staticmethod
    def sems(dims):
        A, B, C = dims
        return 2 * (A - 1) + 2 * (B - 1 + C - 1) + 1

    def along(self, t, ref, axis, base):
        p = self.p
        made = []
        for d in range(1, p.B if axis == "b" else p.C):
            dev = p.dev(b=p.b_peer(d)) if axis == "b" else p.dev(c=p.c_peer(d))
            made.append(remote(ref, ref, self.ssem.at[t, base + d - 1], self.rsem.at[t, base + d - 1], dev))
        return made

    def copies(self, t, phase, half=0):
        p, full = self.p, self.full
        h = self.Rp // 2
        rows = pl.ds(half * h, h)
        mine = cols(p.c, self.K)
        nA, nB, nC = p.A - 1, p.B - 1, p.C - 1
        if phase == 0:
            made = []
            for d in range(1, p.A):
                s = half * nA + d - 1
                made.append(
                    remote(
                        self.blocks.at[t, rows, :],
                        full.at[t, p.a, p.b, p.k, rows, mine],
                        self.ssem.at[t, s],
                        self.rsem.at[t, s],
                        p.dev(a=p.a_peer(d)),
                    )
                )
            return made
        if phase == 1:
            ref = full.at[t, :, p.b, p.k, rows, mine]
            return self.along(t, ref, "b", 2 * nA) if half == 0 else self.along(t, ref, "c", 2 * nA + nB)
        base = 2 * nA + nB + nC
        if phase == 2:
            if half == 0:
                return self.along(t, full.at[t, :, :, p.k, rows, mine], "c", base)
            return self.along(t, full.at[t, :, p.b, p.k, rows, :], "b", base + nC)
        s = base + nB + nC
        ref = full.at[t, :, :, p.k]
        return [remote(ref, ref, self.ssem.at[t, s], self.rsem.at[t, s], p.dev(k=1 - p.k))]

    def start(self, t, phase, half=0):
        for copy in self.copies(t, phase, half):
            copy.start()

    def landed(self, t, phase, half=0):
        for copy in self.copies(t, phase, half):
            copy.wait_recv()

    def first(self, t):
        for half in (0, 1):
            self.start(t, 0, half)

    def slot(self, s, ahead):
        n = self.count

        def advance(t, phase):
            def run():
                for half in (0, 1):
                    self.landed(t, phase - 1, half)
                    if phase < 3:
                        self.start(t, phase, half)
                if phase == 3:
                    self.start(t, 3)

            guard(both(t >= 0, t < n), run)

        guard(s + ahead < n, lambda: self.first(s + ahead))
        for phase in (1, 2, 3):
            advance(s - phase + 1, phase)
        guard(both(s - 3 >= 0, s - 3 < n), lambda: self.landed(s - 3, 3))

    def drain(self):
        def one(t):
            for phase in range(4):
                for half in (0, 1) if phase < 3 else (0,):
                    for copy in self.copies(t, phase, half):
                        copy.wait_send()

        loop(self.count, one)


class Scatter:
    def __init__(self, place, st, held, c0, b1, b0, c1, ra, fin, out, ssem, rsem, fsem):
        self.p, self.st, self.held = place, st, held
        self.c0, self.b1, self.b0, self.c1, self.ra, self.fin, self.out = c0, b1, b0, c1, ra, fin, out
        self.ssem, self.rsem, self.fsem = ssem, rsem, fsem
        self.Rp, self.K = ra.shape[2], ra.shape[3]
        self.count = held.shape[0]

    @staticmethod
    def sems(dims):
        A, B, C = dims
        return 1 + 2 * (B - 1 + C - 1) + (A - 1)

    def one(self, r, s, src, dst, dev):
        return remote(src, dst, self.ssem.at[r, s], self.rsem.at[r, s], dev)

    def sibling(self, r, slot):
        p = self.p
        return self.one(r, 0, self.st[slot].at[:, :, 1 - p.k], self.held.at[r], p.dev(k=1 - p.k))

    def copies(self, r, phase):
        p, K, held = self.p, self.K, self.held
        h = self.Rp // 2
        r0, r1 = pl.ds(0, h), pl.ds(h, h)
        mine = cols(p.c, K)
        nB, nC = p.B - 1, p.C - 1
        made = []
        if phase == 1:
            for d in range(1, p.C):
                made.append(
                    self.one(r, d, held.at[r, :, :, r0, cols(p.c_peer(d), K)], self.c0.at[r, d - 1], p.dev(c=p.c_peer(d)))
                )
            for d in range(1, p.B):
                made.append(
                    self.one(r, nC + d, held.at[r, :, p.b_peer(d), r1, :], self.b1.at[r, d - 1], p.dev(b=p.b_peer(d)))
                )
        elif phase == 2:
            base = nB + nC
            for d in range(1, p.B):
                made.append(
                    self.one(r, base + d, held.at[r, :, p.b_peer(d), r0, mine], self.b0.at[r, d - 1], p.dev(b=p.b_peer(d)))
                )
            base += nB
            for d in range(1, p.C):
                made.append(
                    self.one(
                        r, base + d, held.at[r, :, p.b, r1, cols(p.c_peer(d), K)], self.c1.at[r, d - 1], p.dev(c=p.c_peer(d))
                    )
                )
        else:
            base = 2 * (nB + nC)
            for d in range(1, p.A):
                made.append(
                    self.one(r, base + d, held.at[r, p.a_peer(d), p.b, :, mine], self.ra.at[r, d - 1], p.dev(a=p.a_peer(d)))
                )
        return made

    def start(self, r, phase):
        for copy in self.copies(r, phase):
            copy.start()

    def landed(self, r, phase):
        for copy in self.copies(r, phase):
            copy.wait_recv()

    def flush(self, r, slot):
        p = self.p
        copy = self.sibling(r, slot)
        copy.wait_recv()

        def add(i):
            a, b = i // p.B, lax.rem(i, p.B)
            self.held[r, a, b] = self.held[r, a, b] + self.st[slot][a, b, p.k]

        loop(p.A * p.B, add)
        copy.wait_send()
        self.start(r, 1)

    def mid(self, r):
        p, held = self.p, self.held
        h = self.Rp // 2
        r0, r1 = pl.ds(0, h), pl.ds(h, h)
        mine = cols(p.c, self.K)
        self.landed(r, 1)

        def add0(i):
            a, b = i // p.B, lax.rem(i, p.B)
            total = held[r, a, b, r0, mine]
            for d in range(p.C - 1):
                total = total + self.c0[r, d, a, b]
            held[r, a, b, r0, mine] = total

        loop(p.A * p.B, add0)

        def add1(a):
            total = held[r, a, p.b, r1, :]
            for d in range(p.B - 1):
                total = total + self.b1[r, d, a]
            held[r, a, p.b, r1, :] = total

        loop(p.A, add1)
        self.start(r, 2)

    def late(self, r):
        p, held = self.p, self.held
        h = self.Rp // 2
        r0, r1 = pl.ds(0, h), pl.ds(h, h)
        mine = cols(p.c, self.K)
        self.landed(r, 2)

        def add(a):
            total = held[r, a, p.b, r0, mine]
            for d in range(p.B - 1):
                total = total + self.b0[r, d, a]
            held[r, a, p.b, r0, mine] = total
            other = held[r, a, p.b, r1, mine]
            for d in range(p.C - 1):
                other = other + self.c1[r, d, a]
            held[r, a, p.b, r1, mine] = other

        loop(p.A, add)
        self.start(r, 3)

    def result(self, r):
        s = lax.rem(r, 2)
        return pltpu.make_async_copy(self.fin.at[s], self.out.at[r], self.fsem.at[s])

    def last(self, r):
        p = self.p
        self.landed(r, 3)
        total = self.held[r, p.a, p.b, :, cols(p.c, self.K)].astype(f32)
        for d in range(p.A - 1):
            total = total + self.ra[r, d].astype(f32)
        guard(r >= 2, lambda: self.result(r - 2).wait())
        self.fin[lax.rem(r, 2)] = total
        self.result(r).start()

    def slot(self, u, top):
        guard(both(u >= 0, u < top), lambda: self.mid(u))
        guard(both(u >= 1, u - 1 < top), lambda: self.late(u - 1))
        guard(both(u >= 2, u - 2 < top), lambda: self.last(u - 2))

    def drain(self):
        def one(r):
            for phase in (1, 2, 3):
                for copy in self.copies(r, phase):
                    copy.wait_send()

        loop(self.count, one)
        for r in (self.count - 2, self.count - 1):
            self.result(r).wait()


class Spread:
    def __init__(self, place, block, full, axes, ssem, rsem, base):
        p = place
        self.p, self.block, self.full, self.axes = p, block, full, axes
        self.ssem, self.rsem, self.base = ssem, rsem, base

    def copies(self, phase):
        p = self.p
        with_c = "c" in self.axes
        tail = (p.c,) if with_c else ()
        axis = self.axes[phase]
        base = self.base
        for done in self.axes[:phase]:
            base += {"a": p.A - 1, "b": p.B - 1, "c": p.C - 1, "k": 1}[done]
        every = slice(None)
        done = self.axes[:phase]
        index = (
            every if "a" in done else p.a,
            every if "b" in done else p.b,
            every if "k" in done else p.k,
        )
        if with_c:
            index += (every if "c" in done else p.c,)
        dst = self.full.at[index]
        src = self.block if phase == 0 else dst
        made = []
        count = {"a": p.A, "b": p.B, "c": p.C, "k": 2}[axis]
        for d in range(1, count):
            dev = {
                "a": lambda: p.dev(a=p.a_peer(d)),
                "b": lambda: p.dev(b=p.b_peer(d)),
                "c": lambda: p.dev(c=p.c_peer(d)),
                "k": lambda: p.dev(k=1 - p.k),
            }[axis]()
            s = base + d - 1
            made.append(remote(src, dst, self.ssem.at[s], self.rsem.at[s], dev))
        return made

    def start(self, phase):
        for copy in self.copies(phase):
            copy.start()

    def landed(self, phase):
        for copy in self.copies(phase):
            copy.wait_recv()

    def drain(self):
        for phase in range(len(self.axes)):
            for copy in self.copies(phase):
                copy.wait_send()


LOOKAHEAD = 2
ROWS = 32
NAMES_IN = (
    "mod_blk", "blocks", "x_in", "dy_in", "pick", "uq", "uk", "ut", "tmat", "selv", "ids_row",
)
NAMES_OUT = (
    "full", "mixed", "gx", "rout", "dmf", "tf",
)
NAMES_SCRATCH = (
    "x", "dy", "hid", "dff", "qkv", "heads", "mid", "ffn", "dh2", "wbuf", "mod", "dmod", "modx", "modf", "ms",
    "zacc", "tb", "dmb", "st", "held", "c0", "b1", "b0", "c1", "ra", "fin", "in_sem", "w_sem", "own_sem",
    "o_sem", "g_s", "g_r", "r_s", "r_r", "f_sem", "m_s", "m_r", "s_s", "s_r",
)


def step_kernel(dims, wins, *refs):
    names = NAMES_IN + NAMES_OUT + NAMES_SCRATCH
    R = dict(zip(names, refs))
    p = Place(dims)
    A, B, C = dims
    T = wins * TOK
    D = 1024
    Rp = R["blocks"].shape[1]
    K = R["blocks"].shape[2]
    clips, ncol = R["mod_blk"].shape
    x, dy, hid, dff, qkv, heads = (R[n] for n in ("x", "dy", "hid", "dff", "qkv", "heads"))
    mid, ffn, dh2, wbuf, mod, dmod = (R[n] for n in ("mid", "ffn", "dh2", "wbuf", "mod", "dmod"))
    full = R["full"]
    rows_per_win = TOK // ROWS

    loads = [
        pltpu.make_async_copy(R["x_in"], x, R["in_sem"].at[0]),
        pltpu.make_async_copy(R["dy_in"], dy, R["in_sem"].at[1]),
        pltpu.make_async_copy(R["mod_blk"], R["modx"].at[C - 1], R["in_sem"].at[2]),
    ]
    for copy in loads:
        copy.start()
    p.barrier()
    gather = Gather(p, R["blocks"], full, R["g_s"], R["g_r"])
    scatter = Scatter(
        p, [R["st"].at[0], R["st"].at[1], wbuf.at[0]], R["held"], R["c0"], R["b1"], R["b0"], R["c1"], R["ra"], R["fin"], R["rout"], R["r_s"], R["r_r"], R["f_sem"]
    )

    def mod_c():
        return [
            remote(R["mod_blk"], R["modx"].at[d - 1], R["m_s"].at[d - 1], R["m_r"].at[d - 1], p.dev(c=p.c_peer(d)))
            for d in range(1, C)
        ]

    for copy in mod_c():
        copy.start()
    own = pltpu.make_async_copy(R["blocks"], full.at[:, p.a, p.b, p.k, :, cols(p.c, K)], R["own_sem"].at[0])
    own.start()
    for t in range(LOOKAHEAD):
        gather.first(t)
    spread = Spread(p, R["ms"], R["modf"], "abk", R["m_s"], R["m_r"], C - 1)
    loads[2].wait()
    for copy in mod_c():
        copy.wait_recv()
    total = R["modx"][C - 1]
    for d in range(C - 1):
        total = total + R["modx"][d]
    R["ms"][...] = total
    own_ms = pltpu.make_async_copy(R["ms"], R["modf"].at[p.a, p.b, p.k], R["own_sem"].at[1])
    own_ms.start()
    spread.start(0)
    own.wait()
    gather.slot(0, LOOKAHEAD)
    own_ms.wait()
    spread.landed(0)
    spread.start(1)
    gather.slot(1, LOOKAHEAD)
    spread.landed(1)
    spread.start(2)
    gather.slot(2, LOOKAHEAD)
    spread.landed(2)

    piece = math.gcd(ncol, 128)
    for w in range(2 * A * B):
        blk = R["modf"][w // (2 * B), (w // 2) % B, w % 2]
        for win in range(wins):
            row = jnp.sum(R["pick"][win] * blk, 0, keepdims=True)
            for i in range(ncol // piece):
                col = w * ncol + i * piece
                mod[win * 6 + col // D, :, col % D : col % D + piece] = row[:, i * piece : (i + 1) * piece]
    for copy in loads[:2]:
        copy.wait()

    def rows_loop(fn):
        def run(i):
            win = i // rows_per_win
            fn(pl.ds(pl.multiple_of(i * ROWS, ROWS), ROWS), win * 6)

        loop(T // ROWS, run)

    def make_hidden1():
        def run(rows, m):
            norm, _ = normalize(x[rows, :].astype(f32))
            hid[rows, :] = (norm * (1.0 + mod[m + 1]) + mod[m]).astype(bf16)

        rows_loop(run)

    make_hidden1()
    for i in range(wins * 6):
        dmod[i] = jnp.zeros((1, D), f32)
    loop(HEADS, lambda h: R["zacc"].__setitem__(h, jnp.zeros((32, 128), f32)))

    def weight(t, slot):
        return pltpu.make_async_copy(full.at[t], wbuf.at[slot], R["w_sem"].at[slot])

    for s in (3, 4, 5):
        gather.slot(s, LOOKAHEAD)
        weight(s - 3, s - 3).start()
    for t in range(3):
        weight(t, t).wait()

    def qkv_rows(a, first):
        parts = []
        for b in range(B):
            for k in range(2):
                for t in range(3):
                    parts.append(wbuf[first + t, a, b, k])
        return jnp.concatenate(parts, 0)

    def qkv_cols(a):
        return pl.ds(pl.multiple_of(a * (3 * D // A), 128), 3 * D // A)

    def qkv_step(a):
        qkv[:, qkv_cols(a)] = nt(hid[...], qkv_rows(a, 0)).astype(bf16)

    loop(A, qkv_step)
    gather.slot(6, LOOKAHEAD)
    weight(3, 3).start()

    pairs = D // 128
    low_half = lax.broadcasted_iota(jnp.int32, (TOK, 128), 1) < 64

    def head_refs(i):
        win, pair = i // pairs, lax.rem(i, pairs)
        rows = pl.ds(pl.multiple_of(win * TOK, TOK), TOK)
        spots = [pl.ds(pl.multiple_of(j * D + pair * 128, 128), 128) for j in range(3)]
        return win, pair, rows, spots

    def extended(win, pair, q, k, h):
        own_lanes = low_half if h == 0 else jnp.logical_not(low_half)
        bias = nn(R["uk"][win], R["tmat"][pair * 2 + h]).astype(bf16)
        return own_lanes, jnp.where(own_lanes, q, R["uq"][...]), jnp.where(own_lanes, k, bias)

    def attend(i):
        win, pair, rows, spots = head_refs(i)
        q = qkv[rows, spots[0]] * jnp.asarray(0.125, bf16)
        k, v = qkv[rows, spots[1]], qkv[rows, spots[2]]
        got = []
        for h in range(2):
            _, q_ext, k_ext = extended(win, pair, q, k, h)
            s = nt(q_ext, k_ext)
            e = jnp.exp(s - jnp.max(s, -1, keepdims=True))
            probs = e * (1.0 / jnp.sum(e, -1, keepdims=True))
            got.append(nn(probs.astype(bf16), v))
        heads[rows, spots[0]] = jnp.where(low_half, got[0], got[1]).astype(bf16)
        guard(i == 4, lambda: gather.slot(7, LOOKAHEAD))
        guard(i == 12, lambda: gather.slot(8, LOOKAHEAD))

    loop(wins * pairs, attend)
    weight(4, 0).start()
    weight(5, 1).start()
    weight(3, 3).wait()
    quarter = D // A

    def quarter_cols(a):
        return pl.ds(pl.multiple_of(a * quarter, 128), quarter)

    def out_step(a):
        got = nt(heads[...], wbuf[3, a].reshape(quarter, D))
        at = quarter_cols(a)
        for win in range(wins):
            rows = slice(win * TOK, (win + 1) * TOK)
            mid[rows, at] = x[rows, at].astype(f32) + mod[win * 6 + 2, :, at] * got[rows]

    loop(A, out_step)

    def second_norm(rows, m):
        norm, _ = normalize(mid[rows, :])
        hid[rows, :] = (norm * (1.0 + mod[m + 4]) + mod[m + 3]).astype(bf16)
        dff[rows, :] = (mod[m + 5] * dy[rows, :].astype(f32)).astype(bf16)
        ffn[rows, :] = jnp.zeros((ROWS, D), f32)
        dh2[rows, :] = jnp.zeros((ROWS, D), f32)

    rows_loop(second_norm)

    st = R["st"]
    F = 512

    def ffn_step(s):
        q, hf = s // 2, lax.rem(s, 2)
        su = 2 * lax.rem(q, 2)

        @pl.when(hf == 0)
        def _():
            weight(4 + 2 * q, su).wait()
            weight(5 + 2 * q, su + 1).wait()

        up = wbuf[su, pl.ds(hf * (A // 2), A // 2)].reshape(F, D)
        at = pl.ds(pl.multiple_of(hf * F, F), F)
        down = wbuf[su + 1, :, :, :, :, at].reshape(D, F)
        act, slope = gelu_parts(nt(hid[...], up))
        act = act.astype(bf16)
        ffn[...] += nt(act, down)
        d_pre = (nn(dff[...], down) * slope).astype(bf16)
        dh2[...] += nn(d_pre, up)

        @pl.when(jnp.logical_and(hf == 0, q > 0))
        def _():
            scatter.flush(2 * q - 2, 0)
            scatter.flush(2 * q - 1, 1)

        st[0, pl.ds(hf * (A // 2), A // 2)] = tn(d_pre, hid[...]).astype(bf16).reshape(A // 2, B, 2, Rp, D)
        st[1, :, :, :, :, at] = tn(dff[...], act).astype(bf16).reshape(A, B, 2, Rp, F)

        @pl.when(hf == 1)
        def _():
            scatter.sibling(2 * q, 0).start()
            scatter.sibling(2 * q + 1, 1).start()

        gather.slot(9 + s, LOOKAHEAD)
        scatter.slot(s - 3, 12)

        @pl.when(jnp.logical_and(hf == 1, q < 3))
        def _():
            weight(6 + 2 * q, 2 - su).start()
            weight(7 + 2 * q, 3 - su).start()

    loop(8, ffn_step)
    weight(3, 0).start()
    scatter.flush(6, 0)
    scatter.flush(7, 1)
    weight(0, 1).start()
    weight(1, 2).start()
    weight(2, 3).start()

    def second_back(rows, m):
        norm, inv = normalize(mid[rows, :])
        dyr = dy[rows, :].astype(f32)
        fo = ffn[rows, :]
        dh = dh2[rows, :]
        dmod[m + 5] += jnp.sum(dyr * fo, 0, keepdims=True)
        dmod[m + 3] += jnp.sum(dh, 0, keepdims=True)
        dmod[m + 4] += jnp.sum(dh * norm, 0, keepdims=True)
        dy[rows, :] = (mid[rows, :] + mod[m + 5] * fo).astype(bf16)
        ffn[rows, :] = jnp.zeros((ROWS, D), f32)
        d_mid = dyr + normalize_back(dh * (1.0 + mod[m + 4]), norm, inv)
        dh2[rows, :] = d_mid
        dff[rows, :] = (mod[m + 2] * d_mid).astype(bf16)

    rows_loop(second_back)
    mixed_out = pltpu.make_async_copy(dy, R["mixed"], R["o_sem"].at[0])
    mixed_out.start()
    scatter.slot(5, 12)
    weight(3, 0).wait()

    def out_back(a):
        at = quarter_cols(a)
        wide = wbuf[0, a].reshape(quarter, D)
        attended = nt(heads[...], wide)
        for win in range(wins):
            rows = slice(win * TOK, (win + 1) * TOK)
            dmod[win * 6 + 2, :, at] = jnp.sum(dh2[rows, at] * attended[rows], 0, keepdims=True)
        st[0, a] = tn(dff[:, at], heads[...]).astype(bf16).reshape(B, 2, Rp, D)
        hid[:, at] = nn(dff[...], wbuf[0, :, :, :, :, at].reshape(D, quarter)).astype(bf16)

    loop(A, out_back)
    scatter.sibling(8, 0).start()
    scatter.slot(6, 12)

    def attend_back(i):
        win, pair, rows, spots = head_refs(i)
        q = qkv[rows, spots[0]] * jnp.asarray(0.125, bf16)
        k, v = qkv[rows, spots[1]], qkv[rows, spots[2]]
        do = hid[rows, spots[0]]
        zero = jnp.zeros((TOK, 128), bf16)
        dqs, dks, dvs = [], [], []
        for h in range(2):
            own_lanes, q_ext, k_ext = extended(win, pair, q, k, h)
            s = nt(k_ext, q_ext)
            e = jnp.exp(s - jnp.max(s, 0, keepdims=True))
            probs = e * (1.0 / jnp.sum(e, 0, keepdims=True))
            dvs.append(nn(probs.astype(bf16), do))
            dp = nt(v, jnp.where(own_lanes, do, zero))
            ds = (probs * (dp - jnp.sum(probs * dp, 0, keepdims=True))).astype(bf16)
            dqs.append(tn(ds, k))
            dk = nn(ds, q_ext)
            dks.append(dk)
            bias_part = jnp.where(own_lanes, 0.0, dk)
            top = bias_part.astype(bf16)
            rest = (bias_part - top.astype(f32)).astype(bf16)
            R["zacc"][pair * 2 + h] += nn(R["ut"][...], top) + nn(R["ut"][...], rest)
        qkv[rows, spots[0]] = (jnp.where(low_half, dqs[0], dqs[1]) * 0.125).astype(bf16)
        qkv[rows, spots[1]] = jnp.where(low_half, dks[0], dks[1]).astype(bf16)
        qkv[rows, spots[2]] = jnp.where(low_half, dvs[0], dvs[1]).astype(bf16)
        guard(i == 1, lambda: scatter.flush(8, 0))
        guard(i == 4, lambda: scatter.slot(7, 9))
        guard(i == 7, lambda: scatter.slot(8, 9))
        guard(i == 10, lambda: scatter.slot(9, 9))
        guard(i == 13, lambda: scatter.slot(10, 9))

    loop(wins * pairs, attend_back)
    make_hidden1()
    for t in range(3):
        weight(t, t + 1).wait()

    def qkv_grad(a):
        got = tn(qkv[:, qkv_cols(a)], hid[...]).astype(bf16)
        i = 0
        for b in range(B):
            for k in range(2):
                for t in range(3):
                    scatter.st[t][a, b, k] = got[i * Rp : (i + 1) * Rp]
                    i += 1

    loop(A, qkv_grad)
    for t in range(3):
        scatter.sibling(9 + t, t).start()

    def qkv_back(a):
        ffn[...] += nn(qkv[:, qkv_cols(a)], qkv_rows(a, 1))
        guard(a == 0, lambda: scatter.flush(9, 0))
        guard(a == 1, lambda: scatter.flush(10, 1))
        guard(a == 2, lambda: scatter.flush(11, 2))

    loop(A, qkv_back)
    scatter.mid(9)

    def first_back(rows, m):
        norm, inv = normalize(x[rows, :].astype(f32))
        dh = ffn[rows, :]
        dmod[m] += jnp.sum(dh, 0, keepdims=True)
        dmod[m + 1] += jnp.sum(dh * norm, 0, keepdims=True)
        mid[rows, :] = dh2[rows, :] + normalize_back(dh * (1.0 + mod[m + 1]), norm, inv)

    rows_loop(first_back)
    gx_out = pltpu.make_async_copy(mid, R["gx"], R["o_sem"].at[1])
    gx_out.start()
    filler = (-wins * 6) % 16
    stack = [dmod[i] for i in range(wins * 6)] + [jnp.zeros((1, D), f32)] * filler
    R["dmb"][...] = jnp.concatenate(stack, 0).astype(bf16)
    mods = Spread(p, R["dmb"], R["dmf"], "abck", R["s_s"].at[0], R["s_r"].at[0], 0)
    own_dm = pltpu.make_async_copy(R["dmb"], R["dmf"].at[p.a, p.b, p.k, p.c], R["own_sem"].at[2])
    own_dm.start()
    mods.start(0)
    scatter.mid(10)
    scatter.late(9)

    table = R["ids_row"][...]
    for v in range(21):
        zv = R["zacc"][:, v, :]
        top = zv.astype(bf16)
        rest = (zv - top.astype(f32)).astype(bf16)
        table = table + nn(top, R["selv"][v]) + nn(rest, R["selv"][v])
    R["tb"][...] = table
    tabs = Spread(p, R["tb"], R["tf"], "abck", R["s_s"].at[1], R["s_r"].at[1], 0)
    own_tb = pltpu.make_async_copy(R["tb"], R["tf"].at[p.a, p.b, p.k, p.c], R["own_sem"].at[3])
    own_tb.start()
    tabs.start(0)
    own_dm.wait()
    own_tb.wait()
    for phase in (1, 2, 3):
        for small in (mods, tabs):
            small.landed(phase - 1)
            small.start(phase)
        if phase == 1:
            scatter.mid(11)
            scatter.late(10)
            scatter.last(9)
        if phase == 2:
            scatter.late(11)
            scatter.last(10)
    for small in (mods, tabs):
        small.landed(3)
    scatter.last(11)
    mixed_out.wait()
    gx_out.wait()
    gather.drain()
    scatter.drain()
    for copy in mod_c():
        copy.wait_send()
    for small in (spread, mods, tabs):
        small.drain()


def run_step(dims, wins, ins):
    A, B, C = dims
    blocks = ins[1]
    n, Rp, K = blocks.shape
    clips, ncol = ins[0].shape
    T = wins * TOK
    D = 1024
    h = Rp // 2
    hbm = pl.BlockSpec(memory_space=pltpu.HBM)
    vmem = pl.BlockSpec(memory_space=pltpu.VMEM)
    dm_rows = -(-wins * 6 // 16) * 16
    out_shape = [
        jax.ShapeDtypeStruct((n, A, B, 2, Rp, D), bf16),
        jax.ShapeDtypeStruct((T, D), bf16),
        jax.ShapeDtypeStruct((T, D), f32),
        jax.ShapeDtypeStruct((n, Rp, K), f32),
        jax.ShapeDtypeStruct((A, B, 2, C, dm_rows, D), bf16),
        jax.ShapeDtypeStruct((A, B, 2, C, HEADS, 128), f32),
    ]
    small = A - 1 + B - 1 + C - 1 + 1
    dma = pltpu.SemaphoreType.DMA
    scratch = [
        pltpu.VMEM((T, D), bf16),
        pltpu.VMEM((T, D), bf16),
        pltpu.VMEM((T, D), bf16),
        pltpu.VMEM((T, D), bf16),
        pltpu.VMEM((T, 3 * D), bf16),
        pltpu.VMEM((T, D), bf16),
        pltpu.VMEM((T, D), f32),
        pltpu.VMEM((T, D), f32),
        pltpu.VMEM((T, D), f32),
        pltpu.VMEM((4, A, B, 2, Rp, D), bf16),
        pltpu.VMEM((wins * 6, 1, D), f32),
        pltpu.VMEM((wins * 6, 1, D), f32),
        pltpu.VMEM((C, clips, ncol), f32),
        pltpu.VMEM((A, B, 2, clips, ncol), f32),
        pltpu.VMEM((clips, ncol), f32),
        pltpu.VMEM((HEADS, 32, 128), f32),
        pltpu.VMEM((HEADS, 128), f32),
        pltpu.VMEM((dm_rows, D), bf16),
        pltpu.VMEM((2, A, B, 2, Rp, D), bf16),
        pltpu.VMEM((n, A, B, Rp, D), bf16),
        pltpu.VMEM((n, C - 1, A, B, h, K), bf16),
        pltpu.VMEM((n, B - 1, A, h, D), bf16),
        pltpu.VMEM((n, B - 1, A, h, K), bf16),
        pltpu.VMEM((n, C - 1, A, h, K), bf16),
        pltpu.VMEM((n, A - 1, Rp, K), bf16),
        pltpu.VMEM((2, Rp, K), f32),
        dma((3,)),
        dma((4,)),
        dma((4,)),
        dma((2,)),
        dma((n, Gather.sems(dims))),
        dma((n, Gather.sems(dims))),
        dma((n, Scatter.sems(dims))),
        dma((n, Scatter.sems(dims))),
        dma((2,)),
        dma((C - 1 + small,)),
        dma((C - 1 + small,)),
        dma((2, small)),
        dma((2, small)),
    ]
    return pl.pallas_call(
        functools.partial(step_kernel, dims, wins),
        out_shape=out_shape,
        in_specs=[hbm] * 4 + [vmem] * 7,
        out_specs=[hbm] * 6,
        scratch_shapes=scratch,
        compiler_params=pltpu.CompilerParams(
            collective_id=0, has_side_effects=True, vmem_limit_bytes=63 * 2**20
        ),
        name="block_step",
    )(*ins)


def body(dims, tokens, cotangent, cond, clip_frames, window_clip, window_half, ada, qkv_w, out_w, up_w, down_w, table):
    A, B, C = dims
    W = 2 * A * B
    devices = W * C
    micro, wl, toks, width = tokens.shape
    wins = micro * wl
    clips = cond.shape[0]
    n = lax.axis_index("narrow")
    w = lax.axis_index("wide")
    ids = window_clip.reshape(wins)
    half = window_half.reshape(wins)

    cond_act = jax.nn.silu(cond.astype(f32)).astype(bf16)
    act_rows = lax.dynamic_slice_in_dim(cond_act, n * ada.shape[0], ada.shape[0], 1)
    mod_blk = jnp.dot(act_rows, ada, preferred_element_type=f32)

    Rp = out_w.shape[1]
    K = out_w.shape[0]
    pieces = up_w.shape[1] // Rp
    up_t = up_w.T.reshape(pieces, Rp, K)
    down_t = down_w.reshape(-1, pieces, Rp, Rp).transpose(1, 3, 0, 2).reshape(pieces, Rp, K)
    ffn_t = jnp.stack([up_t, down_t], 1).reshape(2 * pieces, Rp, K)
    blocks = jnp.concatenate([qkv_w.T.reshape(3, Rp, K), out_w.T[None], ffn_t], 0)

    pick = (ids[:, None] == jnp.arange(clips)[None, :]).astype(f32)
    live = jnp.clip(jnp.sum(pick.astype(jnp.int32) * clip_frames[None, :], 1) - WIN_FRAMES * half, 1, WIN_FRAMES)
    feats = position_features()
    uq_const = np.zeros((toks, 128), np.float32)
    for first in (0, 64):
        uq_const[:, first : first + 21] = feats
        uq_const[:, first + 21] = 1
    uk_const = np.zeros((toks, 32), np.float32)
    uk_const[:, :21] = feats
    invalid = (jnp.arange(toks)[None, :] // (WIN_SIDE * WIN_SIDE)) >= live[:, None]
    spot = np.zeros((32,), np.float32)
    spot[21] = 1
    uk = (jnp.asarray(uk_const)[None] + invalid[:, :, None] * jnp.asarray(spot)).astype(bf16)
    sel = offset_selector()
    entries = sel.shape[2]
    spread = np.zeros((entries + 1, 32, 128), np.float32)
    for first in (0, 64):
        spread[:entries, :21, first : first + 21] = sel.transpose(2, 1, 0)
        spread[entries, 21, first + 21] = 1
    rows = jnp.concatenate([table, jnp.full((HEADS, 1), -1e30, bf16)], 1)
    tmat = jnp.dot(rows, jnp.asarray(spread.reshape(entries + 1, -1), bf16), preferred_element_type=f32)
    tmat = tmat.astype(bf16).reshape(HEADS, 32, 128)
    selv = np.zeros((21, 128, 128), np.float32)
    for first in (0, 64):
        selv[:, first : first + 21, :entries] = sel.transpose(1, 0, 2)
    ids_row = jnp.zeros((HEADS, 128), f32).at[0, 128 - wins :].set(ids.astype(f32))

    ins = (
        mod_blk,
        blocks,
        tokens.reshape(wins * toks, width),
        cotangent.reshape(wins * toks, width),
        pick[:, :, None],
        jnp.asarray(uq_const, bf16),
        uk,
        jnp.asarray(uk_const.T, bf16),
        tmat,
        jnp.asarray(selv, bf16),
        ids_row,
    )
    _, mixed, grad_x, rout, mod_grads, table_parts = run_step(dims, wins, ins)

    table_parts = table_parts.reshape(devices, HEADS, 128)
    grad_table = table_parts.sum(0)[:, : table.shape[1]]
    all_ids = table_parts[:, 0, 128 - wins :].reshape(devices, micro, wl).transpose(1, 0, 2).reshape(-1)
    ncol = ada.shape[1]
    dm = mod_grads.reshape(devices, -1, width)[:, : wins * 6].reshape(devices, micro, wl, 6 * width)
    dm = lax.dynamic_slice_in_dim(dm, w * ncol, ncol, 3)
    dm = dm.transpose(1, 0, 2, 3).reshape(-1, ncol)
    picked = (all_ids[:, None] == jnp.arange(clips, dtype=f32)[None, :]).astype(f32)
    by_clip = jnp.einsum("wc,we->ce", picked, dm.astype(f32), precision=highest)
    grad_ada = jnp.einsum("cr,ce->re", act_rows.astype(f32), by_clip, precision=highest)

    ffn_r = rout[: 2 * pieces].reshape(pieces, 2, Rp, K)
    g_up = ffn_r[:, 0].reshape(pieces * Rp, K).T
    g_down = ffn_r[:, 1].reshape(pieces, Rp, -1, Rp).transpose(2, 0, 3, 1).reshape(-1, Rp)
    g_out = rout[2 * pieces].T
    g_qkv = rout[2 * pieces + 1 :].reshape(3 * Rp, K).T
    return (
        mixed.reshape(tokens.shape),
        grad_x.reshape(tokens.shape),
        grad_ada,
        g_qkv,
        g_out,
        g_up,
        g_down,
        grad_table,
    )


def solution(mesh):
    W, C = mesh.shape["wide"], mesh.shape["narrow"]
    A = min(4, W // 2)
    dims = (A, W // 2 // A, C)
    sh = ("wide", "narrow")
    weight = P("narrow", "wide")
    return jax.shard_map(
        functools.partial(body, dims),
        mesh=mesh,
        in_specs=(P(None, sh), P(None, sh), P(), P(), P(None, sh), P(None, sh)) + (weight,) * 5 + (P(),),
        out_specs=(P(None, sh), P(None, sh)) + (weight,) * 5 + (P(),),
        check_vma=False,
    )
```

```python
import functools
import math

import jax
import jax.numpy as jnp
import numpy as np
from jax import lax
from jax.experimental import pallas as pl
from jax.experimental.pallas import tpu as pltpu
from jax.sharding import PartitionSpec as P

HEADS = 16
WIN_FRAMES = 5
WIN_SIDE = 8
TOK = WIN_FRAMES * WIN_SIDE * WIN_SIDE
F_SPAN = 2 * WIN_FRAMES - 1
S_SPAN = 2 * WIN_SIDE - 1
epsilon = 1e-06
inv_root_two = 0.7071067811865476
inv_root_tau = 0.3989422804014327
highest = lax.Precision.HIGHEST
MESH = pl.DeviceIdType.MESH
bf16 = jnp.bfloat16
f32 = jnp.float32


def position_features():
    p = np.arange(TOK)
    feats = np.zeros((TOK, WIN_FRAMES + 2 * WIN_SIDE), np.float32)
    feats[p, p // 64] = 1
    feats[p, WIN_FRAMES + (p // 8) % 8] = 1
    feats[p, WIN_FRAMES + WIN_SIDE + p % 8] = 1
    return feats


def offset_selector():
    sel = np.zeros((21, 21, F_SPAN + 2 * S_SPAN), np.float32)
    for i in range(WIN_FRAMES):
        for j in range(WIN_FRAMES):
            sel[i, j, i - j + WIN_FRAMES - 1] = 1
    for i in range(WIN_SIDE):
        for j in range(WIN_SIDE):
            sel[5 + i, 5 + j, F_SPAN + i - j + WIN_SIDE - 1] = 1
            sel[13 + i, 13 + j, F_SPAN + S_SPAN + i - j + WIN_SIDE - 1] = 1
    return sel


def nt(lhs, rhs):
    return lax.dot_general(lhs, rhs, (((1,), (1,)), ((), ())), preferred_element_type=f32)


def nn(lhs, rhs):
    return lax.dot_general(lhs, rhs, (((1,), (0,)), ((), ())), preferred_element_type=f32)


def tn(lhs, rhs):
    return lax.dot_general(lhs, rhs, (((0,), (0,)), ((), ())), preferred_element_type=f32)


def normalize(values):
    centre = jnp.mean(values, -1, keepdims=True)
    shifted = values - centre
    inv_std = lax.rsqrt(jnp.mean(shifted * shifted, -1, keepdims=True) + epsilon)
    return shifted * inv_std, inv_std


def normalize_back(grad_norm, normed, inv_std):
    return inv_std * (
        grad_norm
        - jnp.mean(grad_norm, -1, keepdims=True)
        - normed * jnp.mean(grad_norm * normed, -1, keepdims=True)
    )


def gelu_parts(pre):
    gate = 0.5 * (1.0 + lax.erf(pre * inv_root_two))
    return pre * gate, gate + pre * inv_root_tau * jnp.exp(-0.5 * pre * pre)


def guard(cond, fn):
    if isinstance(cond, bool):
        if cond:
            fn()
    else:
        pl.when(cond)(fn)


def both(*conds):
    total = True
    for cond in conds:
        if isinstance(cond, bool):
            if not cond:
                return False
        elif total is True:
            total = cond
        else:
            total = jnp.logical_and(total, cond)
    return total


def loop(count, fn):
    def step(i, carry):
        fn(i)
        return carry

    lax.fori_loop(0, count, step, 0)


def cols(c, K):
    return pl.ds(pl.multiple_of(c * K, K), K)


class Place:
    def __init__(self, dims):
        self.A, self.B, self.C = dims
        w = lax.axis_index("wide")
        self.c = lax.axis_index("narrow")
        self.k = lax.rem(w, 2)
        self.b = lax.rem(w // 2, self.B)
        self.a = w // (2 * self.B)

    def dev(self, a=None, b=None, k=None, c=None):
        a = self.a if a is None else a
        b = self.b if b is None else b
        k = self.k if k is None else k
        c = self.c if c is None else c
        return ((a * self.B + b) * 2 + k, c)

    def a_peer(self, d):
        return lax.rem(self.a + d, self.A)

    def b_peer(self, d):
        return lax.rem(self.b + d, self.B)

    def c_peer(self, d):
        return lax.rem(self.c + d, self.C)

    def barrier(self):
        peers = [self.dev(a=self.a_peer(d)) for d in range(1, self.A)]
        peers += [self.dev(b=self.b_peer(d)) for d in range(1, self.B)]
        peers += [self.dev(c=self.c_peer(d)) for d in range(1, self.C)]
        peers += [self.dev(k=1 - self.k)]
        sem = pltpu.get_barrier_semaphore()
        for peer in peers:
            pl.semaphore_signal(sem, inc=1, device_id=peer, device_id_type=MESH)
        pl.semaphore_wait(sem, len(peers))


def remote(src, dst, ssem, rsem, dev):
    return pltpu.make_async_remote_copy(
        src_ref=src, dst_ref=dst, send_sem=ssem, recv_sem=rsem, device_id=dev, device_id_type=MESH
    )


def peers_along(p, axis):
    if axis == "a":
        return [(p.a_peer(d), p.dev(a=p.a_peer(d))) for d in range(1, p.A)]
    if axis == "b":
        return [(p.b_peer(d), p.dev(b=p.b_peer(d))) for d in range(1, p.B)]
    return [(p.c_peer(d), p.dev(c=p.c_peer(d))) for d in range(1, p.C)]


def every_nth(t, n, spot):
    return t % n == spot if isinstance(t, int) else lax.rem(t, n) == spot


def by_kind(kind, fn):
    if isinstance(kind, bool):
        fn(kind)
    else:
        pl.when(kind)(lambda: fn(True))
        pl.when(jnp.logical_not(kind))(lambda: fn(False))


class Gather:
    ORDERS = {False: ("abc", "acb"), True: ("bac", "cab")}

    def __init__(self, place, blocks, full, ssem, rsem):
        self.p, self.blocks, self.full, self.ssem, self.rsem = place, blocks, full, ssem, rsem
        self.Rp, self.K = blocks.shape[1], blocks.shape[2]
        self.count = blocks.shape[0]
        self.size = {"a": place.A - 1, "b": place.B - 1, "c": place.C - 1}

    @staticmethod
    def kind(t):
        return every_nth(t, 2, 1)

    @staticmethod
    def sems(dims):
        A, B, C = dims
        return 2 * (A - 1 + B - 1 + C - 1) + 1 + 2

    def region(self, t, order, phase, half, a):
        p = self.p
        done = order[:phase]
        every = slice(None)
        return self.full.at[
            t,
            every if "a" in done else a,
            every if "b" in done else p.b,
            p.k,
            pl.ds(half * (self.Rp // 2), self.Rp // 2),
            every if "c" in done else cols(p.c, self.K),
        ]

    def copies(self, t, mixed, phase, half=0):
        p = self.p
        if phase == 3:
            s = 2 * sum(self.size.values())
            ref = self.full.at[t, :, :, p.k]
            return [(True, remote(ref, ref, self.ssem.at[t, s], self.rsem.at[t, s], p.dev(k=1 - p.k)))]
        order = self.ORDERS[mixed][half]
        done, axis = order[:phase], order[phase]
        ref = self.region(t, order, phase, half, p.a)
        src = self.blocks.at[t, pl.ds(half * (self.Rp // 2), self.Rp // 2), :] if phase == 0 else ref
        base = half * sum(self.size.values()) + sum(self.size[x] for x in done)
        made = []
        for i, (_, dev) in enumerate(peers_along(p, axis)):
            when = True
            if axis == "a" and i == 0:
                when = p.a != p.A - 1
            if axis == "a" and i == p.A - 2:
                when = p.a != 0
            made.append((when, remote(src, ref, self.ssem.at[t, base + i], self.rsem.at[t, base + i], dev)))
        return made

    def relays(self, t, mixed, phase, half):
        p = self.p
        order = self.ORDERS[mixed][half]
        if phase == 3 or order[phase] != "a":
            return []
        base = half * sum(self.size.values()) + sum(self.size[x] for x in order[:phase])
        ref = self.region(t, order, phase, half, p.a_peer(2))
        s = 2 * sum(self.size.values()) + 1 + half
        return [
            (p.a == near, remote(ref, ref, self.ssem.at[t, s], self.rsem.at[t, base + spot], p.dev(a=end)))
            for near, end, spot in ((2, 3, 2), (1, 0, 0))
        ]

    def start(self, t, mixed, phase, half=0):
        for when, copy in self.copies(t, mixed, phase, half):
            guard(when, copy.start)

    def landed(self, t, mixed, phase, half=0):
        copies = [copy for _, copy in self.copies(t, mixed, phase, half)]
        relays = self.relays(t, mixed, phase, half)
        if relays:
            copies[1].wait_recv()
            for when, copy in relays:
                guard(when, copy.start)
            copies = [copies[0]] + copies[2:]
        for copy in copies:
            copy.wait_recv()

    def first(self, t):
        def run(mixed):
            for half in (0, 1):
                self.start(t, mixed, 0, half)

        by_kind(self.kind(t), run)

    def slot(self, s, ahead):
        n = self.count

        def advance(t, phase):
            def run(mixed):
                for half in (0, 1):
                    self.landed(t, mixed, phase - 1, half)
                    if phase < 3:
                        self.start(t, mixed, phase, half)
                if phase == 3:
                    self.start(t, mixed, 3)

            guard(both(t >= 0, t < n), lambda: by_kind(self.kind(t), run))

        guard(s + ahead < n, lambda: self.first(s + ahead))
        for phase in (1, 2, 3):
            advance(s - phase + 1, phase)
        guard(both(s - 3 >= 0, s - 3 < n), lambda: self.landed(s - 3, False, 3))

    def drain(self):
        def one(t):
            def run(mixed):
                for phase in range(4):
                    for half in (0, 1) if phase < 3 else (0,):
                        for when, copy in self.copies(t, mixed, phase, half) + self.relays(t, mixed, phase, half):
                            guard(when, copy.wait_send)

            by_kind(self.kind(t), run)

        loop(self.count, one)


class Scatter:
    ORDERS = ("cba", "bca")

    def __init__(self, place, st, held, boxes, fin, out, ssem, rsem, fsem):
        self.p, self.st, self.held, self.boxes = place, st, held, boxes
        self.fin, self.out = fin, out
        self.ssem, self.rsem, self.fsem = ssem, rsem, fsem
        self.Rp, self.K = fin.shape[1], fin.shape[2]
        self.count = held.shape[0]
        self.size = {"a": place.A - 1, "b": place.B - 1, "c": place.C - 1}

    @staticmethod
    def sems(dims):
        A, B, C = dims
        return 1 + 2 * (A - 1 + B - 1 + C - 1)

    @classmethod
    def box_shapes(cls, dims, count, Rp, K):
        A, B, C = dims
        shapes = []
        for order in cls.ORDERS:
            for phase in range(3):
                left = order[phase + 1 :]
                lead = ((A,) if "a" in left else ()) + ((B,) if "b" in left else ())
                wide = C * K if "c" in left else K
                shapes.append((count, {"a": A, "b": B, "c": C}[order[phase]] - 1) + lead + (Rp // 2, wide))
        return shapes

    def box(self, r, half, phase):
        return self.boxes[3 * half + phase].at[r]

    def sibling(self, r, slot):
        p = self.p
        return remote(
            self.st[slot].at[:, :, 1 - p.k], self.held.at[r], self.ssem.at[r, 0], self.rsem.at[r, 0], p.dev(k=1 - p.k)
        )

    def sibling_part(self, r, slot, a):
        p = self.p
        return remote(
            self.st[slot].at[a, :, 1 - p.k],
            self.held.at[r, a],
            self.ssem.at[r, 0],
            self.rsem.at[r, 0],
            p.dev(k=1 - p.k),
        )

    def region(self, r, half, done, axis=None, peer=None):
        p = self.p
        every = slice(None)
        a = p.a if "a" in done else every
        b = p.b if "b" in done else every
        c = cols(p.c, self.K) if "c" in done else every
        if axis == "a":
            a = peer
        if axis == "b":
            b = peer
        if axis == "c":
            c = cols(peer, self.K)
        return r, a, b, pl.ds(half * (self.Rp // 2), self.Rp // 2), c

    def copies(self, r, half, phase):
        p = self.p
        order = self.ORDERS[half]
        done, axis = order[:phase], order[phase]
        base = 1 + half * sum(self.size.values()) + sum(self.size[x] for x in done)
        box = self.box(r, half, phase)
        return [
            remote(
                self.held.at[self.region(r, half, done, axis, peer)],
                box.at[i],
                self.ssem.at[r, base + i],
                self.rsem.at[r, base + i],
                dev,
            )
            for i, (peer, dev) in enumerate(peers_along(p, axis))
        ]

    def start(self, r, half, phase):
        for copy in self.copies(r, half, phase):
            copy.start()

    def add(self, r, half, phase):
        p = self.p
        order = self.ORDERS[half]
        for copy in self.copies(r, half, phase):
            copy.wait_recv()
        left = order[phase + 1 :]
        box = self.box(r, half, phase)
        _, a, b, rows, c = self.region(r, half, order[: phase + 1])
        count = self.size[order[phase]]

        def one(i):
            if "a" in left and "b" in left:
                lead = (i // p.B, lax.rem(i, p.B))
                spot = (r,) + lead + (rows, c)
            elif left[:1] == "a" or "a" in left:
                lead = (i,)
                spot = (r, i, b, rows, c)
            elif "b" in left:
                lead = (i,)
                spot = (r, a, i, rows, c)
            else:
                lead = ()
                spot = (r, a, b, rows, c)
            total = self.held[spot]
            for d in range(count):
                total = total + box[(d,) + lead]
            self.held[spot] = total

        trips = (p.A if "a" in left else 1) * (p.B if "b" in left else 1)
        if trips == 1:
            one(0)
        else:
            loop(trips, one)

    def flush(self, r, slot):
        p = self.p
        copy = self.sibling(r, slot)
        copy.wait_recv()

        def add(i):
            a, b = i // p.B, lax.rem(i, p.B)
            self.held[r, a, b] = self.held[r, a, b] + self.st[slot][a, b, p.k]

        loop(p.A * p.B, add)
        copy.wait_send()

    def begin(self, r):
        for half in (0, 1):
            self.start(r, half, 0)

    def step(self, r, phase):
        for half in (0, 1):
            self.add(r, half, phase)
            self.start(r, half, phase + 1)

    def mid(self, r):
        self.step(r, 0)

    def late(self, r):
        self.step(r, 1)

    def result(self, r):
        s = lax.rem(r, 2)
        return pltpu.make_async_copy(self.fin.at[s], self.out.at[r], self.fsem.at[s])

    def last(self, r):
        p = self.p
        guard(r >= 2, lambda: self.result(r - 2).wait())
        h = self.Rp // 2

        for half in (0, 1):
            for copy in self.copies(r, half, 2):
                copy.wait_recv()
            box = self.box(r, half, 2)
            total = self.held[self.region(r, half, "abc")].astype(f32)
            for d in range(self.size[self.ORDERS[half][2]]):
                total = total + box[d].astype(f32)
            self.fin[lax.rem(r, 2), half * h : (half + 1) * h] = total

        self.result(r).start()

    def tick(self, j):
        n = self.count
        guard(both(j >= 0, j < n), lambda: self.begin(j))
        guard(both(j >= 1, j - 1 < n), lambda: self.mid(j - 1))
        guard(both(j >= 2, j - 2 < n), lambda: self.late(j - 2))
        guard(both(j >= 3, j - 3 < n), lambda: self.last(j - 3))

    def drain(self):
        def one(r):
            for half in (0, 1):
                for phase in range(3):
                    for copy in self.copies(r, half, phase):
                        copy.wait_send()

        loop(self.count, one)
        for r in (self.count - 2, self.count - 1):
            self.result(r).wait()


class Spread:
    def __init__(self, place, block, full, axes, ssem, rsem, base):
        p = place
        self.p, self.block, self.full, self.axes = p, block, full, axes
        self.ssem, self.rsem, self.base = ssem, rsem, base

    def copies(self, phase):
        p = self.p
        with_c = "c" in self.axes
        tail = (p.c,) if with_c else ()
        axis = self.axes[phase]
        base = self.base
        for done in self.axes[:phase]:
            base += {"a": p.A - 1, "b": p.B - 1, "c": p.C - 1, "k": 1}[done]
        every = slice(None)
        done = self.axes[:phase]
        index = (
            every if "a" in done else p.a,
            every if "b" in done else p.b,
            every if "k" in done else p.k,
        )
        if with_c:
            index += (every if "c" in done else p.c,)
        dst = self.full.at[index]
        src = self.block if phase == 0 else dst
        made = []
        count = {"a": p.A, "b": p.B, "c": p.C, "k": 2}[axis]
        for d in range(1, count):
            dev = {
                "a": lambda: p.dev(a=p.a_peer(d)),
                "b": lambda: p.dev(b=p.b_peer(d)),
                "c": lambda: p.dev(c=p.c_peer(d)),
                "k": lambda: p.dev(k=1 - p.k),
            }[axis]()
            s = base + d - 1
            made.append(remote(src, dst, self.ssem.at[s], self.rsem.at[s], dev))
        return made

    def start(self, phase):
        for copy in self.copies(phase):
            copy.start()

    def landed(self, phase):
        for copy in self.copies(phase):
            copy.wait_recv()

    def drain(self):
        for phase in range(len(self.axes)):
            for copy in self.copies(phase):
                copy.wait_send()


LOOKAHEAD = 1
ROWS = 160
LOADED = (
    "blocks", "x", "dy", "cond", "ada", "uq", "uk_const", "ut", "selv", "table",
)
NAMES_IN = (
    "ids", "halves", "frames", "blocks_in", "x_in", "dy_in", "cond_in", "ada_in", "uq_in", "uk_const_in",
    "ut_in", "selv_in", "table_in",
)
NAMES_OUT = (
    "full", "mixed", "gx", "rout", "dmf", "tf",
)
NAMES_SCRATCH = (
    "blocks", "x", "dy", "cond", "ada", "uq", "uk_const", "ut", "selv", "table", "hid", "dff", "qkv", "heads",
    "mid", "ffn", "dh2", "wbuf", "mod", "dmod", "modx", "modf", "ms", "zacc", "tmat", "uk", "tb", "dmb", "st",
    "held", "box0", "box1", "box2", "box3", "box4", "box5",
    "fin", "in_sem", "w_sem", "own_sem", "o_sem", "g_s", "g_r", "r_s", "r_r", "f_sem", "m_s", "m_r", "s_s",
    "s_r",
)


def step_kernel(dims, wins, *refs):
    names = NAMES_IN + NAMES_OUT + NAMES_SCRATCH
    R = dict(zip(names, refs))
    p = Place(dims)
    A, B, C = dims
    T = wins * TOK
    D = 1024
    Rp = R["blocks"].shape[1]
    K = R["blocks"].shape[2]
    clips, ncol = R["cond"].shape[0], R["ada"].shape[1]
    x, dy, hid, dff, qkv, heads = (R[n] for n in ("x", "dy", "hid", "dff", "qkv", "heads"))
    mid, ffn, dh2, wbuf, mod, dmod = (R[n] for n in ("mid", "ffn", "dh2", "wbuf", "mod", "dmod"))
    full = R["full"]
    rows_per_win = TOK // ROWS

    loads = {
        name: pltpu.make_async_copy(R[name + "_in"], R[name], R["in_sem"].at[i]) for i, name in enumerate(LOADED)
    }
    for copy in loads.values():
        copy.start()
    p.barrier()
    gather = Gather(p, R["blocks"], full, R["g_s"], R["g_r"])
    scatter = Scatter(
        p, [R["st"].at[0], R["st"].at[1], wbuf.at[0]], R["held"], [R[f"box{i}"] for i in range(6)],
        R["fin"], R["rout"], R["r_s"], R["r_r"], R["f_sem"],
    )
    loads["blocks"].wait()
    gather.first(0)
    own = pltpu.make_async_copy(R["blocks"], full.at[:, p.a, p.b, p.k, :, cols(p.c, K)], R["own_sem"].at[0])
    own.start()

    def mod_c():
        return [
            remote(R["modx"].at[C - 1], R["modx"].at[d - 1], R["m_s"].at[d - 1], R["m_r"].at[d - 1], p.dev(c=p.c_peer(d)))
            for d in range(1, C)
        ]

    loads["cond"].wait()
    loads["ada"].wait()
    act_rows = jax.nn.silu(R["cond"][:, cols(p.c, R["ada"].shape[0])].astype(f32)).astype(bf16)
    R["modx"][C - 1] = nn(act_rows, R["ada"][...])
    for copy in mod_c():
        copy.start()
    spread = Spread(p, R["ms"], R["modf"], "abk", R["m_s"], R["m_r"], C - 1)

    for name in ("selv", "table", "uk_const", "uq", "ut", "x", "dy"):
        loads[name].wait()
    lanes = lax.broadcasted_iota(jnp.int32, (1, 128), 1)
    away = jnp.where(lanes == 21, -1e30, 0.0)
    for v in range(32):
        row = nt(R["table"][...], R["selv"][v]) if v < 21 else jnp.broadcast_to(away if v == 21 else away * 0.0, (HEADS, 128))
        R["zacc"][v * HEADS : (v + 1) * HEADS] = row
    for copy in mod_c():
        copy.wait_recv()
    total = R["modx"][C - 1]
    for d in range(C - 1):
        total = total + R["modx"][d]
    R["ms"][...] = total
    own_ms = pltpu.make_async_copy(R["ms"], R["modf"].at[p.a, p.b, p.k], R["own_sem"].at[1])
    own_ms.start()
    spread.start(0)
    own.wait()
    gather.slot(0, LOOKAHEAD)
    for h in range(HEADS):
        R["tmat"][h] = R["zacc"][pl.ds(h, 32, stride=HEADS), :].astype(bf16)
    own_ms.wait()
    spread.landed(0)
    spread.start(1)
    gather.slot(1, LOOKAHEAD)
    spread.landed(1)
    spread.start(2)
    frame = lax.broadcasted_iota(jnp.int32, (TOK, 128), 0) // (WIN_SIDE * WIN_SIDE)
    flag = lax.broadcasted_iota(jnp.int32, (TOK, 128), 1) == 21
    for win in range(wins):
        live = jnp.clip(R["frames"][R["ids"][win]] - WIN_FRAMES * R["halves"][win], 1, WIN_FRAMES)
        hide = jnp.logical_and(flag, frame >= live)
        R["uk"][win] = jnp.where(hide, 1.0, R["uk_const"][...].astype(f32)).astype(bf16)
    gather.slot(2, LOOKAHEAD)
    spread.landed(2)

    def weight(t, slot):
        return pltpu.make_async_copy(full.at[t], wbuf.at[slot], R["w_sem"].at[slot])

    gather.slot(3, LOOKAHEAD)
    weight(0, 0).start()
    piece = math.gcd(ncol, 128)
    clip_iota = lax.broadcasted_iota(jnp.int32, (clips, ncol), 0)
    for w in range(2 * A * B):
        blk = R["modf"][w // (2 * B), (w // 2) % B, w % 2]
        for win in range(wins):
            row = jnp.sum(jnp.where(clip_iota == R["ids"][win], blk, 0.0), 0, keepdims=True)
            for i in range(ncol // piece):
                col = w * ncol + i * piece
                mod[win * 6 + col // D, :, col % D : col % D + piece] = row[:, i * piece : (i + 1) * piece]
    gather.slot(4, LOOKAHEAD)
    weight(1, 1).start()

    def rows_loop(fn, also={}):
        def run(i):
            win = i // rows_per_win
            fn(pl.ds(pl.multiple_of(i * ROWS, ROWS), ROWS), win * 6)
            for at, extra in also.items():
                guard(i == at, extra)

        loop(T // ROWS, run)

    def make_hidden1():
        def run(rows, m):
            norm, _ = normalize(x[rows, :].astype(f32))
            hid[rows, :] = (norm * (1.0 + mod[m + 1]) + mod[m]).astype(bf16)

        rows_loop(run)

    make_hidden1()
    for i in range(wins * 6):
        dmod[i] = jnp.zeros((1, D), f32)
    R["zacc"][...] = jnp.zeros((HEADS * 32, 128), f32)

    gather.slot(5, LOOKAHEAD)
    weight(2, 2).start()
    for t in range(3):
        weight(t, t).wait()

    def qkv_rows(a, first):
        parts = []
        for b in range(B):
            for k in range(2):
                for t in range(3):
                    parts.append(wbuf[first + t, a, b, k])
        return jnp.concatenate(parts, 0)

    def qkv_cols(a):
        return pl.ds(pl.multiple_of(a * (3 * D // A), 128), 3 * D // A)

    def qkv_step(a):
        qkv[:, qkv_cols(a)] = nt(hid[...], qkv_rows(a, 0)).astype(bf16)

    loop(A, qkv_step)
    gather.slot(6, LOOKAHEAD)
    weight(3, 3).start()

    pairs = D // 128
    low_half = lax.broadcasted_iota(jnp.int32, (TOK, 128), 1) < 64

    def head_refs(i):
        win, pair = i // pairs, lax.rem(i, pairs)
        rows = pl.ds(pl.multiple_of(win * TOK, TOK), TOK)
        spots = [pl.ds(pl.multiple_of(j * D + pair * 128, 128), 128) for j in range(3)]
        return win, pair, rows, spots

    def two_heads(value):
        zero = jnp.zeros_like(value)
        return jnp.concatenate([jnp.where(low_half, value, zero), jnp.where(low_half, zero, value)], 0)

    def one_pair(value):
        return jnp.where(low_half, value[:TOK], value[TOK:])

    def attend(i):
        win, pair, rows, spots = head_refs(i)
        q = qkv[rows, spots[0]] * jnp.asarray(0.125, bf16)
        k, v = qkv[rows, spots[1]], qkv[rows, spots[2]]
        filler = jnp.zeros((96, 128), bf16)
        spread_rows = jnp.concatenate([R["tmat"][pair * 2], filler, R["tmat"][pair * 2 + 1], filler], 0)
        bias = nt(R["uq"][...], spread_rows).astype(bf16)
        bias = jnp.concatenate([bias[:, :128], bias[:, 128:]], 0)
        s = nt(jnp.concatenate([two_heads(q), bias], 1), jnp.concatenate([k, R["uk"][win]], 1))
        e = jnp.exp(s - jnp.max(s, -1, keepdims=True))
        probs = e * (1.0 / jnp.sum(e, -1, keepdims=True))
        heads[rows, spots[0]] = one_pair(nn(probs.astype(bf16), v)).astype(bf16)
        guard(i == 3, lambda: gather.slot(7, LOOKAHEAD))
        guard(i == 9, lambda: gather.slot(8, LOOKAHEAD))

    loop(wins * pairs, attend)
    weight(4, 0).start()
    weight(5, 1).start()
    weight(3, 3).wait()
    quarter = D // A

    def quarter_cols(a):
        return pl.ds(pl.multiple_of(a * quarter, 128), quarter)

    def out_step(a):
        got = nt(heads[...], wbuf[3, a].reshape(quarter, D))
        at = quarter_cols(a)
        for win in range(wins):
            rows = slice(win * TOK, (win + 1) * TOK)
            mid[rows, at] = x[rows, at].astype(f32) + mod[win * 6 + 2, :, at] * got[rows]

    gather.slot(9, LOOKAHEAD)
    loop(A, out_step)

    def second_norm(rows, m):
        norm, _ = normalize(mid[rows, :])
        hid[rows, :] = (norm * (1.0 + mod[m + 4]) + mod[m + 3]).astype(bf16)
        dff[rows, :] = (mod[m + 5] * dy[rows, :].astype(f32)).astype(bf16)
        ffn[rows, :] = jnp.zeros((ROWS, D), f32)
        dh2[rows, :] = jnp.zeros((ROWS, D), f32)

    rows_loop(second_norm)

    st = R["st"]
    F = 512

    def ffn_step(s):
        q, hf = s // 2, lax.rem(s, 2)
        su = 2 * lax.rem(q, 2)

        @pl.when(hf == 0)
        def _():
            weight(4 + 2 * q, su).wait()
            weight(5 + 2 * q, su + 1).wait()

        up = wbuf[su, pl.ds(hf * (A // 2), A // 2)].reshape(F, D)
        at = pl.ds(pl.multiple_of(hf * F, F), F)
        down = wbuf[su + 1, :, :, :, :, at].reshape(D, F)
        act, slope = gelu_parts(nt(hid[...], up))
        act = act.astype(bf16)
        ffn[...] += nt(act, down)
        d_pre = (nn(dff[...], down) * slope).astype(bf16)
        dh2[...] += nn(d_pre, up)

        @pl.when(jnp.logical_and(hf == 0, q > 0))
        def _():
            scatter.flush(2 * q - 2, 0)
            scatter.flush(2 * q - 1, 1)

        st[0, pl.ds(hf * (A // 2), A // 2)] = tn(d_pre, hid[...]).astype(bf16).reshape(A // 2, B, 2, Rp, D)
        st[1, :, :, :, :, at] = tn(dff[...], act).astype(bf16).reshape(A, B, 2, Rp, F)

        @pl.when(hf == 1)
        def _():
            scatter.sibling(2 * q, 0).start()
            scatter.sibling(2 * q + 1, 1).start()

        gather.slot(10 + s, LOOKAHEAD)
        guard(s == 4, lambda: scatter.tick(0))
        guard(s == 5, lambda: scatter.tick(1))
        guard(s == 7, lambda: scatter.tick(2))

        @pl.when(jnp.logical_and(hf == 0, q < 3))
        def _():
            weight(6 + 2 * q, 2 - su).start()
            weight(7 + 2 * q, 3 - su).start()

    loop(8, ffn_step)
    weight(3, 0).start()
    weight(0, 1).start()
    weight(1, 2).start()
    weight(2, 3).start()

    def second_back(rows, m):
        norm, inv = normalize(mid[rows, :])
        dyr = dy[rows, :].astype(f32)
        fo = ffn[rows, :]
        dh = dh2[rows, :]
        dmod[m + 5] += jnp.sum(dyr * fo, 0, keepdims=True)
        dmod[m + 3] += jnp.sum(dh, 0, keepdims=True)
        dmod[m + 4] += jnp.sum(dh * norm, 0, keepdims=True)
        dy[rows, :] = (mid[rows, :] + mod[m + 5] * fo).astype(bf16)
        ffn[rows, :] = jnp.zeros((ROWS, D), f32)
        d_mid = dyr + normalize_back(dh * (1.0 + mod[m + 4]), norm, inv)
        dh2[rows, :] = d_mid
        dff[rows, :] = (mod[m + 2] * d_mid).astype(bf16)

    rows_loop(second_back)
    mixed_out = pltpu.make_async_copy(dy, R["mixed"], R["o_sem"].at[0])
    mixed_out.start()
    scatter.flush(6, 0)
    scatter.flush(7, 1)
    scatter.tick(3)
    weight(3, 0).wait()

    def out_back(a):
        at = quarter_cols(a)
        wide = wbuf[0, a].reshape(quarter, D)
        attended = nt(heads[...], wide)
        for win in range(wins):
            rows = slice(win * TOK, (win + 1) * TOK)
            dmod[win * 6 + 2, :, at] = jnp.sum(dh2[rows, at] * attended[rows], 0, keepdims=True)
        st[0, a] = tn(dff[:, at], heads[...]).astype(bf16).reshape(B, 2, Rp, D)
        scatter.sibling_part(8, 0, a).start()
        hid[:, at] = nn(dff[...], wbuf[0, :, :, :, :, at].reshape(D, quarter)).astype(bf16)

    loop(A, out_back)
    scatter.tick(4)

    def attend_back(i):
        win, pair, rows, spots = head_refs(i)
        q = qkv[rows, spots[0]] * jnp.asarray(0.125, bf16)
        k, v = qkv[rows, spots[1]], qkv[rows, spots[2]]
        do = hid[rows, spots[0]]
        kk = two_heads(k)
        bias = nn(R["uk"][win][:, :32], jnp.concatenate([R["tmat"][pair * 2], R["tmat"][pair * 2 + 1]], 1)).astype(bf16)
        bias = jnp.concatenate([bias[:, :128], bias[:, 128:]], 0)
        query = jnp.concatenate([q, R["uq"][...]], 1)
        s = nt(jnp.concatenate([kk, bias], 1), query)
        dp = nt(two_heads(v), do)
        probs, ds = [], []
        for h in range(2):
            sh, dph = s[h * TOK : (h + 1) * TOK], dp[h * TOK : (h + 1) * TOK]
            e = jnp.exp(sh - jnp.max(sh, 0, keepdims=True))
            ph = e * (1.0 / jnp.sum(e, 0, keepdims=True))
            probs.append(ph.astype(bf16))
            ds.append((ph * (dph - jnp.sum(ph * dph, 0, keepdims=True))).astype(bf16))
        probs = jnp.concatenate(probs, 0)
        ds = jnp.concatenate(ds, 0)
        dk = nn(ds, query)
        qkv[rows, spots[0]] = (tn(ds, kk) * 0.125).astype(bf16)
        qkv[rows, spots[1]] = one_pair(dk[:, :128]).astype(bf16)
        qkv[rows, spots[2]] = one_pair(nn(probs, do)).astype(bf16)
        bias_part = jnp.concatenate([dk[:TOK, 128:], dk[TOK:, 128:]], 1)
        top = bias_part.astype(bf16)
        rest = (bias_part - top.astype(f32)).astype(bf16)
        z = nn(R["ut"][...], top) + nn(R["ut"][...], rest)
        for h in range(2):
            R["zacc"][pl.ds(pl.multiple_of((pair * 2 + h) * 32, 32), 32), :] += z[:, h * 128 : (h + 1) * 128]
        guard(i == 1, lambda: scatter.flush(8, 0))
        guard(i == 3, lambda: scatter.tick(5))
        guard(i == 7, lambda: scatter.tick(6))
        guard(i == 11, lambda: scatter.tick(7))
        guard(i == 15, lambda: scatter.tick(8))

    loop(wins * pairs, attend_back)
    make_hidden1()
    for t in range(3):
        weight(t, t + 1).wait()

    def qkv_grad(a):
        got = tn(qkv[:, qkv_cols(a)], hid[...]).astype(bf16)
        i = 0
        for b in range(B):
            for k in range(2):
                for t in range(3):
                    scatter.st[t][a, b, k] = got[i * Rp : (i + 1) * Rp]
                    i += 1
        for t in range(3):
            scatter.sibling_part(9 + t, t, a).start()

    loop(A, qkv_grad)
    scatter.flush(9, 0)
    scatter.tick(9)
    scatter.flush(10, 1)
    scatter.flush(11, 2)

    def qkv_back(a):
        ffn[...] += nn(qkv[:, qkv_cols(a)], qkv_rows(a, 1))

    loop(A, qkv_back)
    scatter.tick(10)

    def first_back(rows, m):
        norm, inv = normalize(x[rows, :].astype(f32))
        dh = ffn[rows, :]
        dmod[m] += jnp.sum(dh, 0, keepdims=True)
        dmod[m + 1] += jnp.sum(dh * norm, 0, keepdims=True)
        mid[rows, :] = dh2[rows, :] + normalize_back(dh * (1.0 + mod[m + 1]), norm, inv)

    rows_loop(first_back)
    scatter.tick(11)
    gx_out = pltpu.make_async_copy(mid, R["gx"], R["o_sem"].at[1])
    gx_out.start()
    filler = (-wins * 6) % 16
    stack = [dmod[i] for i in range(wins * 6)] + [jnp.zeros((1, D), f32)] * filler
    R["dmb"][...] = jnp.concatenate(stack, 0).astype(bf16)
    mods = Spread(p, R["dmb"], R["dmf"], "abck", R["s_s"].at[0], R["s_r"].at[0], 0)
    own_dm = pltpu.make_async_copy(R["dmb"], R["dmf"].at[p.a, p.b, p.k, p.c], R["own_sem"].at[2])
    own_dm.start()
    mods.start(0)

    lane = lax.broadcasted_iota(jnp.int32, (HEADS, 128), 1)
    table = jnp.zeros((HEADS, 128), f32)
    for win in range(wins):
        table = jnp.where(lane == 128 - wins + win, R["ids"][win].astype(f32), table)
    for v in range(21):
        zv = R["zacc"][pl.ds(v, HEADS, stride=32), :]
        top = zv.astype(bf16)
        rest = (zv - top.astype(f32)).astype(bf16)
        table = table + nn(top, R["selv"][v]) + nn(rest, R["selv"][v])
    R["tb"][...] = table
    tabs = Spread(p, R["tb"], R["tf"], "abck", R["s_s"].at[1], R["s_r"].at[1], 0)
    own_tb = pltpu.make_async_copy(R["tb"], R["tf"].at[p.a, p.b, p.k, p.c], R["own_sem"].at[3])
    own_tb.start()
    tabs.start(0)
    own_dm.wait()
    own_tb.wait()
    for phase in (1, 2, 3):
        for small in (mods, tabs):
            small.landed(phase - 1)
            small.start(phase)
        if phase == 2:
            scatter.tick(12)
    for small in (mods, tabs):
        small.landed(3)
    scatter.tick(13)
    scatter.tick(14)
    mixed_out.wait()
    gx_out.wait()
    gather.drain()
    scatter.drain()
    for copy in mod_c():
        copy.wait_send()
    for small in (spread, mods, tabs):
        small.drain()


def run_step(dims, wins, ins):
    A, B, C = dims
    n, Rp, K = ins[3].shape
    clips, ncol = ins[6].shape[0], ins[7].shape[1]
    T = wins * TOK
    D = 1024
    hbm = pl.BlockSpec(memory_space=pltpu.HBM)
    smem = pl.BlockSpec(memory_space=pltpu.SMEM)
    dm_rows = -(-wins * 6 // 16) * 16
    out_shape = [
        jax.ShapeDtypeStruct((n, A, B, 2, Rp, D), bf16),
        jax.ShapeDtypeStruct((T, D), bf16),
        jax.ShapeDtypeStruct((T, D), f32),
        jax.ShapeDtypeStruct((n, Rp, K), f32),
        jax.ShapeDtypeStruct((A, B, 2, C, dm_rows, D), bf16),
        jax.ShapeDtypeStruct((A, B, 2, C, HEADS, 128), f32),
    ]
    small = A - 1 + B - 1 + C - 1 + 1
    dma = pltpu.SemaphoreType.DMA
    scratch = [
        *[pltpu.VMEM(v.shape, v.dtype) for v in ins[3:]],
        pltpu.VMEM((T, D), bf16),
        pltpu.VMEM((T, D), bf16),
        pltpu.VMEM((T, 3 * D), bf16),
        pltpu.VMEM((T, D), bf16),
        pltpu.VMEM((T, D), f32),
        pltpu.VMEM((T, D), f32),
        pltpu.VMEM((T, D), f32),
        pltpu.VMEM((4, A, B, 2, Rp, D), bf16),
        pltpu.VMEM((wins * 6, 1, D), f32),
        pltpu.VMEM((wins * 6, 1, D), f32),
        pltpu.VMEM((C, clips, ncol), f32),
        pltpu.VMEM((A, B, 2, clips, ncol), f32),
        pltpu.VMEM((clips, ncol), f32),
        pltpu.VMEM((HEADS * 32, 128), f32),
        pltpu.VMEM((HEADS, 32, 128), bf16),
        pltpu.VMEM((wins, TOK, 128), bf16),
        pltpu.VMEM((HEADS, 128), f32),
        pltpu.VMEM((dm_rows, D), bf16),
        pltpu.VMEM((2, A, B, 2, Rp, D), bf16),
        pltpu.VMEM((n, A, B, Rp, D), bf16),
        *[pltpu.VMEM(shape, bf16) for shape in Scatter.box_shapes(dims, n, Rp, K)],
        pltpu.VMEM((2, Rp, K), f32),
        dma((len(LOADED),)),
        dma((4,)),
        dma((4,)),
        dma((2,)),
        dma((n, Gather.sems(dims))),
        dma((n, Gather.sems(dims))),
        dma((n, Scatter.sems(dims))),
        dma((n, Scatter.sems(dims))),
        dma((2,)),
        dma((C - 1 + small,)),
        dma((C - 1 + small,)),
        dma((2, small)),
        dma((2, small)),
    ]
    return pl.pallas_call(
        functools.partial(step_kernel, dims, wins),
        out_shape=out_shape,
        in_specs=[smem] * 3 + [hbm] * 10,
        out_specs=[hbm] * 6,
        scratch_shapes=scratch,
        compiler_params=pltpu.CompilerParams(
            collective_id=0, has_side_effects=True, vmem_limit_bytes=66 * 10**6 + 2**19
        ),
        name="block_step",
    )(*ins)


def body(dims, tokens, cotangent, cond, clip_frames, window_clip, window_half, ada, qkv_w, out_w, up_w, down_w, table):
    A, B, C = dims
    W = 2 * A * B
    devices = W * C
    micro, wl, toks, width = tokens.shape
    wins = micro * wl
    clips = cond.shape[0]
    n = lax.axis_index("narrow")
    w = lax.axis_index("wide")
    ids = window_clip.reshape(wins)
    half = window_half.reshape(wins)

    Rp = out_w.shape[1]
    K = out_w.shape[0]
    pieces = up_w.shape[1] // Rp
    up_t = up_w.T.reshape(pieces, Rp, K)
    down_t = down_w.reshape(-1, pieces, Rp, Rp).transpose(1, 3, 0, 2).reshape(pieces, Rp, K)
    ffn_t = jnp.stack([up_t, down_t], 1).reshape(2 * pieces, Rp, K)
    blocks = jnp.concatenate([qkv_w.T.reshape(3, Rp, K), out_w.T[None], ffn_t], 0)

    feats = position_features()
    uq_const = np.zeros((toks, 128), np.float32)
    uq_const[:, :21] = feats
    uq_const[:, 21] = 1
    uk_const = np.zeros((toks, 128), np.float32)
    uk_const[:, :21] = feats
    sel = offset_selector()
    entries = sel.shape[2]
    selv = np.zeros((21, 128, 128), np.float32)
    selv[:, :21, :entries] = sel.transpose(1, 0, 2)
    ins = (
        ids,
        half,
        clip_frames,
        blocks,
        tokens.reshape(wins * toks, width),
        cotangent.reshape(wins * toks, width),
        cond,
        ada,
        jnp.asarray(uq_const, bf16),
        jnp.asarray(uk_const, bf16),
        jnp.asarray(uk_const[:, :32].T, bf16),
        jnp.asarray(selv, bf16),
        jnp.pad(table, ((0, 0), (0, 128 - table.shape[1]))),
    )
    _, mixed, grad_x, rout, mod_grads, table_parts = run_step(dims, wins, ins)

    table_parts = table_parts.reshape(devices, HEADS, 128)
    grad_table = table_parts.sum(0)[:, : table.shape[1]]
    all_ids = table_parts[:, 0, 128 - wins :].reshape(devices, micro, wl).transpose(1, 0, 2).reshape(-1)
    ncol = ada.shape[1]
    dm = mod_grads.reshape(devices, -1, width)[:, : wins * 6].reshape(devices, micro, wl, 6 * width)
    dm = lax.dynamic_slice_in_dim(dm, w * ncol, ncol, 3)
    dm = dm.transpose(1, 0, 2, 3).reshape(-1, ncol)
    picked = (all_ids[:, None] == jnp.arange(clips, dtype=f32)[None, :]).astype(f32)
    cond_act = jax.nn.silu(cond.astype(f32)).astype(bf16)
    act_rows = lax.dynamic_slice_in_dim(cond_act, n * ada.shape[0], ada.shape[0], 1)
    by_clip = jnp.einsum("wc,we->ce", picked, dm.astype(f32), precision=highest)
    grad_ada = jnp.einsum("cr,ce->re", act_rows.astype(f32), by_clip, precision=highest)

    ffn_r = rout[: 2 * pieces].reshape(pieces, 2, Rp, K)
    g_up = ffn_r[:, 0].reshape(pieces * Rp, K).T
    g_down = ffn_r[:, 1].reshape(pieces, Rp, -1, Rp).transpose(2, 0, 3, 1).reshape(-1, Rp)
    g_out = rout[2 * pieces].T
    g_qkv = rout[2 * pieces + 1 :].reshape(3 * Rp, K).T
    return (
        mixed.reshape(tokens.shape),
        grad_x.reshape(tokens.shape),
        grad_ada,
        g_qkv,
        g_out,
        g_up,
        g_down,
        grad_table,
    )


def solution(mesh):
    W, C = mesh.shape["wide"], mesh.shape["narrow"]
    A = min(4, W // 2)
    dims = (A, W // 2 // A, C)
    sh = ("wide", "narrow")
    weight = P("narrow", "wide")
    return jax.shard_map(
        functools.partial(body, dims),
        mesh=mesh,
        in_specs=(P(None, sh), P(None, sh), P(), P(), P(None, sh), P(None, sh)) + (weight,) * 5 + (P(),),
        out_specs=(P(None, sh), P(None, sh)) + (weight,) * 5 + (P(),),
        check_vma=False,
    )
```

```python
import functools
import math

import jax
import jax.numpy as jnp
import numpy as np
from jax import lax
from jax.experimental import pallas as pl
from jax.experimental.pallas import tpu as pltpu
from jax.sharding import PartitionSpec as P

HEADS = 16
WIN_FRAMES = 5
WIN_SIDE = 8
TOK = WIN_FRAMES * WIN_SIDE * WIN_SIDE
F_SPAN = 2 * WIN_FRAMES - 1
S_SPAN = 2 * WIN_SIDE - 1
epsilon = 1e-06
inv_root_two = 0.7071067811865476
inv_root_tau = 0.3989422804014327
highest = lax.Precision.HIGHEST
MESH = pl.DeviceIdType.MESH
bf16 = jnp.bfloat16
f32 = jnp.float32


def position_features():
    p = np.arange(TOK)
    feats = np.zeros((TOK, WIN_FRAMES + 2 * WIN_SIDE), np.float32)
    feats[p, p // 64] = 1
    feats[p, WIN_FRAMES + (p // 8) % 8] = 1
    feats[p, WIN_FRAMES + WIN_SIDE + p % 8] = 1
    return feats


def offset_selector():
    sel = np.zeros((21, 21, F_SPAN + 2 * S_SPAN), np.float32)
    for i in range(WIN_FRAMES):
        for j in range(WIN_FRAMES):
            sel[i, j, i - j + WIN_FRAMES - 1] = 1
    for i in range(WIN_SIDE):
        for j in range(WIN_SIDE):
            sel[5 + i, 5 + j, F_SPAN + i - j + WIN_SIDE - 1] = 1
            sel[13 + i, 13 + j, F_SPAN + S_SPAN + i - j + WIN_SIDE - 1] = 1
    return sel


def nt(lhs, rhs):
    return lax.dot_general(lhs, rhs, (((1,), (1,)), ((), ())), preferred_element_type=f32)


def nn(lhs, rhs):
    return lax.dot_general(lhs, rhs, (((1,), (0,)), ((), ())), preferred_element_type=f32)


def tn(lhs, rhs):
    return lax.dot_general(lhs, rhs, (((0,), (0,)), ((), ())), preferred_element_type=f32)


def normalize(values):
    centre = jnp.mean(values, -1, keepdims=True)
    shifted = values - centre
    inv_std = lax.rsqrt(jnp.mean(shifted * shifted, -1, keepdims=True) + epsilon)
    return shifted * inv_std, inv_std


def normalize_back(grad_norm, normed, inv_std):
    return inv_std * (
        grad_norm
        - jnp.mean(grad_norm, -1, keepdims=True)
        - normed * jnp.mean(grad_norm * normed, -1, keepdims=True)
    )


def gelu_parts(pre):
    gate = 0.5 * (1.0 + lax.erf(pre * inv_root_two))
    return pre * gate, gate + pre * inv_root_tau * jnp.exp(-0.5 * pre * pre)


def guard(cond, fn):
    if isinstance(cond, bool):
        if cond:
            fn()
    else:
        pl.when(cond)(fn)


def both(*conds):
    total = True
    for cond in conds:
        if isinstance(cond, bool):
            if not cond:
                return False
        elif total is True:
            total = cond
        else:
            total = jnp.logical_and(total, cond)
    return total


def loop(count, fn):
    def step(i, carry):
        fn(i)
        return carry

    lax.fori_loop(0, count, step, 0)


def cols(c, K):
    return pl.ds(pl.multiple_of(c * K, K), K)


class Place:
    def __init__(self, dims):
        self.A, self.B, self.C = dims
        w = lax.axis_index("wide")
        self.c = lax.axis_index("narrow")
        self.k = lax.rem(w, 2)
        self.b = lax.rem(w // 2, self.B)
        self.a = w // (2 * self.B)

    def dev(self, a=None, b=None, k=None, c=None):
        a = self.a if a is None else a
        b = self.b if b is None else b
        k = self.k if k is None else k
        c = self.c if c is None else c
        return ((a * self.B + b) * 2 + k, c)

    def a_peer(self, d):
        return lax.rem(self.a + d, self.A)

    def b_peer(self, d):
        return lax.rem(self.b + d, self.B)

    def c_peer(self, d):
        return lax.rem(self.c + d, self.C)

    def barrier(self):
        peers = [self.dev(a=self.a_peer(d)) for d in range(1, self.A)]
        peers += [self.dev(b=self.b_peer(d)) for d in range(1, self.B)]
        peers += [self.dev(c=self.c_peer(d)) for d in range(1, self.C)]
        peers += [self.dev(k=1 - self.k)]
        sem = pltpu.get_barrier_semaphore()
        for peer in peers:
            pl.semaphore_signal(sem, inc=1, device_id=peer, device_id_type=MESH)
        pl.semaphore_wait(sem, len(peers))


def remote(src, dst, ssem, rsem, dev):
    return pltpu.make_async_remote_copy(
        src_ref=src, dst_ref=dst, send_sem=ssem, recv_sem=rsem, device_id=dev, device_id_type=MESH
    )


def peers_along(p, axis):
    if axis == "a":
        return [(p.a_peer(d), p.dev(a=p.a_peer(d))) for d in range(1, p.A)]
    if axis == "b":
        return [(p.b_peer(d), p.dev(b=p.b_peer(d))) for d in range(1, p.B)]
    return [(p.c_peer(d), p.dev(c=p.c_peer(d))) for d in range(1, p.C)]


def every_nth(t, n, spot):
    return t % n == spot if isinstance(t, int) else lax.rem(t, n) == spot


def by_kind(kind, fn):
    if isinstance(kind, bool):
        fn(kind)
    else:
        pl.when(kind)(lambda: fn(True))
        pl.when(jnp.logical_not(kind))(lambda: fn(False))


class Gather:
    ORDERS = {False: ("abc", "acb"), True: ("bac", "cab")}

    def __init__(self, place, blocks, full, ssem, rsem):
        self.p, self.blocks, self.full, self.ssem, self.rsem = place, blocks, full, ssem, rsem
        self.Rp, self.K = blocks.shape[1], blocks.shape[2]
        self.count = blocks.shape[0]
        self.size = {"a": place.A - 1, "b": place.B - 1, "c": place.C - 1}

    @staticmethod
    def kind(t):
        return every_nth(t, 2, 1)

    @staticmethod
    def sems(dims):
        A, B, C = dims
        return 2 * (A - 1 + B - 1 + C - 1) + 1 + 2

    def region(self, t, order, phase, half, a):
        p = self.p
        done = order[:phase]
        every = slice(None)
        return self.full.at[
            t,
            every if "a" in done else a,
            every if "b" in done else p.b,
            p.k,
            pl.ds(half * (self.Rp // 2), self.Rp // 2),
            every if "c" in done else cols(p.c, self.K),
        ]

    def copies(self, t, mixed, phase, half=0):
        p = self.p
        if phase == 3:
            s = 2 * sum(self.size.values())
            ref = self.full.at[t, :, :, p.k]
            return [(True, remote(ref, ref, self.ssem.at[t, s], self.rsem.at[t, s], p.dev(k=1 - p.k)))]
        order = self.ORDERS[mixed][half]
        done, axis = order[:phase], order[phase]
        ref = self.region(t, order, phase, half, p.a)
        src = self.blocks.at[t, pl.ds(half * (self.Rp // 2), self.Rp // 2), :] if phase == 0 else ref
        base = half * sum(self.size.values()) + sum(self.size[x] for x in done)
        made = []
        for i, (_, dev) in enumerate(peers_along(p, axis)):
            when = True
            if axis == "a" and i == 0:
                when = p.a != p.A - 1
            if axis == "a" and i == p.A - 2:
                when = p.a != 0
            made.append((when, remote(src, ref, self.ssem.at[t, base + i], self.rsem.at[t, base + i], dev)))
        return made

    def relays(self, t, mixed, phase, half):
        p = self.p
        order = self.ORDERS[mixed][half]
        if phase == 3 or order[phase] != "a":
            return []
        base = half * sum(self.size.values()) + sum(self.size[x] for x in order[:phase])
        ref = self.region(t, order, phase, half, p.a_peer(2))
        s = 2 * sum(self.size.values()) + 1 + half
        return [
            (p.a == near, remote(ref, ref, self.ssem.at[t, s], self.rsem.at[t, base + spot], p.dev(a=end)))
            for near, end, spot in ((2, 3, 2), (1, 0, 0))
        ]

    def start(self, t, mixed, phase, half=0):
        for when, copy in self.copies(t, mixed, phase, half):
            guard(when, copy.start)

    def landed(self, t, mixed, phase, half=0):
        copies = [copy for _, copy in self.copies(t, mixed, phase, half)]
        relays = self.relays(t, mixed, phase, half)
        if relays:
            copies[1].wait_recv()
            for when, copy in relays:
                guard(when, copy.start)
            copies = [copies[0]] + copies[2:]
        for copy in copies:
            copy.wait_recv()

    def first(self, t):
        def run(mixed):
            for half in (0, 1):
                self.start(t, mixed, 0, half)

        by_kind(self.kind(t), run)

    def slot(self, s, ahead):
        n = self.count

        def advance(t, phase):
            def run(mixed):
                for half in (0, 1):
                    self.landed(t, mixed, phase - 1, half)
                    if phase < 3:
                        self.start(t, mixed, phase, half)
                if phase == 3:
                    self.start(t, mixed, 3)

            guard(both(t >= 0, t < n), lambda: by_kind(self.kind(t), run))

        guard(s + ahead < n, lambda: self.first(s + ahead))
        for phase in (1, 2, 3):
            advance(s - phase + 1, phase)
        guard(both(s - 3 >= 0, s - 3 < n), lambda: self.landed(s - 3, False, 3))

    def drain(self):
        def one(t):
            def run(mixed):
                for phase in range(4):
                    for half in (0, 1) if phase < 3 else (0,):
                        for when, copy in self.copies(t, mixed, phase, half) + self.relays(t, mixed, phase, half):
                            guard(when, copy.wait_send)

            by_kind(self.kind(t), run)

        loop(self.count, one)


class Scatter:
    ORDERS = ("cba", "bca")

    def __init__(self, place, st, held, boxes, fin, out, ssem, rsem, fsem):
        self.p, self.st, self.held, self.boxes = place, st, held, boxes
        self.fin, self.out = fin, out
        self.ssem, self.rsem, self.fsem = ssem, rsem, fsem
        self.Rp, self.K = fin.shape[1], fin.shape[2]
        self.count = held.shape[0]
        self.size = {"a": place.A - 1, "b": place.B - 1, "c": place.C - 1}

    @staticmethod
    def sems(dims):
        A, B, C = dims
        return 1 + 2 * (A - 1 + B - 1 + C - 1)

    @classmethod
    def box_shapes(cls, dims, count, Rp, K):
        A, B, C = dims
        shapes = []
        for order in cls.ORDERS:
            for phase in range(3):
                left = order[phase + 1 :]
                lead = ((A,) if "a" in left else ()) + ((B,) if "b" in left else ())
                wide = C * K if "c" in left else K
                shapes.append((count, {"a": A, "b": B, "c": C}[order[phase]] - 1) + lead + (Rp // 2, wide))
        return shapes

    def box(self, r, half, phase):
        return self.boxes[3 * half + phase].at[r]

    def sibling(self, r, slot):
        p = self.p
        return remote(
            self.st[slot].at[:, :, 1 - p.k], self.held.at[r], self.ssem.at[r, 0], self.rsem.at[r, 0], p.dev(k=1 - p.k)
        )

    def sibling_part(self, r, slot, a):
        p = self.p
        return remote(
            self.st[slot].at[a, :, 1 - p.k],
            self.held.at[r, a],
            self.ssem.at[r, 0],
            self.rsem.at[r, 0],
            p.dev(k=1 - p.k),
        )

    def region(self, r, half, done, axis=None, peer=None):
        p = self.p
        every = slice(None)
        a = p.a if "a" in done else every
        b = p.b if "b" in done else every
        c = cols(p.c, self.K) if "c" in done else every
        if axis == "a":
            a = peer
        if axis == "b":
            b = peer
        if axis == "c":
            c = cols(peer, self.K)
        return r, a, b, pl.ds(half * (self.Rp // 2), self.Rp // 2), c

    def copies(self, r, half, phase):
        p = self.p
        order = self.ORDERS[half]
        done, axis = order[:phase], order[phase]
        base = 1 + half * sum(self.size.values()) + sum(self.size[x] for x in done)
        box = self.box(r, half, phase)
        return [
            remote(
                self.held.at[self.region(r, half, done, axis, peer)],
                box.at[i],
                self.ssem.at[r, base + i],
                self.rsem.at[r, base + i],
                dev,
            )
            for i, (peer, dev) in enumerate(peers_along(p, axis))
        ]

    def start(self, r, half, phase):
        for copy in self.copies(r, half, phase):
            copy.start()

    def add(self, r, half, phase):
        p = self.p
        order = self.ORDERS[half]
        for copy in self.copies(r, half, phase):
            copy.wait_recv()
        left = order[phase + 1 :]
        box = self.box(r, half, phase)
        _, a, b, rows, c = self.region(r, half, order[: phase + 1])
        count = self.size[order[phase]]

        def one(i):
            if "a" in left and "b" in left:
                lead = (i // p.B, lax.rem(i, p.B))
                spot = (r,) + lead + (rows, c)
            elif left[:1] == "a" or "a" in left:
                lead = (i,)
                spot = (r, i, b, rows, c)
            elif "b" in left:
                lead = (i,)
                spot = (r, a, i, rows, c)
            else:
                lead = ()
                spot = (r, a, b, rows, c)
            total = self.held[spot]
            for d in range(count):
                total = total + box[(d,) + lead]
            self.held[spot] = total

        trips = (p.A if "a" in left else 1) * (p.B if "b" in left else 1)
        if trips == 1:
            one(0)
        else:
            loop(trips, one)

    def flush(self, r, slot):
        p = self.p
        copy = self.sibling(r, slot)
        copy.wait_recv()

        def add(i):
            a, b = i // p.B, lax.rem(i, p.B)
            self.held[r, a, b] = self.held[r, a, b] + self.st[slot][a, b, p.k]

        loop(p.A * p.B, add)
        copy.wait_send()

    def begin(self, r):
        for half in (0, 1):
            self.start(r, half, 0)

    def step(self, r, phase):
        for half in (0, 1):
            self.add(r, half, phase)
            self.start(r, half, phase + 1)

    def mid(self, r):
        self.step(r, 0)

    def late(self, r):
        self.step(r, 1)

    def result(self, r):
        s = lax.rem(r, 2)
        return pltpu.make_async_copy(self.fin.at[s], self.out.at[r], self.fsem.at[s])

    def last(self, r):
        p = self.p
        guard(r >= 2, lambda: self.result(r - 2).wait())
        h = self.Rp // 2

        for half in (0, 1):
            for copy in self.copies(r, half, 2):
                copy.wait_recv()
            box = self.box(r, half, 2)
            total = self.held[self.region(r, half, "abc")].astype(f32)
            for d in range(self.size[self.ORDERS[half][2]]):
                total = total + box[d].astype(f32)
            self.fin[lax.rem(r, 2), half * h : (half + 1) * h] = total

        self.result(r).start()

    def step_of(self, kind, r):
        if kind == 4:
            self.flush(r, r % 2 if r < 8 else max(0, r - 9))
        else:
            (self.begin, self.mid, self.late, self.last)[kind](r)

    def steps(self, *names):
        for what in names:
            self.step_of(*what)

    def at(self, index, table):
        for spot, names in table.items():
            guard(index == spot, functools.partial(self.steps, *names))

    def drain(self, first, count):
        def one(i):
            r = first + i
            for half in (0, 1):
                for phase in range(3):
                    for copy in self.copies(r, half, phase):
                        copy.wait_send()

        loop(count, one)


class Spread:
    def __init__(self, place, block, full, axes, ssem, rsem, base):
        p = place
        self.p, self.block, self.full, self.axes = p, block, full, axes
        self.ssem, self.rsem, self.base = ssem, rsem, base

    def copies(self, phase):
        p = self.p
        with_c = "c" in self.axes
        tail = (p.c,) if with_c else ()
        axis = self.axes[phase]
        base = self.base
        for done in self.axes[:phase]:
            base += {"a": p.A - 1, "b": p.B - 1, "c": p.C - 1, "k": 1}[done]
        every = slice(None)
        done = self.axes[:phase]
        index = (
            every if "a" in done else p.a,
            every if "b" in done else p.b,
            every if "k" in done else p.k,
        )
        if with_c:
            index += (every if "c" in done else p.c,)
        dst = self.full.at[index]
        src = self.block if phase == 0 else dst
        made = []
        count = {"a": p.A, "b": p.B, "c": p.C, "k": 2}[axis]
        for d in range(1, count):
            dev = {
                "a": lambda: p.dev(a=p.a_peer(d)),
                "b": lambda: p.dev(b=p.b_peer(d)),
                "c": lambda: p.dev(c=p.c_peer(d)),
                "k": lambda: p.dev(k=1 - p.k),
            }[axis]()
            s = base + d - 1
            made.append(remote(src, dst, self.ssem.at[s], self.rsem.at[s], dev))
        return made

    def start(self, phase):
        for copy in self.copies(phase):
            copy.start()

    def landed(self, phase):
        for copy in self.copies(phase):
            copy.wait_recv()

    def drain(self):
        for phase in range(len(self.axes)):
            for copy in self.copies(phase):
                copy.wait_send()


class Fold:
    ORDER = "kbac"

    def __init__(self, place, parts, boxes, total, ssem, rsem):
        self.p, self.parts, self.boxes, self.total, self.ssem, self.rsem = place, parts, boxes, total, ssem, rsem

    def peers(self, axis):
        p = self.p
        return [(1 - p.k, p.dev(k=1 - p.k))] if axis == "k" else peers_along(p, axis)

    def region(self, phase, peer=None):
        p = self.p
        every = slice(None)
        done = self.ORDER[: phase + 1]
        mine = {"a": p.a, "b": p.b, "k": p.k}
        if peer is not None and self.ORDER[phase] != "c":
            mine[self.ORDER[phase]] = peer
        return tuple(mine[x] if x in done else every for x in "abk")

    def copies(self, phase):
        base = sum(len(self.peers(x)) for x in self.ORDER[:phase])
        return [
            remote(
                self.parts.at[self.region(phase, peer)],
                self.boxes[phase].at[i],
                self.ssem.at[base + i],
                self.rsem.at[base + i],
                dev,
            )
            for i, (peer, dev) in enumerate(self.peers(self.ORDER[phase]))
        ]

    def start(self, phase):
        for copy in self.copies(phase):
            copy.start()

    def add(self, phase):
        copies = self.copies(phase)
        for copy in copies:
            copy.wait_recv()
        spot = self.region(phase)
        got = self.parts[spot]
        for i in range(len(copies)):
            got = got + self.boxes[phase][i]
        if self.ORDER[phase] == "c":
            self.total[...] = got
        else:
            self.parts[spot] = got

    def drain(self):
        for phase in range(4):
            for copy in self.copies(phase):
                copy.wait_send()


LOOKAHEAD = 1
ROWS = {True: 160, False: 64}
def begin(r):
    return 0, r


def middle(r):
    return 1, r


def late(r):
    return 2, r


def end(r):
    return 3, r


def part(r):
    return 4, r


FFN_EARLY = {4: (begin(1),), 5: (begin(2), late(0)), 6: (begin(3), late(1)), 7: (begin(4), late(2))}
FFN_LATE = {3: (begin(0),), 4: (middle(0),), 5: (middle(1),), 6: (middle(2), end(0)), 7: (middle(3), end(1))}
SECOND_BACK = {0: (begin(5),), 1: (late(3),), 2: (middle(4),), 3: (end(2),)}
OUT_BACK = {0: (begin(6),), 1: (late(4),), 2: (middle(5),), 3: (end(3),)}
ATTEND_BACK = {
    0: (part(8),), 1: (begin(7),), 3: (late(5),), 4: (middle(6),), 5: (end(4),), 7: (begin(8),), 9: (late(6),), 10: (middle(7),), 11: (end(5),), 13: (late(7),), 15: (middle(8),),
}
HIDDEN = {2: (end(6),)}
QKV_GRAD = {1: (late(8),), 3: (end(7),)}
QKV_BACK = {2: (begin(10),), 3: (end(8),)}
AFTER_QKV = (middle(9),)
FIRST_BACK = {0: (begin(11),), 1: (late(9),)}
AFTER_FIRST = (middle(10),)
HOPS = ((late(10), middle(11)), (end(9), late(11)), (end(10), end(11)))
ENDING = ()


def step_kernel(dims, wins, *refs):
    (
        r_ids, r_halves, r_frames, r_blocks_in, r_x_in, r_dy_in, r_cond_in, r_ada_in, r_uq_in, r_uk_const_in, r_ut_in,
        r_selv_in, r_table_in, r_full, r_mixed, r_gx, r_rout, r_by_clip, r_tf, r_blocks, r_x, r_dy, r_cond, r_ada, r_uq,
        r_uk_const, r_ut, r_selv, r_table, r_hid, r_dff, r_qkv, r_heads, r_mid, r_ffn, r_dh2, r_wbuf, r_mod, r_dmod,
        r_modx, r_modf, r_ms, r_zacc, r_tmat, r_uk, r_tb, r_fold0, r_fold1, r_fold2, r_fold3, r_cl, r_st, r_held,
        r_box0, r_box1, r_box2, r_box3, r_box4, r_box5, r_fin, r_in_sem, r_w_sem, r_own_sem, r_o_sem, r_g_s, r_g_r,
        r_r_s, r_r_r, r_f_sem, r_m_s, r_m_r, r_s_s, r_s_r,
    ) = refs
    p = Place(dims)
    A, B, C = dims
    T = wins * TOK
    D = 1024
    Rp = r_blocks.shape[1]
    K = r_blocks.shape[2]
    clips, ncol = r_cond.shape[0], r_ada.shape[1]
    x, dy, hid, dff, qkv, heads = r_x, r_dy, r_hid, r_dff, r_qkv, r_heads
    mid, ffn, dh2, wbuf, mod, dmod = r_mid, r_ffn, r_dh2, r_wbuf, r_mod, r_dmod
    full = r_full
    at_once = ROWS[C <= 2]
    rows_per_win = TOK // at_once

    loads = [
        pltpu.make_async_copy(src, dst, r_in_sem.at[i])
        for i, (src, dst) in enumerate(
            (
                (r_blocks_in, r_blocks),
                (r_x_in, r_x),
                (r_dy_in, r_dy),
                (r_cond_in, r_cond),
                (r_ada_in, r_ada),
                (r_uq_in, r_uq),
                (r_uk_const_in, r_uk_const),
                (r_ut_in, r_ut),
                (r_selv_in, r_selv),
                (r_table_in, r_table),
            )
        )
    ]
    for copy in loads:
        copy.start()
    p.barrier()
    gather = Gather(p, r_blocks, full, r_g_s, r_g_r)
    scatter = Scatter(
        p, [r_st.at[0], r_st.at[1], wbuf.at[0]], r_held, [r_box0, r_box1, r_box2, r_box3, r_box4, r_box5],
        r_fin, r_rout, r_r_s, r_r_r, r_f_sem,
    )
    loads[0].wait()
    gather.first(0)
    own = pltpu.make_async_copy(r_blocks, full.at[:, p.a, p.b, p.k, :, cols(p.c, K)], r_own_sem.at[0])
    own.start()

    def mod_c():
        return [
            remote(r_modx.at[C - 1], r_modx.at[d - 1], r_m_s.at[d - 1], r_m_r.at[d - 1], p.dev(c=p.c_peer(d)))
            for d in range(1, C)
        ]

    loads[3].wait()
    loads[4].wait()
    act_rows = jax.nn.silu(r_cond[:, cols(p.c, r_ada.shape[0])].astype(f32)).astype(bf16)
    r_modx[C - 1] = nn(act_rows, r_ada[...])
    for copy in mod_c():
        copy.start()
    spread = Spread(p, r_ms, r_modf, "abk", r_m_s, r_m_r, C - 1)

    for i in (8, 9, 6, 5, 7, 1, 2):
        loads[i].wait()
    lanes = lax.broadcasted_iota(jnp.int32, (1, 128), 1)
    away = jnp.where(lanes == 21, -1e30, 0.0)
    for v in range(32):
        row = nt(r_table[...], r_selv[v]) if v < 21 else jnp.broadcast_to(away if v == 21 else away * 0.0, (HEADS, 128))
        r_zacc[v * HEADS : (v + 1) * HEADS] = row
    for copy in mod_c():
        copy.wait_recv()
    total = r_modx[C - 1]
    for d in range(C - 1):
        total = total + r_modx[d]
    r_ms[...] = total
    own_ms = pltpu.make_async_copy(r_ms, r_modf.at[p.a, p.b, p.k], r_own_sem.at[1])
    own_ms.start()
    spread.start(0)
    own.wait()
    gather.slot(0, LOOKAHEAD)
    for h in range(HEADS):
        r_tmat[h] = r_zacc[pl.ds(h, 32, stride=HEADS), :].astype(bf16)
    own_ms.wait()
    spread.landed(0)
    spread.start(1)
    gather.slot(1, LOOKAHEAD)
    spread.landed(1)
    spread.start(2)
    frame = lax.broadcasted_iota(jnp.int32, (TOK, 128), 0) // (WIN_SIDE * WIN_SIDE)
    flag = lax.broadcasted_iota(jnp.int32, (TOK, 128), 1) == 21
    for win in range(wins):
        live = jnp.clip(r_frames[r_ids[win]] - WIN_FRAMES * r_halves[win], 1, WIN_FRAMES)
        hide = jnp.logical_and(flag, frame >= live)
        r_uk[win] = jnp.where(hide, 1.0, r_uk_const[...].astype(f32)).astype(bf16)
    gather.slot(2, LOOKAHEAD)
    spread.landed(2)

    def weight(t, slot):
        return pltpu.make_async_copy(full.at[t], wbuf.at[slot], r_w_sem.at[slot])

    gather.slot(3, LOOKAHEAD)
    weight(0, 0).start()
    piece = math.gcd(ncol, 128)
    clip_iota = lax.broadcasted_iota(jnp.int32, (clips, ncol), 0)
    for w in range(2 * A * B):
        blk = r_modf[w // (2 * B), (w // 2) % B, w % 2]
        for win in range(wins):
            row = jnp.sum(jnp.where(clip_iota == r_ids[win], blk, 0.0), 0, keepdims=True)
            for i in range(ncol // piece):
                col = w * ncol + i * piece
                mod[win * 6 + col // D, :, col % D : col % D + piece] = row[:, i * piece : (i + 1) * piece]
    gather.slot(4, LOOKAHEAD)
    weight(1, 1).start()

    def rows_loop(fn, also={}):
        def run(i):
            win = i // rows_per_win
            fn(pl.ds(pl.multiple_of(i * at_once, at_once), at_once), win * 6)
            scatter.at(i, also)

        loop(T // at_once, run)

    def make_hidden1(also={}):
        def run(rows, m):
            norm, _ = normalize(x[rows, :].astype(f32))
            hid[rows, :] = (norm * (1.0 + mod[m + 1]) + mod[m]).astype(bf16)

        rows_loop(run, also)

    make_hidden1()
    for i in range(wins * 6):
        dmod[i] = jnp.zeros((1, D), f32)
    r_zacc[...] = jnp.zeros((HEADS * 32, 128), f32)

    gather.slot(5, LOOKAHEAD)
    weight(2, 2).start()
    for t in range(3):
        weight(t, t).wait()

    def qkv_rows(a, first):
        parts = []
        for b in range(B):
            for k in range(2):
                for t in range(3):
                    parts.append(wbuf[first + t, a, b, k])
        return jnp.concatenate(parts, 0)

    def qkv_cols(a):
        return pl.ds(pl.multiple_of(a * (3 * D // A), 128), 3 * D // A)

    def qkv_step(a):
        qkv[:, qkv_cols(a)] = nt(hid[...], qkv_rows(a, 0)).astype(bf16)

    loop(A, qkv_step)
    gather.slot(6, LOOKAHEAD)
    weight(3, 3).start()

    pairs = D // 128
    low_half = lax.broadcasted_iota(jnp.int32, (TOK, 128), 1) < 64

    def head_refs(i):
        win, pair = i // pairs, lax.rem(i, pairs)
        rows = pl.ds(pl.multiple_of(win * TOK, TOK), TOK)
        spots = [pl.ds(pl.multiple_of(j * D + pair * 128, 128), 128) for j in range(3)]
        return win, pair, rows, spots

    def two_heads(value):
        zero = jnp.zeros_like(value)
        return jnp.concatenate([jnp.where(low_half, value, zero), jnp.where(low_half, zero, value)], 0)

    def one_pair(value):
        return jnp.where(low_half, value[:TOK], value[TOK:])

    def attend(i):
        win, pair, rows, spots = head_refs(i)
        q = qkv[rows, spots[0]] * jnp.asarray(0.125, bf16)
        k, v = qkv[rows, spots[1]], qkv[rows, spots[2]]
        filler = jnp.zeros((96, 128), bf16)
        spread_rows = jnp.concatenate([r_tmat[pair * 2], filler, r_tmat[pair * 2 + 1], filler], 0)
        bias = nt(r_uq[...], spread_rows).astype(bf16)
        bias = jnp.concatenate([bias[:, :128], bias[:, 128:]], 0)
        s = nt(jnp.concatenate([two_heads(q), bias], 1), jnp.concatenate([k, r_uk[win]], 1))
        e = jnp.exp(s - jnp.max(s, -1, keepdims=True))
        probs = e * (1.0 / jnp.sum(e, -1, keepdims=True))
        heads[rows, spots[0]] = one_pair(nn(probs.astype(bf16), v)).astype(bf16)
        guard(i == 3, lambda: gather.slot(7, LOOKAHEAD))
        guard(i == 9, lambda: gather.slot(8, LOOKAHEAD))

    loop(wins * pairs, attend)
    weight(4, 0).start()
    weight(5, 1).start()
    weight(3, 3).wait()
    quarter = D // A

    def quarter_cols(a):
        return pl.ds(pl.multiple_of(a * quarter, 128), quarter)

    def out_step(a):
        got = nt(heads[...], wbuf[3, a].reshape(quarter, D))
        at = quarter_cols(a)
        for win in range(wins):
            rows = slice(win * TOK, (win + 1) * TOK)
            mid[rows, at] = x[rows, at].astype(f32) + mod[win * 6 + 2, :, at] * got[rows]

    gather.slot(9, LOOKAHEAD)
    loop(A, out_step)

    def second_norm(rows, m):
        norm, _ = normalize(mid[rows, :])
        hid[rows, :] = (norm * (1.0 + mod[m + 4]) + mod[m + 3]).astype(bf16)
        dff[rows, :] = (mod[m + 5] * dy[rows, :].astype(f32)).astype(bf16)
        ffn[rows, :] = jnp.zeros((at_once, D), f32)
        dh2[rows, :] = jnp.zeros((at_once, D), f32)

    rows_loop(second_norm)

    st = r_st
    subs = 1 if C <= 2 else 2
    per, F = A // 2 // subs, D // 2 // subs

    def ffn_step(s):
        q, hf = s // 2, lax.rem(s, 2)
        su = 2 * lax.rem(q, 2)

        @pl.when(hf == 0)
        def _():
            weight(4 + 2 * q, su).wait()
            weight(5 + 2 * q, su + 1).wait()

        def between():
            @pl.when(jnp.logical_and(hf == 0, q > 0))
            def _():
                scatter.flush(2 * q - 2, 0)
                scatter.flush(2 * q - 1, 1)

            guard(s == 4, lambda: gather.slot(13, LOOKAHEAD))

            @pl.when(s == 5)
            def _():
                gather.slot(14, LOOKAHEAD)
                weight(10, 2).start()
                weight(11, 3).start()

            scatter.at(s, FFN_EARLY)

        for sub in range(subs):
            first = hf * (A // 2) + sub * per
            up = wbuf[su, pl.ds(first, per)].reshape(F, D)
            at = pl.ds(pl.multiple_of((hf * subs + sub) * F, F), F)
            down = wbuf[su + 1, :, :, :, :, at].reshape(D, F)
            act, slope = gelu_parts(nt(hid[...], up))
            act = act.astype(bf16)
            ffn[...] += nt(act, down)
            d_pre = (nn(dff[...], down) * slope).astype(bf16)
            dh2[...] += nn(d_pre, up)
            if sub == 0:
                between()
            st[0, pl.ds(first, per)] = tn(d_pre, hid[...]).astype(bf16).reshape(per, B, 2, Rp, D)
            st[1, :, :, :, :, at] = tn(dff[...], act).astype(bf16).reshape(A, B, 2, Rp, F)

        @pl.when(hf == 1)
        def _():
            scatter.sibling(2 * q, 0).start()
            scatter.sibling(2 * q + 1, 1).start()

        guard(s < 3, lambda: gather.slot(10 + s, LOOKAHEAD))
        scatter.at(s, FFN_LATE)

        @pl.when(jnp.logical_and(hf == 0, q < 2))
        def _():
            weight(6 + 2 * q, 2 - su).start()
            weight(7 + 2 * q, 3 - su).start()

    loop(8, ffn_step)
    weight(3, 0).start()
    weight(0, 1).start()
    weight(1, 2).start()
    weight(2, 3).start()

    def second_back(rows, m):
        norm, inv = normalize(mid[rows, :])
        dyr = dy[rows, :].astype(f32)
        fo = ffn[rows, :]
        dh = dh2[rows, :]
        dmod[m + 5] += jnp.sum(dyr * fo, 0, keepdims=True)
        dmod[m + 3] += jnp.sum(dh, 0, keepdims=True)
        dmod[m + 4] += jnp.sum(dh * norm, 0, keepdims=True)
        dy[rows, :] = (mid[rows, :] + mod[m + 5] * fo).astype(bf16)
        ffn[rows, :] = jnp.zeros((at_once, D), f32)
        d_mid = dyr + normalize_back(dh * (1.0 + mod[m + 4]), norm, inv)
        dh2[rows, :] = d_mid
        dff[rows, :] = (mod[m + 2] * d_mid).astype(bf16)

    rows_loop(second_back, SECOND_BACK)
    mixed_out = pltpu.make_async_copy(dy, r_mixed, r_o_sem.at[0])
    mixed_out.start()
    scatter.flush(6, 0)
    scatter.flush(7, 1)
    weight(3, 0).wait()

    def out_back(a):
        at = quarter_cols(a)
        wide = wbuf[0, a].reshape(quarter, D)
        attended = nt(heads[...], wide)
        for win in range(wins):
            rows = slice(win * TOK, (win + 1) * TOK)
            dmod[win * 6 + 2, :, at] = jnp.sum(dh2[rows, at] * attended[rows], 0, keepdims=True)
        st[0, a] = tn(dff[:, at], heads[...]).astype(bf16).reshape(B, 2, Rp, D)
        scatter.sibling_part(8, 0, a).start()
        hid[:, at] = nn(dff[...], wbuf[0, :, :, :, :, at].reshape(D, quarter)).astype(bf16)
        scatter.at(a, OUT_BACK)

    loop(A, out_back)
    def attend_back(i):
        win, pair, rows, spots = head_refs(i)
        q = qkv[rows, spots[0]] * jnp.asarray(0.125, bf16)
        k, v = qkv[rows, spots[1]], qkv[rows, spots[2]]
        do = hid[rows, spots[0]]
        kk = two_heads(k)
        bias = nn(r_uk[win][:, :32], jnp.concatenate([r_tmat[pair * 2], r_tmat[pair * 2 + 1]], 1)).astype(bf16)
        bias = jnp.concatenate([bias[:, :128], bias[:, 128:]], 0)
        query = jnp.concatenate([q, r_uq[...]], 1)
        s = nt(jnp.concatenate([kk, bias], 1), query)
        dp = nt(two_heads(v), do)
        probs, ds = [], []
        for h in range(2):
            sh, dph = s[h * TOK : (h + 1) * TOK], dp[h * TOK : (h + 1) * TOK]
            e = jnp.exp(sh - jnp.max(sh, 0, keepdims=True))
            ph = e * (1.0 / jnp.sum(e, 0, keepdims=True))
            probs.append(ph.astype(bf16))
            ds.append((ph * (dph - jnp.sum(ph * dph, 0, keepdims=True))).astype(bf16))
        probs = jnp.concatenate(probs, 0)
        ds = jnp.concatenate(ds, 0)
        dk = nn(ds, query)
        qkv[rows, spots[0]] = (tn(ds, kk) * 0.125).astype(bf16)
        qkv[rows, spots[1]] = one_pair(dk[:, :128]).astype(bf16)
        qkv[rows, spots[2]] = one_pair(nn(probs, do)).astype(bf16)
        bias_part = jnp.concatenate([dk[:TOK, 128:], dk[TOK:, 128:]], 1)
        top = bias_part.astype(bf16)
        rest = (bias_part - top.astype(f32)).astype(bf16)
        z = nn(r_ut[...], top) + nn(r_ut[...], rest)
        for h in range(2):
            r_zacc[pl.ds(pl.multiple_of((pair * 2 + h) * 32, 32), 32), :] += z[:, h * 128 : (h + 1) * 128]
        scatter.at(i, ATTEND_BACK)

    loop(wins * pairs, attend_back)
    table = jnp.zeros((HEADS, 128), f32)
    for v in range(21):
        zv = r_zacc[pl.ds(v, HEADS, stride=32), :]
        top = zv.astype(bf16)
        rest = (zv - top.astype(f32)).astype(bf16)
        table = table + nn(top, r_selv[v]) + nn(rest, r_selv[v])
    r_tb[...] = table
    tabs = Spread(p, r_tb, r_tf, "abck", r_s_s.at[1], r_s_r.at[1], 0)
    own_tb = pltpu.make_async_copy(r_tb, r_tf.at[p.a, p.b, p.k, p.c], r_own_sem.at[3])
    own_tb.start()
    tabs.start(0)
    spread.drain()
    own_tb.wait()
    gather.drain()
    make_hidden1(HIDDEN)
    tabs.landed(0)
    tabs.start(1)
    for t in range(3):
        weight(t, t + 1).wait()

    def qkv_grad(a):
        got = tn(qkv[:, qkv_cols(a)], hid[...]).astype(bf16)
        i = 0
        for b in range(B):
            for k in range(2):
                for t in range(3):
                    scatter.st[t][a, b, k] = got[i * Rp : (i + 1) * Rp]
                    i += 1
        for t in range(3):
            scatter.sibling_part(9 + t, t, a).start()
        scatter.at(a, QKV_GRAD)

    loop(A, qkv_grad)
    scatter.steps(part(9), begin(9), part(10), part(11))
    tabs.landed(1)
    tabs.start(2)

    def qkv_back(a):
        ffn[...] += nn(qkv[:, qkv_cols(a)], qkv_rows(a, 1))
        scatter.at(a, QKV_BACK)

    loop(A, qkv_back)
    tabs.landed(2)
    tabs.start(3)
    scatter.steps(*AFTER_QKV)

    def first_back(rows, m):
        norm, inv = normalize(x[rows, :].astype(f32))
        dh = ffn[rows, :]
        dmod[m] += jnp.sum(dh, 0, keepdims=True)
        dmod[m + 1] += jnp.sum(dh * norm, 0, keepdims=True)
        mid[rows, :] = dh2[rows, :] + normalize_back(dh * (1.0 + mod[m + 1]), norm, inv)

    rows_loop(first_back, FIRST_BACK)
    gx_out = pltpu.make_async_copy(mid, r_gx, r_o_sem.at[1])
    gx_out.start()
    own_clip = [
        (lax.broadcasted_iota(jnp.int32, (clips, piece), 0) == r_ids[win]).astype(f32) for win in range(wins)
    ]
    for w in range(2 * A * B):
        for i in range(ncol // piece):
            col = w * ncol + i * piece
            got = 0.0
            for win in range(wins):
                row = dmod[win * 6 + col // D, :, col % D : col % D + piece].astype(bf16).astype(f32)
                got = got + own_clip[win] * row
            r_modf[w // (2 * B), (w // 2) % B, w % 2, :, i * piece : (i + 1) * piece] = got
    fold = Fold(p, r_modf, [r_fold0, r_fold1, r_fold2, r_fold3], r_cl, r_s_s.at[0], r_s_r.at[0])
    fold.start(0)
    scatter.steps(*AFTER_FIRST)
    scatter.drain(0, 9)
    for phase in (1, 2, 3):
        fold.add(phase - 1)
        fold.start(phase)
        scatter.steps(*HOPS[phase - 1])
    fold.add(3)
    clip_out = pltpu.make_async_copy(r_cl, r_by_clip, r_own_sem.at[2])
    clip_out.start()
    tabs.landed(3)
    scatter.steps(*ENDING)
    clip_out.wait()
    mixed_out.wait()
    gx_out.wait()
    for r in (scatter.count - 2, scatter.count - 1):
        scatter.result(r).wait()
    scatter.drain(9, 3)
    for copy in mod_c():
        copy.wait_send()
    for small in (fold, tabs):
        small.drain()


def run_step(dims, wins, ins):
    A, B, C = dims
    n, Rp, K = ins[3].shape
    clips, ncol = ins[6].shape[0], ins[7].shape[1]
    T = wins * TOK
    D = 1024
    hbm = pl.BlockSpec(memory_space=pltpu.HBM)
    smem = pl.BlockSpec(memory_space=pltpu.SMEM)
    out_shape = [
        jax.ShapeDtypeStruct((n, A, B, 2, Rp, D), bf16),
        jax.ShapeDtypeStruct((T, D), bf16),
        jax.ShapeDtypeStruct((T, D), f32),
        jax.ShapeDtypeStruct((n, Rp, K), f32),
        jax.ShapeDtypeStruct((clips, ncol), f32),
        jax.ShapeDtypeStruct((A, B, 2, C, HEADS, 128), f32),
    ]
    small = A - 1 + B - 1 + C - 1 + 1
    dma = pltpu.SemaphoreType.DMA
    scratch = [
        *[pltpu.VMEM(v.shape, v.dtype) for v in ins[3:]],
        pltpu.VMEM((T, D), bf16),
        pltpu.VMEM((T, D), bf16),
        pltpu.VMEM((T, 3 * D), bf16),
        pltpu.VMEM((T, D), bf16),
        pltpu.VMEM((T, D), f32),
        pltpu.VMEM((T, D), f32),
        pltpu.VMEM((T, D), f32),
        pltpu.VMEM((4, A, B, 2, Rp, D), bf16),
        pltpu.VMEM((wins * 6, 1, D), f32),
        pltpu.VMEM((wins * 6, 1, D), f32),
        pltpu.VMEM((C, clips, ncol), f32),
        pltpu.VMEM((A, B, 2, clips, ncol), f32),
        pltpu.VMEM((clips, ncol), f32),
        pltpu.VMEM((HEADS * 32, 128), f32),
        pltpu.VMEM((HEADS, 32, 128), bf16),
        pltpu.VMEM((wins, TOK, 128), bf16),
        pltpu.VMEM((HEADS, 128), f32),
        pltpu.VMEM((1, A, B, clips, ncol), f32),
        pltpu.VMEM((B - 1, A, clips, ncol), f32),
        pltpu.VMEM((A - 1, clips, ncol), f32),
        pltpu.VMEM((C - 1, clips, ncol), f32),
        pltpu.VMEM((clips, ncol), f32),
        pltpu.VMEM((2, A, B, 2, Rp, D), bf16),
        pltpu.VMEM((n, A, B, Rp, D), bf16),
        *[pltpu.VMEM(shape, bf16) for shape in Scatter.box_shapes(dims, n, Rp, K)],
        pltpu.VMEM((2, Rp, K), f32),
        dma((10,)),
        dma((4,)),
        dma((4,)),
        dma((2,)),
        dma((n, Gather.sems(dims))),
        dma((n, Gather.sems(dims))),
        dma((n, Scatter.sems(dims))),
        dma((n, Scatter.sems(dims))),
        dma((2,)),
        dma((C - 1 + small,)),
        dma((C - 1 + small,)),
        dma((2, small)),
        dma((2, small)),
    ]
    return pl.pallas_call(
        functools.partial(step_kernel, dims, wins),
        out_shape=out_shape,
        in_specs=[smem] * 3 + [hbm] * 10,
        out_specs=[hbm] * 6,
        scratch_shapes=scratch,
        compiler_params=pltpu.CompilerParams(
            collective_id=0, has_side_effects=True, vmem_limit_bytes=66 * 10**6 + 2**19
        ),
        name="block_step",
    )(*ins)


def body(dims, tokens, cotangent, cond, clip_frames, window_clip, window_half, ada, qkv_w, out_w, up_w, down_w, table):
    A, B, C = dims
    W = 2 * A * B
    devices = W * C
    micro, wl, toks, width = tokens.shape
    wins = micro * wl
    clips = cond.shape[0]
    n = lax.axis_index("narrow")
    ids = window_clip.reshape(wins)
    half = window_half.reshape(wins)

    Rp = out_w.shape[1]
    K = out_w.shape[0]
    pieces = up_w.shape[1] // Rp
    up_t = up_w.T.reshape(pieces, Rp, K)
    down_t = down_w.reshape(-1, pieces, Rp, Rp).transpose(1, 3, 0, 2).reshape(pieces, Rp, K)
    ffn_t = jnp.stack([up_t, down_t], 1).reshape(2 * pieces, Rp, K)
    blocks = jnp.concatenate([qkv_w.T.reshape(3, Rp, K), out_w.T[None], ffn_t], 0)

    feats = position_features()
    uq_const = np.zeros((toks, 128), np.float32)
    uq_const[:, :21] = feats
    uq_const[:, 21] = 1
    uk_const = np.zeros((toks, 128), np.float32)
    uk_const[:, :21] = feats
    sel = offset_selector()
    entries = sel.shape[2]
    selv = np.zeros((21, 128, 128), np.float32)
    selv[:, :21, :entries] = sel.transpose(1, 0, 2)
    ins = (
        ids,
        half,
        clip_frames,
        blocks,
        tokens.reshape(wins * toks, width),
        cotangent.reshape(wins * toks, width),
        cond,
        ada,
        jnp.asarray(uq_const, bf16),
        jnp.asarray(uk_const, bf16),
        jnp.asarray(uk_const[:, :32].T, bf16),
        jnp.asarray(selv, bf16),
        jnp.pad(table, ((0, 0), (0, 128 - table.shape[1]))),
    )
    _, mixed, grad_x, rout, by_clip, table_parts = run_step(dims, wins, ins)

    table_parts = table_parts.reshape(devices, HEADS, 128)
    grad_table = table_parts.sum(0)[:, : table.shape[1]]
    cond_act = jax.nn.silu(cond.astype(f32)).astype(bf16)
    act_rows = lax.dynamic_slice_in_dim(cond_act, n * ada.shape[0], ada.shape[0], 1)
    grad_ada = jnp.einsum("cr,ce->re", act_rows.astype(f32), by_clip, precision=highest)

    ffn_r = rout[: 2 * pieces].reshape(pieces, 2, Rp, K)
    g_up = ffn_r[:, 0].reshape(pieces * Rp, K).T
    g_down = ffn_r[:, 1].reshape(pieces, Rp, -1, Rp).transpose(2, 0, 3, 1).reshape(-1, Rp)
    g_out = rout[2 * pieces].T
    g_qkv = rout[2 * pieces + 1 :].reshape(3 * Rp, K).T
    return (
        mixed.reshape(tokens.shape),
        grad_x.reshape(tokens.shape),
        grad_ada,
        g_qkv,
        g_out,
        g_up,
        g_down,
        grad_table,
    )


def solution(mesh):
    W, C = mesh.shape["wide"], mesh.shape["narrow"]
    A = min(4, W // 2)
    dims = (A, W // 2 // A, C)
    sh = ("wide", "narrow")
    weight = P("narrow", "wide")
    return jax.shard_map(
        functools.partial(body, dims),
        mesh=mesh,
        in_specs=(P(None, sh), P(None, sh), P(), P(), P(None, sh), P(None, sh)) + (weight,) * 5 + (P(),),
        out_specs=(P(None, sh), P(None, sh)) + (weight,) * 5 + (P(),),
        check_vma=False,
    )
```

```python
import functools
import math

import jax
import jax.numpy as jnp
import numpy as np
from jax import lax
from jax.experimental import pallas as pl
from jax.experimental.pallas import tpu as pltpu
from jax.sharding import PartitionSpec as P

HEADS = 16
WIN_FRAMES = 5
WIN_SIDE = 8
TOK = WIN_FRAMES * WIN_SIDE * WIN_SIDE
F_SPAN = 2 * WIN_FRAMES - 1
S_SPAN = 2 * WIN_SIDE - 1
epsilon = 1e-06
inv_root_two = 0.7071067811865476
inv_root_tau = 0.3989422804014327
highest = lax.Precision.HIGHEST
MESH = pl.DeviceIdType.MESH
bf16 = jnp.bfloat16
f32 = jnp.float32


def position_features():
    p = np.arange(TOK)
    feats = np.zeros((TOK, WIN_FRAMES + 2 * WIN_SIDE), np.float32)
    feats[p, p // 64] = 1
    feats[p, WIN_FRAMES + (p // 8) % 8] = 1
    feats[p, WIN_FRAMES + WIN_SIDE + p % 8] = 1
    return feats


def offset_selector():
    sel = np.zeros((21, 21, F_SPAN + 2 * S_SPAN), np.float32)
    for i in range(WIN_FRAMES):
        for j in range(WIN_FRAMES):
            sel[i, j, i - j + WIN_FRAMES - 1] = 1
    for i in range(WIN_SIDE):
        for j in range(WIN_SIDE):
            sel[5 + i, 5 + j, F_SPAN + i - j + WIN_SIDE - 1] = 1
            sel[13 + i, 13 + j, F_SPAN + S_SPAN + i - j + WIN_SIDE - 1] = 1
    return sel


def nt(lhs, rhs):
    return lax.dot_general(lhs, rhs, (((1,), (1,)), ((), ())), preferred_element_type=f32)


def nn(lhs, rhs):
    return lax.dot_general(lhs, rhs, (((1,), (0,)), ((), ())), preferred_element_type=f32)


def tn(lhs, rhs):
    return lax.dot_general(lhs, rhs, (((0,), (0,)), ((), ())), preferred_element_type=f32)


def normalize(values):
    centre = jnp.mean(values, -1, keepdims=True)
    shifted = values - centre
    inv_std = lax.rsqrt(jnp.mean(shifted * shifted, -1, keepdims=True) + epsilon)
    return shifted * inv_std, inv_std


def normalize_back(grad_norm, normed, inv_std):
    return inv_std * (
        grad_norm
        - jnp.mean(grad_norm, -1, keepdims=True)
        - normed * jnp.mean(grad_norm * normed, -1, keepdims=True)
    )


def gelu_parts(pre):
    gate = 0.5 * (1.0 + lax.erf(pre * inv_root_two))
    return pre * gate, gate + pre * inv_root_tau * jnp.exp(-0.5 * pre * pre)


def guard(cond, fn):
    if isinstance(cond, bool):
        if cond:
            fn()
    else:
        pl.when(cond)(fn)


def both(*conds):
    total = True
    for cond in conds:
        if isinstance(cond, bool):
            if not cond:
                return False
        elif total is True:
            total = cond
        else:
            total = jnp.logical_and(total, cond)
    return total


def loop(count, fn):
    def step(i, carry):
        fn(i)
        return carry

    lax.fori_loop(0, count, step, 0)


def cols(c, K):
    return pl.ds(pl.multiple_of(c * K, K), K)


class Place:
    def __init__(self, dims):
        self.A, self.B, self.C = dims
        w = lax.axis_index("wide")
        self.c = lax.axis_index("narrow")
        self.k = lax.rem(w, 2)
        self.b = lax.rem(w // 2, self.B)
        self.a = w // (2 * self.B)

    def dev(self, a=None, b=None, k=None, c=None):
        a = self.a if a is None else a
        b = self.b if b is None else b
        k = self.k if k is None else k
        c = self.c if c is None else c
        return ((a * self.B + b) * 2 + k, c)

    def a_peer(self, d):
        return lax.rem(self.a + d, self.A)

    def b_peer(self, d):
        return lax.rem(self.b + d, self.B)

    def c_peer(self, d):
        return lax.rem(self.c + d, self.C)

    def barrier(self):
        peers = [self.dev(a=self.a_peer(d)) for d in range(1, self.A)]
        peers += [self.dev(b=self.b_peer(d)) for d in range(1, self.B)]
        peers += [self.dev(c=self.c_peer(d)) for d in range(1, self.C)]
        peers += [self.dev(k=1 - self.k)]
        sem = pltpu.get_barrier_semaphore()
        for peer in peers:
            pl.semaphore_signal(sem, inc=1, device_id=peer, device_id_type=MESH)
        pl.semaphore_wait(sem, len(peers))


def remote(src, dst, ssem, rsem, dev):
    return pltpu.make_async_remote_copy(
        src_ref=src, dst_ref=dst, send_sem=ssem, recv_sem=rsem, device_id=dev, device_id_type=MESH
    )


def peers_along(p, axis):
    if axis == "a":
        return [(p.a_peer(d), p.dev(a=p.a_peer(d))) for d in range(1, p.A)]
    if axis == "b":
        return [(p.b_peer(d), p.dev(b=p.b_peer(d))) for d in range(1, p.B)]
    return [(p.c_peer(d), p.dev(c=p.c_peer(d))) for d in range(1, p.C)]


def every_nth(t, n, spot):
    return t % n == spot if isinstance(t, int) else lax.rem(t, n) == spot


def by_kind(kind, fn):
    if isinstance(kind, bool):
        fn(kind)
    else:
        pl.when(kind)(lambda: fn(True))
        pl.when(jnp.logical_not(kind))(lambda: fn(False))


class Gather:
    ORDERS = {False: ("abc", "acb"), True: ("bac", "cab")}

    def __init__(self, place, blocks, full, ssem, rsem):
        self.p, self.blocks, self.full, self.ssem, self.rsem = place, blocks, full, ssem, rsem
        self.Rp, self.K = blocks.shape[1], blocks.shape[2]
        self.count = blocks.shape[0]
        self.size = {"a": place.A - 1, "b": place.B - 1, "c": place.C - 1}

    @staticmethod
    def kind(t):
        return every_nth(t, 2, 1)

    @staticmethod
    def sems(dims):
        A, B, C = dims
        return 2 * (A - 1 + B - 1 + C - 1) + 1 + 2

    def region(self, t, order, phase, half, a):
        p = self.p
        done = order[:phase]
        every = slice(None)
        return self.full.at[
            t,
            every if "a" in done else a,
            every if "b" in done else p.b,
            p.k,
            pl.ds(half * (self.Rp // 2), self.Rp // 2),
            every if "c" in done else cols(p.c, self.K),
        ]

    def copies(self, t, mixed, phase, half=0):
        p = self.p
        if phase == 3:
            s = 2 * sum(self.size.values())
            ref = self.full.at[t, :, :, p.k]
            return [(True, remote(ref, ref, self.ssem.at[t, s], self.rsem.at[t, s], p.dev(k=1 - p.k)))]
        order = self.ORDERS[mixed][half]
        done, axis = order[:phase], order[phase]
        ref = self.region(t, order, phase, half, p.a)
        src = self.blocks.at[t, pl.ds(half * (self.Rp // 2), self.Rp // 2), :] if phase == 0 else ref
        base = half * sum(self.size.values()) + sum(self.size[x] for x in done)
        made = []
        for i, (_, dev) in enumerate(peers_along(p, axis)):
            when = True
            if axis == "a" and i == 0:
                when = p.a != p.A - 1
            if axis == "a" and i == p.A - 2:
                when = p.a != 0
            made.append((when, remote(src, ref, self.ssem.at[t, base + i], self.rsem.at[t, base + i], dev)))
        return made

    def relays(self, t, mixed, phase, half):
        p = self.p
        order = self.ORDERS[mixed][half]
        if phase == 3 or order[phase] != "a":
            return []
        base = half * sum(self.size.values()) + sum(self.size[x] for x in order[:phase])
        ref = self.region(t, order, phase, half, p.a_peer(2))
        s = 2 * sum(self.size.values()) + 1 + half
        return [
            (p.a == near, remote(ref, ref, self.ssem.at[t, s], self.rsem.at[t, base + spot], p.dev(a=end)))
            for near, end, spot in ((2, 3, 2), (1, 0, 0))
        ]

    def start(self, t, mixed, phase, half=0):
        for when, copy in self.copies(t, mixed, phase, half):
            guard(when, copy.start)

    def landed(self, t, mixed, phase, half=0):
        copies = [copy for _, copy in self.copies(t, mixed, phase, half)]
        relays = self.relays(t, mixed, phase, half)
        if relays:
            copies[1].wait_recv()
            for when, copy in relays:
                guard(when, copy.start)
            copies = [copies[0]] + copies[2:]
        for copy in copies:
            copy.wait_recv()

    def first(self, t):
        def run(mixed):
            for half in (0, 1):
                self.start(t, mixed, 0, half)

        by_kind(self.kind(t), run)

    def slot(self, s, ahead):
        n = self.count

        def advance(t, phase):
            def run(mixed):
                for half in (0, 1):
                    self.landed(t, mixed, phase - 1, half)
                    if phase < 3:
                        self.start(t, mixed, phase, half)
                if phase == 3:
                    self.start(t, mixed, 3)

            guard(both(t >= 0, t < n), lambda: by_kind(self.kind(t), run))

        guard(s + ahead < n, lambda: self.first(s + ahead))
        for phase in (1, 2, 3):
            advance(s - phase + 1, phase)
        guard(both(s - 3 >= 0, s - 3 < n), lambda: self.landed(s - 3, False, 3))

    def drain(self):
        def one(t):
            def run(mixed):
                for phase in range(4):
                    for half in (0, 1) if phase < 3 else (0,):
                        for when, copy in self.copies(t, mixed, phase, half) + self.relays(t, mixed, phase, half):
                            guard(when, copy.wait_send)

            by_kind(self.kind(t), run)

        loop(self.count, one)


class Scatter:
    ORDERS = ("cba", "bca")

    def __init__(self, place, st, held, boxes, fin, out, ssem, rsem, fsem):
        self.p, self.st, self.held, self.boxes = place, st, held, boxes
        self.fin, self.out = fin, out
        self.ssem, self.rsem, self.fsem = ssem, rsem, fsem
        self.Rp, self.K = fin.shape[1], fin.shape[2]
        self.count = held.shape[0]
        self.size = {"a": place.A - 1, "b": place.B - 1, "c": place.C - 1}

    @staticmethod
    def sems(dims):
        A, B, C = dims
        return 1 + 2 * (A - 1 + B - 1 + C - 1)

    @classmethod
    def box_shapes(cls, dims, count, Rp, K):
        A, B, C = dims
        shapes = []
        for order in cls.ORDERS:
            for phase in range(3):
                left = order[phase + 1 :]
                lead = ((A,) if "a" in left else ()) + ((B,) if "b" in left else ())
                wide = C * K if "c" in left else K
                shapes.append((count, {"a": A, "b": B, "c": C}[order[phase]] - 1) + lead + (Rp // 2, wide))
        return shapes

    def box(self, r, half, phase):
        return self.boxes[3 * half + phase].at[r]

    def sibling(self, r, slot):
        p = self.p
        return remote(
            self.st[slot].at[:, :, 1 - p.k], self.held.at[r], self.ssem.at[r, 0], self.rsem.at[r, 0], p.dev(k=1 - p.k)
        )

    def sibling_part(self, r, slot, a):
        p = self.p
        return remote(
            self.st[slot].at[a, :, 1 - p.k],
            self.held.at[r, a],
            self.ssem.at[r, 0],
            self.rsem.at[r, 0],
            p.dev(k=1 - p.k),
        )

    def region(self, r, half, done, axis=None, peer=None):
        p = self.p
        every = slice(None)
        a = p.a if "a" in done else every
        b = p.b if "b" in done else every
        c = cols(p.c, self.K) if "c" in done else every
        if axis == "a":
            a = peer
        if axis == "b":
            b = peer
        if axis == "c":
            c = cols(peer, self.K)
        return r, a, b, pl.ds(half * (self.Rp // 2), self.Rp // 2), c

    def copies(self, r, half, phase):
        p = self.p
        order = self.ORDERS[half]
        done, axis = order[:phase], order[phase]
        base = 1 + half * sum(self.size.values()) + sum(self.size[x] for x in done)
        box = self.box(r, half, phase)
        return [
            remote(
                self.held.at[self.region(r, half, done, axis, peer)],
                box.at[i],
                self.ssem.at[r, base + i],
                self.rsem.at[r, base + i],
                dev,
            )
            for i, (peer, dev) in enumerate(peers_along(p, axis))
        ]

    def start(self, r, half, phase):
        for copy in self.copies(r, half, phase):
            copy.start()

    def add(self, r, half, phase):
        p = self.p
        order = self.ORDERS[half]
        for copy in self.copies(r, half, phase):
            copy.wait_recv()
        left = order[phase + 1 :]
        box = self.box(r, half, phase)
        _, a, b, rows, c = self.region(r, half, order[: phase + 1])
        count = self.size[order[phase]]

        def one(i):
            if "a" in left and "b" in left:
                lead = (i // p.B, lax.rem(i, p.B))
                spot = (r,) + lead + (rows, c)
            elif left[:1] == "a" or "a" in left:
                lead = (i,)
                spot = (r, i, b, rows, c)
            elif "b" in left:
                lead = (i,)
                spot = (r, a, i, rows, c)
            else:
                lead = ()
                spot = (r, a, b, rows, c)
            total = self.held[spot]
            for d in range(count):
                total = total + box[(d,) + lead]
            self.held[spot] = total

        trips = (p.A if "a" in left else 1) * (p.B if "b" in left else 1)
        if trips == 1:
            one(0)
        else:
            loop(trips, one)

    def flush(self, r, slot):
        p = self.p
        copy = self.sibling(r, slot)
        copy.wait_recv()

        def add(i):
            a, b = i // p.B, lax.rem(i, p.B)
            self.held[r, a, b] = self.held[r, a, b] + self.st[slot][a, b, p.k]

        loop(p.A * p.B, add)
        copy.wait_send()

    def begin(self, r):
        for half in (0, 1):
            self.start(r, half, 0)

    def step(self, r, phase):
        for half in (0, 1):
            self.add(r, half, phase)
            self.start(r, half, phase + 1)

    def mid(self, r):
        self.step(r, 0)

    def late(self, r):
        self.step(r, 1)

    def result(self, r):
        s = lax.rem(r, 2)
        return pltpu.make_async_copy(self.fin.at[s], self.out.at[r], self.fsem.at[s])

    def last(self, r):
        p = self.p
        guard(r >= 2, lambda: self.result(r - 2).wait())
        h = self.Rp // 2

        for half in (0, 1):
            for copy in self.copies(r, half, 2):
                copy.wait_recv()
            box = self.box(r, half, 2)
            total = self.held[self.region(r, half, "abc")].astype(f32)
            for d in range(self.size[self.ORDERS[half][2]]):
                total = total + box[d].astype(f32)
            self.fin[lax.rem(r, 2), half * h : (half + 1) * h] = total

        self.result(r).start()

    def step_of(self, kind, r):
        if kind == 4:
            self.flush(r, r % 2 if r < 8 else max(0, r - 9))
        else:
            (self.begin, self.mid, self.late, self.last)[kind](r)

    def steps(self, *names):
        for what in names:
            self.step_of(*what)

    def at(self, index, table):
        for spot, names in table.items():
            guard(index == spot, functools.partial(self.steps, *names))

    def drain(self, first, count):
        def one(i):
            r = first + i
            for half in (0, 1):
                for phase in range(3):
                    for copy in self.copies(r, half, phase):
                        copy.wait_send()

        loop(count, one)


class Spread:
    def __init__(self, place, block, full, axes, ssem, rsem, base):
        p = place
        self.p, self.block, self.full, self.axes = p, block, full, axes
        self.ssem, self.rsem, self.base = ssem, rsem, base

    def copies(self, phase):
        p = self.p
        with_c = "c" in self.axes
        tail = (p.c,) if with_c else ()
        axis = self.axes[phase]
        base = self.base
        for done in self.axes[:phase]:
            base += {"a": p.A - 1, "b": p.B - 1, "c": p.C - 1, "k": 1}[done]
        every = slice(None)
        done = self.axes[:phase]
        index = (
            every if "a" in done else p.a,
            every if "b" in done else p.b,
            every if "k" in done else p.k,
        )
        if with_c:
            index += (every if "c" in done else p.c,)
        dst = self.full.at[index]
        src = self.block if phase == 0 else dst
        made = []
        count = {"a": p.A, "b": p.B, "c": p.C, "k": 2}[axis]
        for d in range(1, count):
            dev = {
                "a": lambda: p.dev(a=p.a_peer(d)),
                "b": lambda: p.dev(b=p.b_peer(d)),
                "c": lambda: p.dev(c=p.c_peer(d)),
                "k": lambda: p.dev(k=1 - p.k),
            }[axis]()
            s = base + d - 1
            made.append(remote(src, dst, self.ssem.at[s], self.rsem.at[s], dev))
        return made

    def start(self, phase):
        for copy in self.copies(phase):
            copy.start()

    def landed(self, phase):
        for copy in self.copies(phase):
            copy.wait_recv()

    def drain(self):
        for phase in range(len(self.axes)):
            for copy in self.copies(phase):
                copy.wait_send()


class Fold:
    ORDER = "kbac"

    def __init__(self, place, parts, boxes, total, ssem, rsem):
        self.p, self.parts, self.boxes, self.total, self.ssem, self.rsem = place, parts, boxes, total, ssem, rsem

    def peers(self, axis):
        p = self.p
        return [(1 - p.k, p.dev(k=1 - p.k))] if axis == "k" else peers_along(p, axis)

    def region(self, phase, peer=None):
        p = self.p
        every = slice(None)
        done = self.ORDER[: phase + 1]
        mine = {"a": p.a, "b": p.b, "k": p.k}
        if peer is not None and self.ORDER[phase] != "c":
            mine[self.ORDER[phase]] = peer
        return tuple(mine[x] if x in done else every for x in "abk")

    def copies(self, phase):
        base = sum(len(self.peers(x)) for x in self.ORDER[:phase])
        return [
            remote(
                self.parts.at[self.region(phase, peer)],
                self.boxes[phase].at[i],
                self.ssem.at[base + i],
                self.rsem.at[base + i],
                dev,
            )
            for i, (peer, dev) in enumerate(self.peers(self.ORDER[phase]))
        ]

    def start(self, phase):
        for copy in self.copies(phase):
            copy.start()

    def add(self, phase):
        copies = self.copies(phase)
        for copy in copies:
            copy.wait_recv()
        spot = self.region(phase)
        got = self.parts[spot]
        for i in range(len(copies)):
            got = got + self.boxes[phase][i]
        if self.ORDER[phase] == "c":
            self.total[...] = got
        else:
            self.parts[spot] = got

    def drain(self):
        for phase in range(4):
            for copy in self.copies(phase):
                copy.wait_send()


LOOKAHEAD = 1
ROWS = {True: 160, False: 64}
def begin(r):
    return 0, r


def middle(r):
    return 1, r


def late(r):
    return 2, r


def end(r):
    return 3, r


def part(r):
    return 4, r


FFN_EARLY = {4: (begin(1),), 5: (begin(2), late(0)), 6: (begin(3), late(1)), 7: (begin(4), late(2))}
FFN_LATE = {3: (begin(0),), 4: (middle(0),), 5: (middle(1),), 6: (middle(2), end(0)), 7: (middle(3), end(1))}
SECOND_BACK = {0: (begin(5),), 1: (late(3),), 2: (middle(4),), 3: (end(2),)}
OUT_BACK = {0: (begin(6),), 1: (late(4),), 2: (middle(5),), 3: (end(3),)}
ATTEND_BACK = {
    0: (part(8),), 1: (begin(7),), 3: (late(5),), 4: (middle(6),), 5: (end(4),), 7: (begin(8),), 9: (late(6),), 10: (middle(7),), 11: (end(5),), 13: (late(7),), 15: (middle(8),),
}
HIDDEN = {2: (end(6),)}
QKV_GRAD = {1: (late(8),), 3: (end(7),)}
QKV_BACK = {2: (begin(10),), 3: (end(8),)}
AFTER_QKV = (middle(9),)
FIRST_BACK = {0: (begin(11),), 1: (late(9),)}
AFTER_FIRST = (middle(10),)
HOPS = ((late(10), middle(11)), (end(9), late(11)), (end(10), end(11)))
ENDING = ()


def step_kernel(dims, wins, *refs):
    (
        r_ids, r_halves, r_frames, r_blocks_in, r_x_in, r_dy_in, r_cond_in, r_ada_in, r_uq_in, r_uk_const_in, r_ut_in,
        r_selv_in, r_table_in, r_full, r_mixed, r_gx, r_rout, r_by_clip, r_tf, r_blocks, r_x, r_dy, r_cond, r_ada, r_uq,
        r_uk_const, r_ut, r_selv, r_table, r_hid, r_dff, r_qkv, r_heads, r_mid, r_ffn, r_dh2, r_wbuf, r_mod, r_dmod,
        r_modx, r_modf, r_ms, r_zacc, r_tmat, r_uk, r_tb, r_fold0, r_fold1, r_fold2, r_fold3, r_cl, r_st, r_held,
        r_box0, r_box1, r_box2, r_box3, r_box4, r_box5, r_fin, r_in_sem, r_w_sem, r_own_sem, r_o_sem, r_g_s, r_g_r,
        r_r_s, r_r_r, r_f_sem, r_m_s, r_m_r, r_s_s, r_s_r,
    ) = refs
    p = Place(dims)
    A, B, C = dims
    T = wins * TOK
    D = 1024
    Rp = r_blocks.shape[1]
    K = r_blocks.shape[2]
    clips, ncol = r_cond.shape[0], r_ada.shape[1]
    x, dy, hid, dff, qkv, heads = r_x, r_dy, r_hid, r_dff, r_qkv, r_heads
    mid, ffn, dh2, wbuf, mod, dmod = r_mid, r_ffn, r_dh2, r_wbuf, r_mod, r_dmod
    full = r_full
    at_once = ROWS[C <= 2]
    rows_per_win = TOK // at_once

    loads = [
        pltpu.make_async_copy(src, dst, r_in_sem.at[i])
        for i, (src, dst) in enumerate(
            (
                (r_blocks_in, r_blocks),
                (r_x_in, r_x),
                (r_dy_in, r_dy),
                (r_cond_in, r_cond),
                (r_ada_in, r_ada),
                (r_uq_in, r_uq),
                (r_uk_const_in, r_uk_const),
                (r_ut_in, r_ut),
                (r_selv_in, r_selv),
                (r_table_in, r_table),
            )
        )
    ]
    for copy in loads:
        copy.start()
    p.barrier()
    gather = Gather(p, r_blocks, full, r_g_s, r_g_r)
    scatter = Scatter(
        p, [r_st.at[0], r_st.at[1], wbuf.at[0]], r_held, [r_box0, r_box1, r_box2, r_box3, r_box4, r_box5],
        r_fin, r_rout, r_r_s, r_r_r, r_f_sem,
    )
    loads[0].wait()
    gather.first(0)
    own = pltpu.make_async_copy(r_blocks, full.at[:, p.a, p.b, p.k, :, cols(p.c, K)], r_own_sem.at[0])
    own.start()

    def mod_c():
        return [
            remote(r_modx.at[C - 1], r_modx.at[d - 1], r_m_s.at[d - 1], r_m_r.at[d - 1], p.dev(c=p.c_peer(d)))
            for d in range(1, C)
        ]

    loads[3].wait()
    loads[4].wait()
    act_rows = jax.nn.silu(r_cond[:, cols(p.c, r_ada.shape[0])].astype(f32)).astype(bf16)
    r_modx[C - 1] = nn(act_rows, r_ada[...])
    for copy in mod_c():
        copy.start()
    spread = Spread(p, r_ms, r_modf, "abk", r_m_s, r_m_r, C - 1)

    for i in (8, 9, 6, 5, 7, 1, 2):
        loads[i].wait()
    lanes = lax.broadcasted_iota(jnp.int32, (1, 128), 1)
    away = jnp.where(lanes == 21, -1e30, 0.0)
    for v in range(32):
        row = nt(r_table[...], r_selv[v]) if v < 21 else jnp.broadcast_to(away if v == 21 else away * 0.0, (HEADS, 128))
        r_zacc[v * HEADS : (v + 1) * HEADS] = row
    for copy in mod_c():
        copy.wait_recv()
    total = r_modx[C - 1]
    for d in range(C - 1):
        total = total + r_modx[d]
    r_ms[...] = total
    own_ms = pltpu.make_async_copy(r_ms, r_modf.at[p.a, p.b, p.k], r_own_sem.at[1])
    own_ms.start()
    spread.start(0)
    own.wait()
    gather.slot(0, LOOKAHEAD)
    for h in range(HEADS):
        r_tmat[h] = r_zacc[pl.ds(h, 32, stride=HEADS), :].astype(bf16)
    own_ms.wait()
    spread.landed(0)
    spread.start(1)
    gather.slot(1, LOOKAHEAD)
    spread.landed(1)
    spread.start(2)
    frame = lax.broadcasted_iota(jnp.int32, (TOK, 128), 0) // (WIN_SIDE * WIN_SIDE)
    flag = lax.broadcasted_iota(jnp.int32, (TOK, 128), 1) == 21
    for win in range(wins):
        live = jnp.clip(r_frames[r_ids[win]] - WIN_FRAMES * r_halves[win], 1, WIN_FRAMES)
        hide = jnp.logical_and(flag, frame >= live)
        r_uk[win] = jnp.where(hide, 1.0, r_uk_const[...].astype(f32)).astype(bf16)
    gather.slot(2, LOOKAHEAD)
    spread.landed(2)

    def weight(t, slot):
        return pltpu.make_async_copy(full.at[t], wbuf.at[slot], r_w_sem.at[slot])

    gather.slot(3, LOOKAHEAD)
    weight(0, 0).start()
    piece = math.gcd(ncol, 128)
    clip_iota = lax.broadcasted_iota(jnp.int32, (clips, ncol), 0)
    for w in range(2 * A * B):
        blk = r_modf[w // (2 * B), (w // 2) % B, w % 2]
        for win in range(wins):
            row = jnp.sum(jnp.where(clip_iota == r_ids[win], blk, 0.0), 0, keepdims=True)
            for i in range(ncol // piece):
                col = w * ncol + i * piece
                mod[win * 6 + col // D, :, col % D : col % D + piece] = row[:, i * piece : (i + 1) * piece]
    gather.slot(4, LOOKAHEAD)
    weight(1, 1).start()

    def rows_loop(fn, also={}):
        def run(i):
            win = i // rows_per_win
            fn(pl.ds(pl.multiple_of(i * at_once, at_once), at_once), win * 6)
            scatter.at(i, also)

        loop(T // at_once, run)

    def make_hidden1(also={}):
        def run(rows, m):
            norm, _ = normalize(x[rows, :].astype(f32))
            hid[rows, :] = (norm * (1.0 + mod[m + 1]) + mod[m]).astype(bf16)

        rows_loop(run, also)

    make_hidden1()
    for i in range(wins * 6):
        dmod[i] = jnp.zeros((1, D), f32)
    r_zacc[...] = jnp.zeros((HEADS * 32, 128), f32)

    gather.slot(5, LOOKAHEAD)
    weight(2, 2).start()
    for t in range(3):
        weight(t, t).wait()

    def qkv_rows(a, first):
        parts = []
        for b in range(B):
            for k in range(2):
                for t in range(3):
                    parts.append(wbuf[first + t, a, b, k])
        return jnp.concatenate(parts, 0)

    def qkv_cols(a):
        return pl.ds(pl.multiple_of(a * (3 * D // A), 128), 3 * D // A)

    def qkv_step(a):
        qkv[:, qkv_cols(a)] = nt(hid[...], qkv_rows(a, 0)).astype(bf16)

    loop(A, qkv_step)
    gather.slot(6, LOOKAHEAD)
    weight(3, 3).start()

    pairs = D // 128
    low_half = lax.broadcasted_iota(jnp.int32, (TOK, 128), 1) < 64

    def head_refs(i):
        win, pair = i // pairs, lax.rem(i, pairs)
        rows = pl.ds(pl.multiple_of(win * TOK, TOK), TOK)
        spots = [pl.ds(pl.multiple_of(j * D + pair * 128, 128), 128) for j in range(3)]
        return win, pair, rows, spots

    def two_heads(value):
        zero = jnp.zeros_like(value)
        return jnp.concatenate([jnp.where(low_half, value, zero), jnp.where(low_half, zero, value)], 0)

    def one_pair(value):
        return jnp.where(low_half, value[:TOK], value[TOK:])

    def attend(i):
        win, pair, rows, spots = head_refs(i)
        q = qkv[rows, spots[0]] * jnp.asarray(0.125, bf16)
        k, v = qkv[rows, spots[1]], qkv[rows, spots[2]]
        filler = jnp.zeros((96, 128), bf16)
        spread_rows = jnp.concatenate([r_tmat[pair * 2], filler, r_tmat[pair * 2 + 1], filler], 0)
        bias = nt(r_uq[...], spread_rows).astype(bf16)
        bias = jnp.concatenate([bias[:, :128], bias[:, 128:]], 0)
        s = nt(jnp.concatenate([two_heads(q), bias], 1), jnp.concatenate([k, r_uk[win]], 1))
        e = jnp.exp(s - jnp.max(s, -1, keepdims=True))
        probs = e * (1.0 / jnp.sum(e, -1, keepdims=True))
        heads[rows, spots[0]] = one_pair(nn(probs.astype(bf16), v)).astype(bf16)
        guard(i == 5, lambda: gather.slot(7, LOOKAHEAD))
        guard(i == 12, lambda: gather.slot(8, LOOKAHEAD))

    loop(wins * pairs, attend)
    weight(4, 0).start()
    weight(5, 1).start()
    weight(3, 3).wait()
    quarter = D // A

    def quarter_cols(a):
        return pl.ds(pl.multiple_of(a * quarter, 128), quarter)

    def out_step(a):
        got = nt(heads[...], wbuf[3, a].reshape(quarter, D))
        at = quarter_cols(a)
        for win in range(wins):
            rows = slice(win * TOK, (win + 1) * TOK)
            mid[rows, at] = x[rows, at].astype(f32) + mod[win * 6 + 2, :, at] * got[rows]

    loop(A, out_step)
    gather.slot(9, LOOKAHEAD)

    def second_norm(rows, m):
        norm, _ = normalize(mid[rows, :])
        hid[rows, :] = (norm * (1.0 + mod[m + 4]) + mod[m + 3]).astype(bf16)
        dff[rows, :] = (mod[m + 5] * dy[rows, :].astype(f32)).astype(bf16)
        ffn[rows, :] = jnp.zeros((at_once, D), f32)
        dh2[rows, :] = jnp.zeros((at_once, D), f32)

    rows_loop(second_norm)

    st = r_st
    subs = 1 if C <= 2 else 2
    per, F = A // 2 // subs, D // 2 // subs

    def ffn_step(s):
        q, hf = s // 2, lax.rem(s, 2)
        su = 2 * lax.rem(q, 2)

        @pl.when(hf == 0)
        def _():
            weight(4 + 2 * q, su).wait()
            weight(5 + 2 * q, su + 1).wait()

        def between():
            @pl.when(jnp.logical_and(hf == 0, q > 0))
            def _():
                scatter.flush(2 * q - 2, 0)
                scatter.flush(2 * q - 1, 1)

            guard(s == 4, lambda: gather.slot(13, LOOKAHEAD))

            @pl.when(s == 5)
            def _():
                gather.slot(14, LOOKAHEAD)
                weight(10, 2).start()
                weight(11, 3).start()

            scatter.at(s, FFN_EARLY)

        for sub in range(subs):
            first = hf * (A // 2) + sub * per
            up = wbuf[su, pl.ds(first, per)].reshape(F, D)
            at = pl.ds(pl.multiple_of((hf * subs + sub) * F, F), F)
            down = wbuf[su + 1, :, :, :, :, at].reshape(D, F)
            act, slope = gelu_parts(nt(hid[...], up))
            act = act.astype(bf16)
            ffn[...] += nt(act, down)
            d_pre = (nn(dff[...], down) * slope).astype(bf16)
            dh2[...] += nn(d_pre, up)
            if sub == 0:
                between()
            st[0, pl.ds(first, per)] = tn(d_pre, hid[...]).astype(bf16).reshape(per, B, 2, Rp, D)
            st[1, :, :, :, :, at] = tn(dff[...], act).astype(bf16).reshape(A, B, 2, Rp, F)

        @pl.when(hf == 1)
        def _():
            scatter.sibling(2 * q, 0).start()
            scatter.sibling(2 * q + 1, 1).start()

        guard(s < 3, lambda: gather.slot(10 + s, LOOKAHEAD))
        scatter.at(s, FFN_LATE)

        @pl.when(jnp.logical_and(hf == 0, q < 2))
        def _():
            weight(6 + 2 * q, 2 - su).start()
            weight(7 + 2 * q, 3 - su).start()

    loop(8, ffn_step)
    weight(3, 0).start()
    weight(0, 1).start()
    weight(1, 2).start()
    weight(2, 3).start()

    def second_back(rows, m):
        norm, inv = normalize(mid[rows, :])
        dyr = dy[rows, :].astype(f32)
        fo = ffn[rows, :]
        dh = dh2[rows, :]
        dmod[m + 5] += jnp.sum(dyr * fo, 0, keepdims=True)
        dmod[m + 3] += jnp.sum(dh, 0, keepdims=True)
        dmod[m + 4] += jnp.sum(dh * norm, 0, keepdims=True)
        dy[rows, :] = (mid[rows, :] + mod[m + 5] * fo).astype(bf16)
        ffn[rows, :] = jnp.zeros((at_once, D), f32)
        d_mid = dyr + normalize_back(dh * (1.0 + mod[m + 4]), norm, inv)
        dh2[rows, :] = d_mid
        dff[rows, :] = (mod[m + 2] * d_mid).astype(bf16)

    rows_loop(second_back, SECOND_BACK)
    mixed_out = pltpu.make_async_copy(dy, r_mixed, r_o_sem.at[0])
    mixed_out.start()
    scatter.flush(6, 0)
    scatter.flush(7, 1)
    weight(3, 0).wait()

    def out_back(a):
        at = quarter_cols(a)
        wide = wbuf[0, a].reshape(quarter, D)
        attended = nt(heads[...], wide)
        for win in range(wins):
            rows = slice(win * TOK, (win + 1) * TOK)
            dmod[win * 6 + 2, :, at] = jnp.sum(dh2[rows, at] * attended[rows], 0, keepdims=True)
        st[0, a] = tn(dff[:, at], heads[...]).astype(bf16).reshape(B, 2, Rp, D)
        scatter.sibling_part(8, 0, a).start()
        hid[:, at] = nn(dff[...], wbuf[0, :, :, :, :, at].reshape(D, quarter)).astype(bf16)
        scatter.at(a, OUT_BACK)

    loop(A, out_back)
    def attend_back(i):
        win, pair, rows, spots = head_refs(i)
        q = qkv[rows, spots[0]] * jnp.asarray(0.125, bf16)
        k, v = qkv[rows, spots[1]], qkv[rows, spots[2]]
        do = hid[rows, spots[0]]
        kk = two_heads(k)
        bias = nn(r_uk[win][:, :32], jnp.concatenate([r_tmat[pair * 2], r_tmat[pair * 2 + 1]], 1)).astype(bf16)
        bias = jnp.concatenate([bias[:, :128], bias[:, 128:]], 0)
        query = jnp.concatenate([q, r_uq[...]], 1)
        s = nt(jnp.concatenate([kk, bias], 1), query)
        dp = nt(two_heads(v), do)
        probs, ds = [], []
        for h in range(2):
            sh, dph = s[h * TOK : (h + 1) * TOK], dp[h * TOK : (h + 1) * TOK]
            e = jnp.exp(sh - jnp.max(sh, 0, keepdims=True))
            ph = e * (1.0 / jnp.sum(e, 0, keepdims=True))
            probs.append(ph.astype(bf16))
            ds.append((ph * (dph - jnp.sum(ph * dph, 0, keepdims=True))).astype(bf16))
        probs = jnp.concatenate(probs, 0)
        ds = jnp.concatenate(ds, 0)
        dk = nn(ds, query)
        qkv[rows, spots[0]] = (tn(ds, kk) * 0.125).astype(bf16)
        qkv[rows, spots[1]] = one_pair(dk[:, :128]).astype(bf16)
        qkv[rows, spots[2]] = one_pair(nn(probs, do)).astype(bf16)
        bias_part = jnp.concatenate([dk[:TOK, 128:], dk[TOK:, 128:]], 1)
        top = bias_part.astype(bf16)
        rest = (bias_part - top.astype(f32)).astype(bf16)
        z = nn(r_ut[...], top) + nn(r_ut[...], rest)
        for h in range(2):
            r_zacc[pl.ds(pl.multiple_of((pair * 2 + h) * 32, 32), 32), :] += z[:, h * 128 : (h + 1) * 128]
        scatter.at(i, ATTEND_BACK)

    loop(wins * pairs, attend_back)
    table = jnp.zeros((HEADS, 128), f32)
    for v in range(21):
        zv = r_zacc[pl.ds(v, HEADS, stride=32), :]
        top = zv.astype(bf16)
        rest = (zv - top.astype(f32)).astype(bf16)
        table = table + nn(top, r_selv[v]) + nn(rest, r_selv[v])
    r_tb[...] = table
    tabs = Spread(p, r_tb, r_tf, "abck", r_s_s.at[1], r_s_r.at[1], 0)
    own_tb = pltpu.make_async_copy(r_tb, r_tf.at[p.a, p.b, p.k, p.c], r_own_sem.at[3])
    own_tb.start()
    tabs.start(0)
    spread.drain()
    own_tb.wait()
    gather.drain()
    make_hidden1(HIDDEN)
    tabs.landed(0)
    tabs.start(1)
    for t in range(3):
        weight(t, t + 1).wait()

    def qkv_grad(a):
        got = tn(qkv[:, qkv_cols(a)], hid[...]).astype(bf16)
        i = 0
        for b in range(B):
            for k in range(2):
                for t in range(3):
                    scatter.st[t][a, b, k] = got[i * Rp : (i + 1) * Rp]
                    i += 1
        for t in range(3):
            scatter.sibling_part(9 + t, t, a).start()
        scatter.at(a, QKV_GRAD)

    loop(A, qkv_grad)
    scatter.steps(part(9), begin(9), part(10), part(11))
    tabs.landed(1)
    tabs.start(2)

    def qkv_back(a):
        ffn[...] += nn(qkv[:, qkv_cols(a)], qkv_rows(a, 1))
        scatter.at(a, QKV_BACK)

    loop(A, qkv_back)
    tabs.landed(2)
    tabs.start(3)
    scatter.steps(*AFTER_QKV)

    def first_back(rows, m):
        norm, inv = normalize(x[rows, :].astype(f32))
        dh = ffn[rows, :]
        dmod[m] += jnp.sum(dh, 0, keepdims=True)
        dmod[m + 1] += jnp.sum(dh * norm, 0, keepdims=True)
        mid[rows, :] = dh2[rows, :] + normalize_back(dh * (1.0 + mod[m + 1]), norm, inv)

    rows_loop(first_back, FIRST_BACK)
    gx_out = pltpu.make_async_copy(mid, r_gx, r_o_sem.at[1])
    gx_out.start()
    own_clip = [
        (lax.broadcasted_iota(jnp.int32, (clips, piece), 0) == r_ids[win]).astype(f32) for win in range(wins)
    ]
    for w in range(2 * A * B):
        for i in range(ncol // piece):
            col = w * ncol + i * piece
            got = 0.0
            for win in range(wins):
                row = dmod[win * 6 + col // D, :, col % D : col % D + piece].astype(bf16).astype(f32)
                got = got + own_clip[win] * row
            r_modf[w // (2 * B), (w // 2) % B, w % 2, :, i * piece : (i + 1) * piece] = got
    fold = Fold(p, r_modf, [r_fold0, r_fold1, r_fold2, r_fold3], r_cl, r_s_s.at[0], r_s_r.at[0])
    fold.start(0)
    scatter.steps(*AFTER_FIRST)
    scatter.drain(0, 9)
    for phase in (1, 2, 3):
        fold.add(phase - 1)
        fold.start(phase)
        scatter.steps(*HOPS[phase - 1])
    fold.add(3)
    clip_out = pltpu.make_async_copy(r_cl, r_by_clip, r_own_sem.at[2])
    clip_out.start()
    tabs.landed(3)
    scatter.steps(*ENDING)
    clip_out.wait()
    mixed_out.wait()
    gx_out.wait()
    for r in (scatter.count - 2, scatter.count - 1):
        scatter.result(r).wait()
    scatter.drain(9, 3)
    for copy in mod_c():
        copy.wait_send()
    for small in (fold, tabs):
        small.drain()


def run_step(dims, wins, ins):
    A, B, C = dims
    n, Rp, K = ins[3].shape
    clips, ncol = ins[6].shape[0], ins[7].shape[1]
    T = wins * TOK
    D = 1024
    hbm = pl.BlockSpec(memory_space=pltpu.HBM)
    smem = pl.BlockSpec(memory_space=pltpu.SMEM)
    out_shape = [
        jax.ShapeDtypeStruct((n, A, B, 2, Rp, D), bf16),
        jax.ShapeDtypeStruct((T, D), bf16),
        jax.ShapeDtypeStruct((T, D), f32),
        jax.ShapeDtypeStruct((n, Rp, K), f32),
        jax.ShapeDtypeStruct((clips, ncol), f32),
        jax.ShapeDtypeStruct((A, B, 2, C, HEADS, 128), f32),
    ]
    small = A - 1 + B - 1 + C - 1 + 1
    dma = pltpu.SemaphoreType.DMA
    scratch = [
        *[pltpu.VMEM(v.shape, v.dtype) for v in ins[3:]],
        pltpu.VMEM((T, D), bf16),
        pltpu.VMEM((T, D), bf16),
        pltpu.VMEM((T, 3 * D), bf16),
        pltpu.VMEM((T, D), bf16),
        pltpu.VMEM((T, D), f32),
        pltpu.VMEM((T, D), f32),
        pltpu.VMEM((T, D), f32),
        pltpu.VMEM((4, A, B, 2, Rp, D), bf16),
        pltpu.VMEM((wins * 6, 1, D), f32),
        pltpu.VMEM((wins * 6, 1, D), f32),
        pltpu.VMEM((C, clips, ncol), f32),
        pltpu.VMEM((A, B, 2, clips, ncol), f32),
        pltpu.VMEM((clips, ncol), f32),
        pltpu.VMEM((HEADS * 32, 128), f32),
        pltpu.VMEM((HEADS, 32, 128), bf16),
        pltpu.VMEM((wins, TOK, 128), bf16),
        pltpu.VMEM((HEADS, 128), f32),
        pltpu.VMEM((1, A, B, clips, ncol), f32),
        pltpu.VMEM((B - 1, A, clips, ncol), f32),
        pltpu.VMEM((A - 1, clips, ncol), f32),
        pltpu.VMEM((C - 1, clips, ncol), f32),
        pltpu.VMEM((clips, ncol), f32),
        pltpu.VMEM((2, A, B, 2, Rp, D), bf16),
        pltpu.VMEM((n, A, B, Rp, D), bf16),
        *[pltpu.VMEM(shape, bf16) for shape in Scatter.box_shapes(dims, n, Rp, K)],
        pltpu.VMEM((2, Rp, K), f32),
        dma((10,)),
        dma((4,)),
        dma((4,)),
        dma((2,)),
        dma((n, Gather.sems(dims))),
        dma((n, Gather.sems(dims))),
        dma((n, Scatter.sems(dims))),
        dma((n, Scatter.sems(dims))),
        dma((2,)),
        dma((C - 1 + small,)),
        dma((C - 1 + small,)),
        dma((2, small)),
        dma((2, small)),
    ]
    return pl.pallas_call(
        functools.partial(step_kernel, dims, wins),
        out_shape=out_shape,
        in_specs=[smem] * 3 + [hbm] * 10,
        out_specs=[hbm] * 6,
        scratch_shapes=scratch,
        compiler_params=pltpu.CompilerParams(
            collective_id=0, has_side_effects=True, vmem_limit_bytes=66 * 10**6 + 2**19
        ),
        name="block_step",
    )(*ins)


def body(dims, tokens, cotangent, cond, clip_frames, window_clip, window_half, ada, qkv_w, out_w, up_w, down_w, table):
    A, B, C = dims
    W = 2 * A * B
    devices = W * C
    micro, wl, toks, width = tokens.shape
    wins = micro * wl
    clips = cond.shape[0]
    n = lax.axis_index("narrow")
    ids = window_clip.reshape(wins)
    half = window_half.reshape(wins)

    Rp = out_w.shape[1]
    K = out_w.shape[0]
    pieces = up_w.shape[1] // Rp
    up_t = up_w.T.reshape(pieces, Rp, K)
    down_t = down_w.reshape(-1, pieces, Rp, Rp).transpose(1, 3, 0, 2).reshape(pieces, Rp, K)
    ffn_t = jnp.stack([up_t, down_t], 1).reshape(2 * pieces, Rp, K)
    blocks = jnp.concatenate([qkv_w.T.reshape(3, Rp, K), out_w.T[None], ffn_t], 0)

    feats = position_features()
    uq_const = np.zeros((toks, 128), np.float32)
    uq_const[:, :21] = feats
    uq_const[:, 21] = 1
    uk_const = np.zeros((toks, 128), np.float32)
    uk_const[:, :21] = feats
    sel = offset_selector()
    entries = sel.shape[2]
    selv = np.zeros((21, 128, 128), np.float32)
    selv[:, :21, :entries] = sel.transpose(1, 0, 2)
    ins = (
        ids,
        half,
        clip_frames,
        blocks,
        tokens.reshape(wins * toks, width),
        cotangent.reshape(wins * toks, width),
        cond,
        ada,
        jnp.asarray(uq_const, bf16),
        jnp.asarray(uk_const, bf16),
        jnp.asarray(uk_const[:, :32].T, bf16),
        jnp.asarray(selv, bf16),
        jnp.pad(table, ((0, 0), (0, 128 - table.shape[1]))),
    )
    _, mixed, grad_x, rout, by_clip, table_parts = run_step(dims, wins, ins)

    table_parts = table_parts.reshape(devices, HEADS, 128)
    grad_table = table_parts.sum(0)[:, : table.shape[1]]
    cond_act = jax.nn.silu(cond.astype(f32)).astype(bf16)
    act_rows = lax.dynamic_slice_in_dim(cond_act, n * ada.shape[0], ada.shape[0], 1)
    grad_ada = jnp.einsum("cr,ce->re", act_rows.astype(f32), by_clip, precision=highest)

    ffn_r = rout[: 2 * pieces].reshape(pieces, 2, Rp, K)
    g_up = ffn_r[:, 0].reshape(pieces * Rp, K).T
    g_down = ffn_r[:, 1].reshape(pieces, Rp, -1, Rp).transpose(2, 0, 3, 1).reshape(-1, Rp)
    g_out = rout[2 * pieces].T
    g_qkv = rout[2 * pieces + 1 :].reshape(3 * Rp, K).T
    return (
        mixed.reshape(tokens.shape),
        grad_x.reshape(tokens.shape),
        grad_ada,
        g_qkv,
        g_out,
        g_up,
        g_down,
        grad_table,
    )


def solution(mesh):
    W, C = mesh.shape["wide"], mesh.shape["narrow"]
    A = min(4, W // 2)
    dims = (A, W // 2 // A, C)
    sh = ("wide", "narrow")
    weight = P("narrow", "wide")
    return jax.shard_map(
        functools.partial(body, dims),
        mesh=mesh,
        in_specs=(P(None, sh), P(None, sh), P(), P(), P(None, sh), P(None, sh)) + (weight,) * 5 + (P(),),
        out_specs=(P(None, sh), P(None, sh)) + (weight,) * 5 + (P(),),
        check_vma=False,
    )
```
